256 devices in a mesh: gx: 8 (over y, core), gy: 8 (over z), gz: 4 (over x).
Axes of the slice: x: 4, y: 4, z: 8, core: 2. Of those that a mesh axis runs over, the one named last changes fastest.
Arguments:
- fields: bfloat16 [384, 16, 32, 512], P(None, 'gx', 'gy', 'gz'), may hold values from -6 to 6
- trace_old: float32 [3, 32, 16, 32, 512], P(None, None, 'gx', 'gy', 'gz'), may hold values from -4 to 4
- face_load: float32 [3, 32, 16, 32, 512], P(None, None, 'gx', 'gy', 'gz'), may hold values from -6 to 6
- face_diag: float32 [3, 16, 32, 512], P(None, 'gx', 'gy', 'gz'), may hold values from 0.5 to 4
- fine_flag: int32 [16, 32, 512], P('gx', 'gy', 'gz'), may hold values from 0 to 1
- coeff: float32 [16, 32, 512], P('gx', 'gy', 'gz'), may hold values from 0.5 to 8
- volume_op: bfloat16 [384, 384], replicated, may hold values from -0.3125 to 0.3125
- lift_op: bfloat16 [384, 192], replicated, may hold values from -0.4375 to 0.4375
- schur_op: float32 [192, 192], replicated, may hold values from -8 to 8.5, as said below
Outputs:
- fields_new: bfloat16 [384, 16, 32, 512], P(None, 'gx', 'gy', 'gz')
- trace_new: float32 [3, 32, 16, 32, 512], P(None, None, 'gx', 'gy', 'gz')
The draws below stay inside these ranges and needn't reach their ends.
Inputs may be any that keep to these rules, and one draw needn't show every extreme that they name: schur_op is symmetric and positive definite.
All inputs are finite; a program needn't handle non-finite values.
Results may differ from the reference program's by a relative error of at most 0.0013.
Values sent between devices are 32-bit elements; how exact they have to be, the bound alone decides.
A program may use at most 64 MiB of HBM per device.

```python
import math
import jax
import jax.numpy as jnp
from jax import lax

EX = 2
EY = 4
EZ = 128
ELEMDOF = 384
FACEDOF = 32
ITERS = 2
SCHUR = 192
NX = 16
NY = 32
NZ = 512


def draw_fine_flag(key, part):
    level_key, roll_key = jax.random.split(jax.random.fold_in(key, 17))
    levels = jax.random.randint(level_key, (NX // EX, NY // EY, NZ // EZ), 1, 10)
    spread = jnp.repeat(jnp.repeat(jnp.repeat(levels, EX, 0), EY, 1), EZ, 2)
    dice_rolls = jax.random.randint(roll_key, (NX, NY, NZ), 0, 10)
    return (dice_rolls < spread).astype(jnp.int32)


def draw_schur_op(key, part):
    base_key = jax.random.fold_in(key, 29)
    factor = jnp.clip(jax.random.normal(base_key, (SCHUR, SCHUR), jnp.float32), -4.0, 4.0)
    factor = factor / jnp.sqrt(jnp.float32(SCHUR))
    product = jnp.dot(factor, factor.T, precision=lax.Precision.HIGHEST)
    product = 0.5 * (product + product.T)
    return 0.5 * product + 0.5 * jnp.eye(SCHUR, dtype=jnp.float32)


def block_levels(stream_key, shape, shards, least, top_value):
    def one(axis_at, parts):
        draws = jax.random.uniform(jax.random.fold_in(jax.random.fold_in(stream_key, 6), axis_at), (parts,), jnp.float32, least / len(shards), top_value / len(shards))
        return jnp.repeat(jnp.exp(draws), shape[axis_at] // parts).reshape((-1,) + (1,) * (len(shape) - axis_at - 1))

    loudness = one(*shards[0])
    for cut in shards[1:]:
        loudness = loudness * one(*cut)
    return loudness


def bell_draw(stream_key, extent, deviation, limit, cuts=(), held_as=jnp.bfloat16):
    drawn = deviation * jax.random.normal(stream_key, extent, jnp.float32)
    if cuts:
        drawn = drawn * block_levels(stream_key, extent, cuts, -0.22, 0.18)
    return jnp.clip(drawn, -limit, limit).astype(held_as)


def setup_inputs(seed: int = 0) -> dict:
    arg_keys = jax.random.split(jax.random.key(seed), 10)
    return {
        "fields": bell_draw(arg_keys[0], (ELEMDOF, NX, NY, NZ), 1.0, 6.0, ((1, 8), (2, 8), (3, 4))),
        "trace_old": bell_draw(arg_keys[1], (3, FACEDOF, NX, NY, NZ), 0.5, 4.0, ((2, 8), (3, 8), (4, 4)), jnp.float32),
        "face_load": bell_draw(arg_keys[2], (3, FACEDOF, NX, NY, NZ), 1.0, 6.0, ((2, 8), (3, 8), (4, 4)), jnp.float32),
        "face_diag": jnp.clip(jnp.exp(math.log(4.0) - 2.0794415 * jax.random.uniform(arg_keys[3], (3, NX, NY, NZ), jnp.float32) ** block_levels(arg_keys[3], (3, NX, NY, NZ), ((1, 8), (2, 8), (3, 4)), -0.2, 0.2)), 0.5, 4.0),
        "fine_flag": draw_fine_flag(jax.random.fold_in(arg_keys[9], 71), 0),
        "coeff": jnp.clip(jnp.exp(math.log(8.0) - 2.7725887 * jax.random.uniform(arg_keys[5], (NX, NY, NZ), jnp.float32) ** block_levels(arg_keys[5], (NX, NY, NZ), ((0, 8), (1, 8), (2, 4)), -0.2, 0.2)), 0.5, 8.0),
        "volume_op": bell_draw(arg_keys[6], (ELEMDOF, ELEMDOF), ELEMDOF ** -0.5, 0.3125),
        "lift_op": bell_draw(arg_keys[7], (ELEMDOF, SCHUR), SCHUR ** -0.5, 0.4375),
        "schur_op": draw_schur_op(jax.random.fold_in(arg_keys[9], 71), 0),
    }


time_step = 0.25
highest = lax.Precision.HIGHEST


def pad_upper(traces):
    return jnp.pad(traces, ((0, 0), (0, 0), (0, 1), (0, 1), (0, 1)))


def element_faces(padded, position):
    current = lax.dynamic_index_in_dim(padded, position, 2, keepdims=False)
    following = lax.dynamic_index_in_dim(padded, position + 1, 2, keepdims=False)
    pieces = [current[0, :, :NY, :NZ], following[0, :, :NY, :NZ],
              current[1, :, :NY, :NZ], current[1, :, 1:, :NZ],
              current[2, :, :NY, :NZ], current[2, :, :NY, 1:]]
    return jnp.concatenate(pieces, 0).reshape(SCHUR, NY * NZ)


def operate(traces, weight, face_diag, schur_op):
    padded = pad_upper(traces)

    def one_slab(position):
        face_values = element_faces(padded, position)
        applied = jnp.dot(schur_op, face_values, precision=highest, preferred_element_type=jnp.float32)
        element_weight = lax.dynamic_index_in_dim(weight, position, 0, keepdims=False).reshape(1, NY * NZ)
        return (applied * element_weight).reshape(6, FACEDOF, NY, NZ)

    images = lax.map(one_slab, jnp.arange(NX).astype(jnp.int32))
    along_x = images[:, 0] + jnp.concatenate([jnp.zeros_like(images[:1, 1]), images[:-1, 1]], 0)
    along_y = images[:, 2] + jnp.pad(images[:, 3], ((0, 0), (0, 0), (1, 0), (0, 0)))[:, :, :NY]
    along_z = images[:, 4] + jnp.pad(images[:, 5], ((0, 0), (0, 0), (0, 0), (1, 0)))[:, :, :, :NZ]
    coupled = jnp.stack([along_x, along_y, along_z], 0).transpose(0, 2, 1, 3, 4)
    return face_diag[:, None] * traces + coupled


def reference(fields, trace_old, face_load, face_diag, fine_flag, coeff, volume_op, lift_op, schur_op):
    fine_mask = fine_flag.astype(jnp.float32)
    weight = fine_mask * coeff
    solution = trace_old
    residual = face_load - operate(trace_old, weight, face_diag, schur_op)
    direction = residual
    norm_now = jnp.sum(residual * residual)
    for iteration in range(ITERS):
        applied = operate(direction, weight, face_diag, schur_op)
        step_length = norm_now / jnp.sum(direction * applied)
        solution = solution + step_length * direction
        if iteration + 1 < ITERS:
            residual = residual - step_length * applied
            norm_next = jnp.sum(residual * residual)
            direction = residual + (norm_next / norm_now) * direction
            norm_now = norm_next
    old_padded = pad_upper(trace_old)
    new_padded = pad_upper(solution)

    def update(position):
        nodal = lax.dynamic_index_in_dim(fields, position, 1, keepdims=False).reshape(ELEMDOF, NY * NZ)
        fine_row = lax.dynamic_index_in_dim(fine_mask, position, 0, keepdims=False).reshape(1, NY * NZ)
        traced = fine_row * element_faces(new_padded, position) + (1.0 - fine_row) * element_faces(old_padded, position)
        volume = jnp.dot(volume_op, nodal, preferred_element_type=jnp.float32)
        lifted = jnp.dot(lift_op, traced.astype(jnp.bfloat16), preferred_element_type=jnp.float32)
        result = nodal.astype(jnp.float32) + time_step * ((1.0 - fine_row) * volume + lifted)
        return result.astype(jnp.bfloat16).reshape(ELEMDOF, NY, NZ)

    updated = lax.map(update, jnp.arange(NX).astype(jnp.int32))
    return updated.transpose(1, 0, 2, 3), solution
```

```python
import functools

import jax
import jax.numpy as jnp
from jax import lax
from jax.experimental import pallas as pl
from jax.experimental.pallas import tpu as pltpu
from jax.sharding import PartitionSpec as P

MESH = pl.DeviceIdType.MESH
EX, EY, EZ = 2, 4, 128
CELLS = EX * EY
FD = 32
F32, BF16 = jnp.float32, jnp.bfloat16
TIME_STEP = 0.25


def dot(a, b):
    return jnp.dot(a, b, preferred_element_type=F32)


def fold(value):
    return jnp.sum(value.reshape(-1, 8, 128), axis=0)


def total(value):
    return jnp.sum(jnp.sum(value, axis=0, keepdims=True), axis=1, keepdims=True)


def kernel(sizes, *refs):
    (x_hbm, b_hbm, diag_hbm, fine_hbm, coeff_hbm, f_hbm, v_hbm, lt_hbm, s_hbm, fo_hbm, xo_hbm) = refs[:11]
    (xn, bn, dg, fi, co, fb, vb, ltb, sf, X, PR, R0, P0, W1, T, GH, GL, SH, SL, LF, FN, BASE, ON, FO, XO,
     gx, gy, gz, ux, uy, uz, cx, cy, cz, zs, hx, hy, hz, own, ra, own_b, rb, own_c, rc,
     load_sem, out_sem, send_sem, recv_sem) = refs[11:]
    names = ("gx", "gy", "gz")
    me = [lax.axis_index(n) for n in names]
    up = [lax.rem(m + 1, n) for m, n in zip(me, sizes)]
    down = [lax.rem(m + n - 1, n) for m, n in zip(me, sizes)]
    has_up = [m < n - 1 for m, n in zip(me, sizes)]
    has_down = [m > 0 for m in me]

    loads = [
        pltpu.make_async_copy(src, dst, load_sem.at[k])
        for k, (src, dst) in enumerate(
            [(x_hbm, xn), (s_hbm, sf), (fine_hbm, fi), (coeff_hbm, co), (diag_hbm, dg), (b_hbm, bn),
             (f_hbm, fb), (v_hbm, vb), (lt_hbm, ltb)]
        )
    ]
    for copy in loads:
        copy.start()

    barrier = pltpu.get_barrier_semaphore()
    partners = 0
    for axis, (name, n) in enumerate(zip(names, sizes)):
        for k in range(1, n):
            pl.semaphore_signal(barrier, inc=1, device_id={name: lax.rem(me[axis] + k, n)}, device_id_type=MESH)
            partners += 1

    counter = [0]

    def send(src, dst, name, target):
        k = counter[0]
        counter[0] += 1
        copy = pltpu.make_async_remote_copy(
            src_ref=src, dst_ref=dst, send_sem=send_sem.at[k], recv_sem=recv_sem.at[k],
            device_id={name: target}, device_id_type=MESH,
        )
        copy.start()
        return copy

    lane = lax.broadcasted_iota(jnp.int32, (FD, EZ), 1)
    cells = [(i, j) for i in range(EX) for j in range(EY)]

    def keep(flag, value):
        return jnp.where(flag, value, 0.0)

    def pack(pieces, at):
        out = jnp.zeros((FD, EZ), F32)
        for n, piece in enumerate(pieces):
            out = jnp.where(lane == n, pltpu.roll(piece, (n - at) % EZ, 1), out)
        return out

    def unpack(packed, n, at):
        return pltpu.roll(packed, (at - n) % EZ, 1)

    def faces(v, k, i, j):
        n = i * EY + j
        z = v[i, j, 64:96, :]
        return [
            v[i, j, 0:32, :],
            v[i + 1, j, 0:32, :] if i + 1 < EX else hx[k, j],
            v[i, j, 32:64, :],
            v[i, j + 1, 32:64, :] if j + 1 < EY else hy[k, i],
            z,
            jnp.where(lane == EZ - 1, unpack(hz[k], n, EZ - 1), pltpu.roll(z, EZ - 1, 1)),
        ]

    def apply(v, k):
        for n, (i, j) in enumerate(cells):
            for at, block in enumerate(faces(v, k, i, j)):
                high = block.astype(BF16)
                low = (block - high.astype(F32)).astype(BF16)
                GH[32 * at : 32 * at + 32, EZ * n : EZ * n + EZ] = high
                GL[32 * at : 32 * at + 32, EZ * n : EZ * n + EZ] = low
        for n in range(0, CELLS, 2):
            cols = slice(EZ * n, EZ * n + 2 * EZ)
            high = GH[:, cols]
            product = dot(SH[...], high) + (dot(SH[...], GL[:, cols]) + dot(SL[...], high))
            for m in range(2):
                T[n + m] = product[:, EZ * m : EZ * m + EZ] * weight(n + m)

    def weight(n):
        return fi[n : n + 1, :].astype(F32) * co[n : n + 1, :]

    def gathered(i, j):
        n = i * EY + j
        along_x, along_y = T[n, 0:32, :], T[n, 64:96, :]
        if i > 0:
            along_x = along_x + T[n - EY, 32:64, :]
        if j > 0:
            along_y = along_y + T[n - 1, 96:128, :]
        along_z = T[n, 128:160, :] + jnp.where(lane == 0, 0.0, pltpu.roll(T[n, 160:192, :], 1, 1))
        return [along_x, along_y, along_z]

    def upper(i_or_j, axis):
        if axis == 0:
            return T[(EX - 1) * EY + i_or_j, 32:64, :]
        return T[i_or_j * EY + EY - 1, 96:128, :]

    def upper_z():
        return pack([T[n, 160:192, :] for n in range(CELLS)], EZ - 1)

    def diag(a, n):
        return dg[a * CELLS + n : a * CELLS + n + 1, :]

    def exchange(k, p):
        out = [send(p.at[0, :, 0:32, :], gx.at[k], "gx", down[0])]
        if k > 0:
            for j in range(EY):
                cx[k - 1, j] = upper(j, 0)
            out.append(send(cx.at[k - 1], ux.at[k - 1], "gx", up[0]))
        out.append(send(p.at[:, 0, 32:64, :], gy.at[k], "gy", down[1]))
        if k > 0:
            for i in range(EX):
                cy[k - 1, i] = upper(i, 1)
            out.append(send(cy.at[k - 1], uy.at[k - 1], "gy", up[1]))
        zs[k] = pack([p[i, j, 64:96, :] for i, j in cells], 0)
        out.append(send(zs.at[k], gz.at[k], "gz", down[2]))
        if k > 0:
            cz[k - 1] = upper_z()
            out.append(send(cz.at[k - 1], uz.at[k - 1], "gz", up[2]))
        return out

    def ghosts(k, sign):
        for j in range(EY):
            hx[k, j] = keep(has_up[0], gx[k, j] + sign * cx[k - 1, j] if k > 0 else gx[k, j])
        for i in range(EX):
            hy[k, i] = keep(has_up[1], gy[k, i] + sign * cy[k - 1, i] if k > 0 else gy[k, i])
        hz[k] = keep(has_up[2], gz[k] + sign * cz[k - 1] if k > 0 else gz[k])

    def complete(p, out, k, sign):
        for n, (i, j) in enumerate(cells):
            along_x, along_y, along_z = p[i, j, 0:32, :], p[i, j, 32:64, :], p[i, j, 64:96, :]
            if i == 0:
                along_x = along_x + sign * keep(has_down[0], ux[k - 1, j])
            if j == 0:
                along_y = along_y + sign * keep(has_down[1], uy[k - 1, i])
            below = jnp.where(lane == 0, unpack(uz[k - 1], n, 0), 0.0)
            along_z = along_z + sign * keep(has_down[2], below)
            out[i, j, 0:32, :] = along_x
            out[i, j, 32:64, :] = along_y
            out[i, j, 64:96, :] = along_z

    loads[0].wait()
    for n, (i, j) in enumerate(cells):
        X[i, j] = xn[pl.ds(n, 96, stride=CELLS), :]
    pl.semaphore_wait(barrier, partners)
    copies = exchange(0, X)
    loads[1].wait()
    s = sf[...]
    high = s.astype(BF16)
    SH[...] = high
    SL[...] = (s - high.astype(F32)).astype(BF16)
    loads[2].wait()
    loads[3].wait()
    loads[4].wait()
    loads[5].wait()
    loads[6].wait()
    for n in range(0, 3072, 128):
        FN[n : n + 128, :] = fb[n : n + 128, :].astype(F32)
    for copy in copies:
        copy.wait()
    ghosts(0, 0.0)

    apply(X, 0)
    for n, (i, j) in enumerate(cells):
        parts = gathered(i, j)
        for a in range(3):
            load = bn[pl.ds(a * FD * CELLS + n, FD, stride=CELLS), :]
            PR[i, j, 32 * a : 32 * a + 32, :] = load - diag(a, n) * X[i, j, 32 * a : 32 * a + 32, :] - parts[a]
    copies = exchange(1, PR)

    def volume(n):
        pair = [FN[pl.ds(n + m, 384, stride=CELLS), :] for m in range(2)]
        moved = dot(vb[...], jnp.concatenate([p.astype(BF16) for p in pair], axis=1))
        for m in range(2):
            coarse = 1.0 - fi[n + m : n + m + 1, :].astype(F32)
            BASE[n + m] = pair[m] + TIME_STEP * (coarse * moved[:, EZ * m : EZ * m + EZ])

    loads[7].wait()
    volume(0)
    volume(2)
    for copy in copies:
        copy.wait()
    ghosts(1, -1.0)
    complete(PR, R0, 1, -1.0)

    apply(R0, 1)
    for n, (i, j) in enumerate(cells):
        parts = gathered(i, j)
        for a in range(3):
            at = slice(32 * a, 32 * a + 32)
            P0[i, j, at, :] = diag(a, n) * R0[i, j, at, :] + parts[a]
    copies = exchange(2, P0)
    zero = jnp.zeros((8, EZ), F32)

    def over_ghosts(value):
        out = zero
        for j in range(EY):
            out = out + fold(value(hx[1, j], hx[2, j], cx[1, j], upper(j, 0)))
        for i in range(EX):
            out = out + fold(value(hy[1, i], hy[2, i], cy[1, i], upper(i, 1)))
        return out

    sum_a, sum_e00 = zero, zero
    for i, j in cells:
        r = R0[i, j]
        sum_a = sum_a + fold(r * r)
        sum_e00 = sum_e00 + fold(r * P0[i, j])
    sum_e00 = sum_e00 + over_ghosts(lambda r, w, c0, c1: r * c0) + fold(hz[1] * cz[1])
    a = total(sum_a)
    e00 = total(sum_e00)
    shift = jnp.where(a > 0.0, e00 / jnp.where(a > 0.0, a, 1.0), 0.0)
    volume(4)
    volume(6)
    loads[8].wait()
    LF[...] = ltb[...].astype(F32).T.astype(BF16)
    for copy in copies:
        copy.wait()
    ghosts(2, 1.0)
    complete(P0, W1, 2, 1.0)

    apply(W1, 2)
    sum_b, sum_c, sum_e01, sum_e11 = zero, zero, zero, zero
    for n, (i, j) in enumerate(cells):
        parts = gathered(i, j)
        for k in range(3):
            at = slice(32 * k, 32 * k + 32)
            r, w, p = R0[i, j, at, :], W1[i, j, at, :], P0[i, j, at, :]
            q = w - shift * r
            sum_b = sum_b + fold(r * q)
            sum_c = sum_c + fold(q * q)
            sum_e01 = sum_e01 + fold(q * p)
            sum_e11 = sum_e11 + fold(q * (diag(k, n) * w + parts[k] - shift * p))
    top = upper_z()
    q = hz[2] - shift * hz[1]
    sum_e01 = sum_e01 + fold(q * cz[1]) + over_ghosts(lambda r, w, c0, c1: (w - shift * r) * c0)
    sum_e11 = sum_e11 + fold(q * (top - shift * cz[1]))
    sum_e11 = sum_e11 + over_ghosts(lambda r, w, c0, c1: (w - shift * r) * (c1 - shift * c0))
    row = lax.broadcasted_iota(jnp.int32, (8, EZ), 0)
    column = lax.broadcasted_iota(jnp.int32, (8, EZ), 1)
    tile = zero
    for n, value in enumerate([shift, a, total(sum_b), total(sum_c), e00, total(sum_e01), total(sum_e11)]):
        tile = jnp.where(row == n, value, tile)
    own[...] = jnp.where(column == me[0] + sizes[0] * me[1], tile, 0.0)

    def gather(axis, source, landing):
        n = sizes[axis]
        made = [
            send(source, landing.at[k - 1], names[axis], lax.rem(me[axis] + k, n)) for k in range(1, n)
        ]
        for copy in made:
            copy.wait()

    gather(0, own, ra)
    tile = own[...]
    for k in range(sizes[0] - 1):
        tile = tile + ra[k]
    own_b[...] = tile
    gather(1, own_b, rb)
    for k in range(sizes[1] - 1):
        tile = tile + rb[k]
    own_c[...] = tile
    gather(2, own_c, rc)
    tiles = [tile] + [rc[k] for k in range(sizes[2] - 1)]

    def summed(value):
        out = value(tiles[0])
        for t in tiles[1:]:
            out = out + value(t)
        return jnp.sum(out, axis=1, keepdims=True)

    norm0 = summed(lambda t: t[1:2])
    alpha0 = norm0 / summed(lambda t: t[4:5])

    def norm1_of(t):
        f = 1.0 - alpha0 * t[0:1]
        return f * f * t[1:2] - 2.0 * alpha0 * f * t[2:3] + alpha0 * alpha0 * t[3:4]

    norm1 = summed(norm1_of)
    beta = norm1 / norm0

    def energy_of(t):
        f = 1.0 + beta - alpha0 * t[0:1]
        return f * f * t[4:5] - 2.0 * alpha0 * f * t[5:6] + alpha0 * alpha0 * t[6:7]

    alpha1 = norm1 / summed(energy_of)
    on_r = alpha0 + alpha1 * (1.0 + beta)
    on_w = -alpha1 * alpha0

    for n, (i, j) in enumerate(cells):
        new = X[i, j] + on_r * R0[i, j] + on_w * W1[i, j]
        R0[i, j] = new
        XO[pl.ds(n, 96, stride=CELLS), :] = new
    out_x = pltpu.make_async_copy(XO, xo_hbm, out_sem.at[0])
    out_x.start()
    for j in range(EY):
        hx[1, j] = hx[0, j] + on_r * hx[1, j] + on_w * hx[2, j]
    for i in range(EX):
        hy[1, i] = hy[0, i] + on_r * hy[1, i] + on_w * hy[2, i]
    hz[1] = hz[0] + on_r * hz[1] + on_w * hz[2]
    for n, (i, j) in enumerate(cells):
        fine = fi[n : n + 1, :] > 0
        for at, (new, old) in enumerate(zip(faces(R0, 1, i, j), faces(X, 0, i, j))):
            GH[32 * at : 32 * at + 32, EZ * n : EZ * n + EZ] = jnp.where(fine, new, old).astype(BF16)
    for n in range(0, CELLS, 2):
        lifted = dot(LF[...], GH[:, EZ * n : EZ * n + 2 * EZ])
        for m in range(2):
            ON[pl.ds(n + m, 384, stride=CELLS), :] = BASE[n + m] + TIME_STEP * lifted[:, EZ * m : EZ * m + EZ]
    for n in range(0, 3072, 128):
        FO[n : n + 128, :] = ON[n : n + 128, :].astype(BF16)
    out_f = pltpu.make_async_copy(FO, fo_hbm, out_sem.at[1])
    out_f.start()
    out_x.wait()
    out_f.wait()


def solution(mesh):
    sizes = tuple(mesh.shape[n] for n in ("gx", "gy", "gz"))

    def body(fields, trace_old, face_load, face_diag, fine_flag, coeff, volume_op, lift_op, schur_op):
        vmem = pltpu.VMEM
        field = (EX, EY, 96, EZ)
        copies = 3 + 6 + 6 + sum(sizes) - 3
        scratch = [
            vmem((768, EZ), F32), vmem((768, EZ), F32), vmem((24, EZ), F32), vmem((8, EZ), jnp.int32),
            vmem((8, EZ), F32), vmem((3072, EZ), BF16), vmem((384, 384), BF16), vmem((192, 384), BF16),
            vmem((192, 192), F32),
            vmem(field, F32), vmem(field, F32), vmem(field, F32), vmem(field, F32), vmem(field, F32),
            vmem((CELLS, 192, EZ), F32), vmem((192, CELLS * EZ), BF16), vmem((192, CELLS * EZ), BF16),
            vmem((192, 192), BF16), vmem((192, 192), BF16), vmem((384, 192), BF16),
            vmem((3072, EZ), F32), vmem((CELLS, 384, EZ), F32), vmem((3072, EZ), F32), vmem((3072, EZ), BF16),
            vmem((768, EZ), F32),
            vmem((3, EY, FD, EZ), F32), vmem((3, EX, FD, EZ), F32), vmem((3, FD, EZ), F32),
            vmem((2, EY, FD, EZ), F32), vmem((2, EX, FD, EZ), F32), vmem((2, FD, EZ), F32),
            vmem((2, EY, FD, EZ), F32), vmem((2, EX, FD, EZ), F32), vmem((2, FD, EZ), F32),
            vmem((3, FD, EZ), F32),
            vmem((3, EY, FD, EZ), F32), vmem((3, EX, FD, EZ), F32), vmem((3, FD, EZ), F32),
            vmem((8, EZ), F32), vmem((sizes[0] - 1, 8, EZ), F32), vmem((8, EZ), F32),
            vmem((sizes[1] - 1, 8, EZ), F32), vmem((8, EZ), F32), vmem((sizes[2] - 1, 8, EZ), F32),
            pltpu.SemaphoreType.DMA((9,)), pltpu.SemaphoreType.DMA((2,)),
            pltpu.SemaphoreType.DMA((copies,)), pltpu.SemaphoreType.DMA((copies,)),
        ]
        out_f, out_x = pl.pallas_call(
            functools.partial(kernel, sizes),
            out_shape=(jax.ShapeDtypeStruct((3072, EZ), BF16), jax.ShapeDtypeStruct((768, EZ), F32)),
            in_specs=[pl.BlockSpec(memory_space=pl.ANY)] * 9,
            out_specs=(pl.BlockSpec(memory_space=pl.ANY),) * 2,
            scratch_shapes=scratch,
            compiler_params=pltpu.CompilerParams(
                collective_id=0, has_side_effects=True, vmem_limit_bytes=40 * 1024 * 1024
            ),
            name="step",
        )(
            trace_old.reshape(768, EZ), face_load.reshape(768, EZ), face_diag.reshape(24, EZ),
            fine_flag.reshape(8, EZ), coeff.reshape(8, EZ), fields.reshape(3072, EZ), volume_op, lift_op.T, schur_op,
        )
        return out_f.reshape(fields.shape), out_x.reshape(trace_old.shape)

    return jax.shard_map(
        body,
        mesh=mesh,
        in_specs=(
            P(None, "gx", "gy", "gz"),
            P(None, None, "gx", "gy", "gz"),
            P(None, None, "gx", "gy", "gz"),
            P(None, "gx", "gy", "gz"),
            P("gx", "gy", "gz"),
            P("gx", "gy", "gz"),
            P(),
            P(),
            P(),
        ),
        out_specs=(P(None, "gx", "gy", "gz"), P(None, None, "gx", "gy", "gz")),
        check_vma=False,
    )
```

```python
import functools

import jax
import jax.numpy as jnp
from jax import lax
from jax.experimental import pallas as pl
from jax.experimental.pallas import tpu as pltpu
from jax.sharding import PartitionSpec as P

MESH = pl.DeviceIdType.MESH
EX, EY, EZ = 2, 4, 128
CELLS = EX * EY
FD = 32
F32, BF16 = jnp.float32, jnp.bfloat16
TIME_STEP = 0.25


def dot(a, b):
    return jnp.dot(a, b, preferred_element_type=F32)


def fold(value):
    return jnp.sum(value.reshape(-1, 8, 128), axis=0)


def total(value):
    return jnp.sum(jnp.sum(value, axis=0, keepdims=True), axis=1, keepdims=True)


def across(sizes):
    steps = [(y, z) for y in range(sizes[0] // 2) for z in range(sizes[2]) if y or z]
    return sorted(steps, key=lambda s: -min(s[0], sizes[0] // 2 - s[0]) - min(s[1], sizes[2] - s[1]))


def along(sizes):
    steps = [(c, z) for z in range(sizes[1]) for c in range(2) if c or z]
    return sorted(steps, key=lambda s: -min(s[1], sizes[1] - s[1]) - 0.5 * s[0])


def kernel(sizes, *refs):
    (x_hbm, b_hbm, diag_hbm, fine_hbm, coeff_hbm, f_hbm, v_hbm, lt_hbm, s_hbm, FO, XO) = refs[:11]
    (xn, bn, dg, fi, co, fb, vb, ltb, sf, X, PR, R0, P0, W1, T, GH, GL, SH, SL, LF, FN, BASE, ON,
     gx, gy, gz, ux, uy, uz, cx, cy, cz, zs, hx, hy, hz, own, ra, own_b, rb,
     load_sem, send_sem, recv_sem, gather_send, gather_recv, know) = refs[11:]
    names = ("gx", "gy", "gz")
    me = [lax.axis_index(n) for n in names]
    up = [lax.rem(m + 1, n) for m, n in zip(me, sizes)]
    down = [lax.rem(m + n - 1, n) for m, n in zip(me, sizes)]
    has_up = [m < n - 1 for m, n in zip(me, sizes)]
    has_down = [m > 0 for m in me]

    loads = [
        pltpu.make_async_copy(src, dst, load_sem.at[k])
        for k, (src, dst) in enumerate(
            [(x_hbm, xn), (s_hbm, sf), (fine_hbm, fi), (coeff_hbm, co), (diag_hbm, dg), (b_hbm, bn),
             (f_hbm, fb), (v_hbm, vb), (lt_hbm, ltb)]
        )
    ]
    for copy in loads:
        copy.start()

    barrier = pltpu.get_barrier_semaphore()

    def announce(sem, steps):
        count = 0
        for axis, step in steps:
            n = sizes[axis]
            if step % n:
                target = lax.rem(me[axis] + step + n, n)
                pl.semaphore_signal(sem, inc=1, device_id={names[axis]: target}, device_id_type=MESH)
                count += 1
        return count

    near = [(axis, step) for axis in range(3) for step in (1, -1)]
    partners = announce(barrier, near)
    core = lax.rem(me[0], 2)
    other_core = me[0] + 1 - 2 * core

    started = []

    def send(src, dst, name, target):
        k = len(started)
        copy = pltpu.make_async_remote_copy(
            src_ref=src, dst_ref=dst, send_sem=send_sem.at[k], recv_sem=recv_sem.at[k],
            device_id={name: target}, device_id_type=MESH,
        )
        copy.start()
        started.append(copy)
        return copy

    lane = lax.broadcasted_iota(jnp.int32, (FD, EZ), 1)
    cells = [(i, j) for i in range(EX) for j in range(EY)]

    def keep(flag, value):
        return jnp.where(flag, value, 0.0)

    def pack(pieces, at):
        out = jnp.zeros((FD, EZ), F32)
        for n, piece in enumerate(pieces):
            out = jnp.where(lane == n, pltpu.roll(piece, (n - at) % EZ, 1), out)
        return out

    def unpack(packed, n, at):
        return pltpu.roll(packed, (at - n) % EZ, 1)

    def faces(v, k, i, j):
        n = i * EY + j
        z = v[i, j, 64:96, :]
        return [
            v[i, j, 0:32, :],
            v[i + 1, j, 0:32, :] if i + 1 < EX else hx[k, j],
            v[i, j, 32:64, :],
            v[i, j + 1, 32:64, :] if j + 1 < EY else hy[k, i],
            z,
            jnp.where(lane == EZ - 1, unpack(hz[k], n, EZ - 1), pltpu.roll(z, EZ - 1, 1)),
        ]

    def apply(v, k):
        for n, (i, j) in enumerate(cells):
            for at, block in enumerate(faces(v, k, i, j)):
                high = block.astype(BF16)
                low = (block - high.astype(F32)).astype(BF16)
                GH[32 * at : 32 * at + 32, EZ * n : EZ * n + EZ] = high
                GL[32 * at : 32 * at + 32, EZ * n : EZ * n + EZ] = low
        for n in range(0, CELLS, 2):
            cols = slice(EZ * n, EZ * n + 2 * EZ)
            high = GH[:, cols]
            product = dot(SH[...], high) + (dot(SH[...], GL[:, cols]) + dot(SL[...], high))
            for m in range(2):
                T[n + m] = product[:, EZ * m : EZ * m + EZ] * weight(n + m)

    def weight(n):
        return fi[n : n + 1, :].astype(F32) * co[n : n + 1, :]

    def gathered(i, j):
        n = i * EY + j
        along_x, along_y = T[n, 0:32, :], T[n, 64:96, :]
        if i > 0:
            along_x = along_x + T[n - EY, 32:64, :]
        if j > 0:
            along_y = along_y + T[n - 1, 96:128, :]
        along_z = T[n, 128:160, :] + jnp.where(lane == 0, 0.0, pltpu.roll(T[n, 160:192, :], 1, 1))
        return [along_x, along_y, along_z]

    def upper(i_or_j, axis):
        if axis == 0:
            return T[(EX - 1) * EY + i_or_j, 32:64, :]
        return T[i_or_j * EY + EY - 1, 96:128, :]

    def upper_z():
        return pack([T[n, 160:192, :] for n in range(CELLS)], EZ - 1)

    def diag(a, n):
        return dg[a * CELLS + n : a * CELLS + n + 1, :]

    def exchange(k, p):
        out = [send(p.at[0, :, 0:32, :], gx.at[k], "gx", down[0])]
        if k > 0:
            for j in range(EY):
                cx[k - 1, j] = upper(j, 0)
            out.append(send(cx.at[k - 1], ux.at[k - 1], "gx", up[0]))
        out.append(send(p.at[:, 0, 32:64, :], gy.at[k], "gy", down[1]))
        if k > 0:
            for i in range(EX):
                cy[k - 1, i] = upper(i, 1)
            out.append(send(cy.at[k - 1], uy.at[k - 1], "gy", up[1]))
        zs[k] = pack([p[i, j, 64:96, :] for i, j in cells], 0)
        out.append(send(zs.at[k], gz.at[k], "gz", down[2]))
        if k > 0:
            cz[k - 1] = upper_z()
            out.append(send(cz.at[k - 1], uz.at[k - 1], "gz", up[2]))
        return out

    def ghosts(k, sign):
        for j in range(EY):
            hx[k, j] = keep(has_up[0], gx[k, j] + sign * cx[k - 1, j] if k > 0 else gx[k, j])
        for i in range(EX):
            hy[k, i] = keep(has_up[1], gy[k, i] + sign * cy[k - 1, i] if k > 0 else gy[k, i])
        hz[k] = keep(has_up[2], gz[k] + sign * cz[k - 1] if k > 0 else gz[k])

    def complete(p, out, k, sign):
        for n, (i, j) in enumerate(cells):
            along_x, along_y, along_z = p[i, j, 0:32, :], p[i, j, 32:64, :], p[i, j, 64:96, :]
            if i == 0:
                along_x = along_x + sign * keep(has_down[0], ux[k - 1, j])
            if j == 0:
                along_y = along_y + sign * keep(has_down[1], uy[k - 1, i])
            below = jnp.where(lane == 0, unpack(uz[k - 1], n, 0), 0.0)
            along_z = along_z + sign * keep(has_down[2], below)
            out[i, j, 0:32, :] = along_x
            out[i, j, 32:64, :] = along_y
            out[i, j, 64:96, :] = along_z

    loads[0].wait()
    for n, (i, j) in enumerate(cells):
        X[i, j] = xn[pl.ds(n, 96, stride=CELLS), :]
    pl.semaphore_wait(barrier, partners)
    known_1 = announce(know.at[0], near)
    copies = exchange(0, X)
    loads[1].wait()
    s = sf[...]
    high = s.astype(BF16)
    SH[...] = high
    SL[...] = (s - high.astype(F32)).astype(BF16)
    loads[2].wait()
    loads[3].wait()
    loads[4].wait()
    loads[5].wait()
    loads[6].wait()
    for n in range(0, 3072, 128):
        FN[n : n + 128, :] = fb[n : n + 128, :].astype(F32)
    for copy in copies:
        copy.wait_recv()
    pl.semaphore_wait(know.at[0], known_1)
    known_2 = announce(know.at[1], [(axis, step) for axis in range(2) for step in (2, -2)])
    ghosts(0, 0.0)

    apply(X, 0)
    for n, (i, j) in enumerate(cells):
        parts = gathered(i, j)
        for a in range(3):
            load = bn[pl.ds(a * FD * CELLS + n, FD, stride=CELLS), :]
            PR[i, j, 32 * a : 32 * a + 32, :] = load - diag(a, n) * X[i, j, 32 * a : 32 * a + 32, :] - parts[a]
    copies = exchange(1, PR)

    def volume(n):
        pair = [FN[pl.ds(n + m, 384, stride=CELLS), :] for m in range(2)]
        moved = dot(vb[...], jnp.concatenate([p.astype(BF16) for p in pair], axis=1))
        for m in range(2):
            coarse = 1.0 - fi[n + m : n + m + 1, :].astype(F32)
            BASE[n + m] = pair[m] + TIME_STEP * (coarse * moved[:, EZ * m : EZ * m + EZ])

    loads[7].wait()
    volume(0)
    volume(2)
    for copy in copies:
        copy.wait_recv()
    if known_2:
        pl.semaphore_wait(know.at[1], known_2)
    known_3 = 1 + announce(know.at[2], [(2, 1), (2, -1), (2, 2)])
    pl.semaphore_signal(know.at[2], inc=1, device_id={"gx": other_core}, device_id_type=MESH)
    ghosts(1, -1.0)
    complete(PR, R0, 1, -1.0)

    apply(R0, 1)
    for n, (i, j) in enumerate(cells):
        parts = gathered(i, j)
        for a in range(3):
            at = slice(32 * a, 32 * a + 32)
            P0[i, j, at, :] = diag(a, n) * R0[i, j, at, :] + parts[a]
    copies = exchange(2, P0)
    zero = jnp.zeros((8, EZ), F32)

    def over_ghosts(value):
        out = zero
        for j in range(EY):
            out = out + fold(value(hx[1, j], hx[2, j], cx[1, j], upper(j, 0)))
        for i in range(EX):
            out = out + fold(value(hy[1, i], hy[2, i], cy[1, i], upper(i, 1)))
        return out

    sum_a, sum_e00 = zero, zero
    for i, j in cells:
        r = R0[i, j]
        sum_a = sum_a + fold(r * r)
        sum_e00 = sum_e00 + fold(r * P0[i, j])
    sum_e00 = sum_e00 + over_ghosts(lambda r, w, c0, c1: r * c0) + fold(hz[1] * cz[1])
    a = total(sum_a)
    e00 = total(sum_e00)
    shift = jnp.where(a > 0.0, e00 / jnp.where(a > 0.0, a, 1.0), 0.0)
    volume(4)
    volume(6)
    loads[8].wait()
    LF[...] = ltb[...].astype(F32).T.astype(BF16)
    for copy in copies:
        copy.wait_recv()
    pl.semaphore_wait(know.at[2], known_3)
    ghosts(2, 1.0)
    complete(P0, W1, 2, 1.0)

    apply(W1, 2)
    sum_b, sum_c, sum_e01, sum_e11 = zero, zero, zero, zero
    for n, (i, j) in enumerate(cells):
        parts = gathered(i, j)
        for k in range(3):
            at = slice(32 * k, 32 * k + 32)
            r, w, p = R0[i, j, at, :], W1[i, j, at, :], P0[i, j, at, :]
            q = w - shift * r
            sum_b = sum_b + fold(r * q)
            sum_c = sum_c + fold(q * q)
            sum_e01 = sum_e01 + fold(q * p)
            sum_e11 = sum_e11 + fold(q * (diag(k, n) * w + parts[k] - shift * p))
    top = upper_z()
    q = hz[2] - shift * hz[1]
    sum_e01 = sum_e01 + fold(q * cz[1]) + over_ghosts(lambda r, w, c0, c1: (w - shift * r) * c0)
    sum_e11 = sum_e11 + fold(q * (top - shift * cz[1]))
    sum_e11 = sum_e11 + over_ghosts(lambda r, w, c0, c1: (w - shift * r) * (c1 - shift * c0))
    row = lax.broadcasted_iota(jnp.int32, (8, EZ), 0)
    column = lax.broadcasted_iota(jnp.int32, (8, EZ), 1)
    tile = zero
    for n, value in enumerate([shift, a, total(sum_b), total(sum_c), e00, total(sum_e01), total(sum_e11)]):
        tile = jnp.where(row == n, value, tile)
    planes, layers = sizes[0] // 2, max(sizes[1] // 2, 1)
    group = planes * sizes[2]
    place = lax.div(me[0], 2) + planes * me[2] + group * (core + 2 * lax.rem(me[1], layers))
    own[...] = jnp.where(column == place, tile, 0.0)

    def gather(k, source, landing, targets):
        for n, target in enumerate(targets):
            pltpu.make_async_remote_copy(
                src_ref=source, dst_ref=landing.at[n], send_sem=gather_send.at[k], recv_sem=gather_recv.at[k],
                device_id=target, device_id_type=MESH,
            ).start()
        out = source[...]
        pltpu.make_async_copy(landing, landing, gather_recv.at[k]).wait()
        for n in range(len(targets)):
            out = out + landing[n]
        return out

    tile = gather(0, own, ra, [
        {"gx": lax.rem(me[0] + 2 * y, sizes[0]), "gz": lax.rem(me[2] + z, sizes[2])} for y, z in across(sizes)
    ])
    low = me[1] < layers
    own_b[0:8, :] = keep(low, tile)
    own_b[8:16, :] = keep(jnp.logical_not(low), tile)
    tile = gather(1, own_b, rb, [
        {"gx": other_core if c else me[0], "gy": lax.rem(me[1] + z, sizes[1])} for c, z in along(sizes)
    ])

    def summed(value):
        return jnp.sum(value(tile[0:8]) + value(tile[8:16]), axis=1, keepdims=True)

    norm0 = summed(lambda t: t[1:2])
    alpha0 = norm0 / summed(lambda t: t[4:5])

    def norm1_of(t):
        f = 1.0 - alpha0 * t[0:1]
        return f * f * t[1:2] - 2.0 * alpha0 * f * t[2:3] + alpha0 * alpha0 * t[3:4]

    norm1 = summed(norm1_of)
    beta = norm1 / norm0

    def energy_of(t):
        f = 1.0 + beta - alpha0 * t[0:1]
        return f * f * t[4:5] - 2.0 * alpha0 * f * t[5:6] + alpha0 * alpha0 * t[6:7]

    alpha1 = norm1 / summed(energy_of)
    on_r = alpha0 + alpha1 * (1.0 + beta)
    on_w = -alpha1 * alpha0

    for n, (i, j) in enumerate(cells):
        new = X[i, j] + on_r * R0[i, j] + on_w * W1[i, j]
        R0[i, j] = new
        XO[pl.ds(n, 96, stride=CELLS), :] = new
    for j in range(EY):
        hx[1, j] = hx[0, j] + on_r * hx[1, j] + on_w * hx[2, j]
    for i in range(EX):
        hy[1, i] = hy[0, i] + on_r * hy[1, i] + on_w * hy[2, i]
    hz[1] = hz[0] + on_r * hz[1] + on_w * hz[2]
    for n, (i, j) in enumerate(cells):
        fine = fi[n : n + 1, :] > 0
        for at, (new, old) in enumerate(zip(faces(R0, 1, i, j), faces(X, 0, i, j))):
            GH[32 * at : 32 * at + 32, EZ * n : EZ * n + EZ] = jnp.where(fine, new, old).astype(BF16)
    for n in range(0, CELLS, 2):
        lifted = dot(LF[...], GH[:, EZ * n : EZ * n + 2 * EZ])
        for m in range(2):
            ON[pl.ds(n + m, 384, stride=CELLS), :] = BASE[n + m] + TIME_STEP * lifted[:, EZ * m : EZ * m + EZ]
    for n in range(0, 3072, 128):
        FO[n : n + 128, :] = ON[n : n + 128, :].astype(BF16)
    for copy in started:
        copy.wait_send()
    pltpu.make_async_copy(ra, ra, gather_send.at[0]).wait()
    pltpu.make_async_copy(rb, rb, gather_send.at[1]).wait()


def solution(mesh):
    sizes = tuple(mesh.shape[n] for n in ("gx", "gy", "gz"))

    def body(fields, trace_old, face_load, face_diag, fine_flag, coeff, volume_op, lift_op, schur_op):
        vmem = pltpu.VMEM
        field = (EX, EY, 96, EZ)
        copies = 3 + 6 + 6
        group, column = len(across(sizes)), len(along(sizes))
        scratch = [
            vmem((768, EZ), F32), vmem((768, EZ), F32), vmem((24, EZ), F32), vmem((8, EZ), jnp.int32),
            vmem((8, EZ), F32), vmem((3072, EZ), BF16), vmem((384, 384), BF16), vmem((192, 384), BF16),
            vmem((192, 192), F32),
            vmem(field, F32), vmem(field, F32), vmem(field, F32), vmem(field, F32), vmem(field, F32),
            vmem((CELLS, 192, EZ), F32), vmem((192, CELLS * EZ), BF16), vmem((192, CELLS * EZ), BF16),
            vmem((192, 192), BF16), vmem((192, 192), BF16), vmem((384, 192), BF16),
            vmem((3072, EZ), F32), vmem((CELLS, 384, EZ), F32), vmem((3072, EZ), F32),
            vmem((3, EY, FD, EZ), F32), vmem((3, EX, FD, EZ), F32), vmem((3, FD, EZ), F32),
            vmem((2, EY, FD, EZ), F32), vmem((2, EX, FD, EZ), F32), vmem((2, FD, EZ), F32),
            vmem((2, EY, FD, EZ), F32), vmem((2, EX, FD, EZ), F32), vmem((2, FD, EZ), F32),
            vmem((3, FD, EZ), F32),
            vmem((3, EY, FD, EZ), F32), vmem((3, EX, FD, EZ), F32), vmem((3, FD, EZ), F32),
            vmem((8, EZ), F32), vmem((group, 8, EZ), F32), vmem((16, EZ), F32), vmem((column, 16, EZ), F32),
            pltpu.SemaphoreType.DMA((9,)),
            pltpu.SemaphoreType.DMA((copies,)), pltpu.SemaphoreType.DMA((copies,)),
            pltpu.SemaphoreType.DMA((2,)), pltpu.SemaphoreType.DMA((2,)), pltpu.SemaphoreType.REGULAR((3,)),
        ]
        out_f, out_x = pl.pallas_call(
            functools.partial(kernel, sizes),
            out_shape=(jax.ShapeDtypeStruct((3072, EZ), BF16), jax.ShapeDtypeStruct((768, EZ), F32)),
            in_specs=[pl.BlockSpec(memory_space=pltpu.HBM)] * 9,
            out_specs=(pl.BlockSpec(memory_space=pltpu.VMEM),) * 2,
            scratch_shapes=scratch,
            compiler_params=pltpu.CompilerParams(
                collective_id=0, has_side_effects=True, vmem_limit_bytes=40 * 1024 * 1024
            ),
            name="step",
        )(
            *(
                pltpu.with_memory_space_constraint(value, pltpu.HBM)
                for value in (
                    trace_old.reshape(768, EZ), face_load.reshape(768, EZ), face_diag.reshape(24, EZ),
                    fine_flag.reshape(8, EZ), coeff.reshape(8, EZ), fields.reshape(3072, EZ), volume_op, lift_op.T,
                    schur_op,
                )
            )
        )
        return out_f.reshape(fields.shape), out_x.reshape(trace_old.shape)

    return jax.shard_map(
        body,
        mesh=mesh,
        in_specs=(
            P(None, "gx", "gy", "gz"),
            P(None, None, "gx", "gy", "gz"),
            P(None, None, "gx", "gy", "gz"),
            P(None, "gx", "gy", "gz"),
            P("gx", "gy", "gz"),
            P("gx", "gy", "gz"),
            P(),
            P(),
            P(),
        ),
        out_specs=(P(None, "gx", "gy", "gz"), P(None, None, "gx", "gy", "gz")),
        check_vma=False,
    )
```

```python
import functools

import jax
import jax.numpy as jnp
from jax import lax
from jax.experimental import pallas as pl
from jax.experimental.pallas import tpu as pltpu
from jax.sharding import PartitionSpec as P

MESH = pl.DeviceIdType.MESH
EX, EY, EZ = 2, 4, 128
CELLS = EX * EY
FD = 32
F32, BF16 = jnp.float32, jnp.bfloat16
TIME_STEP = 0.25
CHUNKS = 3


def dot(a, b):
    return jnp.dot(a, b, preferred_element_type=F32)


def fold(value):
    return jnp.sum(value.reshape(-1, 8, 128), axis=0)


def total(value):
    return jnp.sum(jnp.sum(value, axis=0, keepdims=True), axis=1, keepdims=True)


def across(sizes):
    steps = [(y, z) for y in range(sizes[0] // 2) for z in range(sizes[2]) if y or z]
    return sorted(steps, key=lambda s: -min(s[0], sizes[0] // 2 - s[0]) - min(s[1], sizes[2] - s[1]))


def along(sizes):
    steps = [(c, z) for z in range(sizes[1]) for c in range(2) if c or z]
    return sorted(steps, key=lambda s: -min(s[1], sizes[1] - s[1]) - 0.5 * s[0])


def unpack(packed, n, at):
    return pltpu.roll(packed, (at - n) % EZ, 1)


def faces_of(v, hx, hy, hz, lane, i, j):
    n = i * EY + j
    z = v[i, j, 64:96, :]
    return [
        v[i, j, 0:32, :],
        v[i + 1, j, 0:32, :] if i + 1 < EX else hx[j],
        v[i, j, 32:64, :],
        v[i, j + 1, 32:64, :] if j + 1 < EY else hy[i],
        z,
        jnp.where(lane == EZ - 1, unpack(hz[...], n, EZ - 1), pltpu.roll(z, EZ - 1, 1)),
    ]


def kernel(sizes, *refs):
    (x_hbm, b_hbm, diag_hbm, fine_hbm, coeff_hbm, f_hbm, v_hbm, lt_hbm, s_hbm) = refs[:9]
    (moments, X, R0, W1, hx, hy, hz, BASE, LF, fi) = refs[9:19]
    (xn, bn, dg, co, fb, vb, ltb, sf, PR, P0, T, GH, GL, SH, SL, FN,
     gx, gy, gz, ux, uy, uz, cx, cy, cz, zs, own, ra, own_b, rb,
     load_sem, send_sem, recv_sem, gather_send, gather_recv, know) = refs[19:]
    names = ("gx", "gy", "gz")
    me = [lax.axis_index(n) for n in names]
    up = [lax.rem(m + 1, n) for m, n in zip(me, sizes)]
    down = [lax.rem(m + n - 1, n) for m, n in zip(me, sizes)]
    has_up = [m < n - 1 for m, n in zip(me, sizes)]
    has_down = [m > 0 for m in me]

    barrier = pltpu.get_barrier_semaphore()

    def announce(sem, steps):
        count = 0
        for axis, step in steps:
            n = sizes[axis]
            if step % n:
                target = lax.rem(me[axis] + step + n, n)
                pl.semaphore_signal(sem, inc=1, device_id={names[axis]: target}, device_id_type=MESH)
                count += 1
        return count

    near = [(axis, step) for axis in range(3) for step in (1, -1)]
    partners = announce(barrier, near)
    loads = [
        pltpu.make_async_copy(src, dst, load_sem.at[k])
        for k, (src, dst) in enumerate(
            [(x_hbm.at[256 * a : 256 * a + 256, :], xn.at[256 * a : 256 * a + 256, :]) for a in range(3)]
            + [(s_hbm, sf), (fine_hbm, fi), (coeff_hbm, co), (diag_hbm, dg), (b_hbm, bn),
               (f_hbm, fb), (v_hbm, vb), (lt_hbm, ltb)]
        )
    ]
    for copy in loads:
        copy.start()
    core = lax.rem(me[0], 2)
    other_core = me[0] + 1 - 2 * core

    started = []

    def send(src, dst, name, target):
        k = len(started)
        copy = pltpu.make_async_remote_copy(
            src_ref=src, dst_ref=dst, send_sem=send_sem.at[k], recv_sem=recv_sem.at[k],
            device_id={name: target}, device_id_type=MESH,
        )
        copy.start()
        started.append(copy)
        return copy

    lane = lax.broadcasted_iota(jnp.int32, (FD, EZ), 1)
    cells = [(i, j) for i in range(EX) for j in range(EY)]

    def keep(flag, value):
        return jnp.where(flag, value, 0.0)

    def pack(pieces, at):
        out = jnp.zeros((FD, EZ), F32)
        for n, piece in enumerate(pieces):
            out = jnp.where(lane == n, pltpu.roll(piece, (n - at) % EZ, 1), out)
        return out

    def faces(v, k, i, j):
        return faces_of(v, hx.at[k], hy.at[k], hz.at[k], lane, i, j)

    def apply(v, k, half):
        for n, (i, j) in enumerate(cells):
            if i != half:
                continue
            for at, block in enumerate(faces(v, k, i, j)):
                high = block.astype(BF16)
                low = (block - high.astype(F32)).astype(BF16)
                GH[32 * at : 32 * at + 32, EZ * n : EZ * n + EZ] = high
                GL[32 * at : 32 * at + 32, EZ * n : EZ * n + EZ] = low
        for n in range(EY * half, EY * half + EY, 2):
            cols = slice(EZ * n, EZ * n + 2 * EZ)
            high = GH[:, cols]
            product = dot(SH[...], high) + (dot(SH[...], GL[:, cols]) + dot(SL[...], high))
            for m in range(2):
                T[n + m] = product[:, EZ * m : EZ * m + EZ] * weight(n + m)

    def weight(n):
        return fi[n : n + 1, :].astype(F32) * co[n : n + 1, :]

    def gathered(i, j, a):
        n = i * EY + j
        at = 64 * a
        value = T[n, at : at + 32, :]
        if a == 0 and i > 0:
            value = value + T[n - EY, at + 32 : at + 64, :]
        if a == 1 and j > 0:
            value = value + T[n - 1, at + 32 : at + 64, :]
        if a == 2:
            value = value + jnp.where(lane == 0, 0.0, pltpu.roll(T[n, at + 32 : at + 64, :], 1, 1))
        return value

    def upper(i_or_j, axis):
        if axis == 0:
            return T[(EX - 1) * EY + i_or_j, 32:64, :]
        return T[i_or_j * EY + EY - 1, 96:128, :]

    def upper_z():
        return pack([T[n, 160:192, :] for n in range(CELLS)], EZ - 1)

    def diag(a, n):
        return dg[a * CELLS + n : a * CELLS + n + 1, :]

    def old_exchange(k, p):
        return [
            send(p.at[0, :, 0:32, :], gx.at[k], "gx", down[0]),
            send(p.at[:, 0, 32:64, :], gy.at[k], "gy", down[1]),
        ]

    def round_trip(v, p, k, partial):
        out = []
        done = set()

        def put(i, j, a):
            p[i, j, 32 * a : 32 * a + 32, :] = partial(i, j, a)
            done.add((i, j, a))

        apply(v, k - 1, 0)
        for j in range(EY):
            put(0, j, 0)
        out.append(send(p.at[0, :, 0:32, :], gx.at[k], "gx", down[0]))
        apply(v, k - 1, 1)
        for j in range(EY):
            cx[k - 1, j] = upper(j, 0)
        out.append(send(cx.at[k - 1], ux.at[k - 1], "gx", up[0]))
        for i in range(EX):
            put(i, 0, 1)
        out.append(send(p.at[:, 0, 32:64, :], gy.at[k], "gy", down[1]))
        for i in range(EX):
            cy[k - 1, i] = upper(i, 1)
        out.append(send(cy.at[k - 1], uy.at[k - 1], "gy", up[1]))
        for i, j in cells:
            put(i, j, 2)
        zs[k] = pack([p[i, j, 64:96, :] for i, j in cells], 0)
        out.append(send(zs.at[k], gz.at[k], "gz", down[2]))
        cz[k - 1] = upper_z()
        out.append(send(cz.at[k - 1], uz.at[k - 1], "gz", up[2]))
        for i, j in cells:
            for a in range(3):
                if (i, j, a) not in done:
                    put(i, j, a)
        return out

    def ghosts(k, sign):
        for j in range(EY):
            hx[k, j] = keep(has_up[0], gx[k, j] + sign * cx[k - 1, j] if k > 0 else gx[k, j])
        for i in range(EX):
            hy[k, i] = keep(has_up[1], gy[k, i] + sign * cy[k - 1, i] if k > 0 else gy[k, i])
        hz[k] = keep(has_up[2], gz[k] + sign * cz[k - 1] if k > 0 else gz[k])

    def complete(p, out, k, sign):
        for n, (i, j) in enumerate(cells):
            along_x, along_y, along_z = p[i, j, 0:32, :], p[i, j, 32:64, :], p[i, j, 64:96, :]
            if i == 0:
                along_x = along_x + sign * keep(has_down[0], ux[k - 1, j])
            if j == 0:
                along_y = along_y + sign * keep(has_down[1], uy[k - 1, i])
            below = jnp.where(lane == 0, unpack(uz[k - 1], n, 0), 0.0)
            along_z = along_z + sign * keep(has_down[2], below)
            out[i, j, 0:32, :] = along_x
            out[i, j, 32:64, :] = along_y
            out[i, j, 64:96, :] = along_z

    for a in range(3):
        loads[a].wait()
        for n, (i, j) in enumerate(cells):
            X[i, j, 32 * a : 32 * a + 32, :] = xn[pl.ds(256 * a + n, FD, stride=CELLS), :]
    zs[0] = pack([X[i, j, 64:96, :] for i, j in cells], 0)
    pl.semaphore_wait(barrier, partners)
    copies = old_exchange(0, X)
    copies.append(send(zs.at[0], gz.at[0], "gz", down[2]))
    known_1 = announce(know.at[0], near)
    for copy in loads[3:9]:
        copy.wait()
    s = sf[...]
    high = s.astype(BF16)
    SH[...] = high
    SL[...] = (s - high.astype(F32)).astype(BF16)
    for n in range(0, 3072, 128):
        FN[n : n + 128, :] = fb[n : n + 128, :].astype(F32)
    for copy in copies:
        copy.wait_recv()
    pl.semaphore_wait(know.at[0], known_1)
    known_2 = announce(know.at[1], [(axis, step) for axis in range(2) for step in (2, -2)])
    ghosts(0, 0.0)

    def residual(i, j, a):
        n = i * EY + j
        load = bn[pl.ds(a * FD * CELLS + n, FD, stride=CELLS), :]
        return load - diag(a, n) * X[i, j, 32 * a : 32 * a + 32, :] - gathered(i, j, a)

    copies = round_trip(X, PR, 1, residual)

    def volume(n):
        pair = [FN[pl.ds(n + m, 384, stride=CELLS), :] for m in range(2)]
        moved = dot(vb[...], jnp.concatenate([p.astype(BF16) for p in pair], axis=1))
        for m in range(2):
            coarse = 1.0 - fi[n + m : n + m + 1, :].astype(F32)
            BASE[n + m] = pair[m] + TIME_STEP * (coarse * moved[:, EZ * m : EZ * m + EZ])

    loads[9].wait()
    volume(0)
    volume(2)
    for copy in copies:
        copy.wait_recv()
    if known_2:
        pl.semaphore_wait(know.at[1], known_2)
    known_3 = 1 + announce(know.at[2], [(2, 1), (2, -1), (2, 2)])
    pl.semaphore_signal(know.at[2], inc=1, device_id={"gx": other_core}, device_id_type=MESH)
    ghosts(1, -1.0)
    complete(PR, R0, 1, -1.0)

    def image(i, j, a):
        return diag(a, i * EY + j) * R0[i, j, 32 * a : 32 * a + 32, :] + gathered(i, j, a)

    copies = round_trip(R0, P0, 2, image)
    zero = jnp.zeros((8, EZ), F32)

    def over_ghosts(value):
        out = zero
        for j in range(EY):
            out = out + fold(value(hx[1, j], hx[2, j], cx[1, j], upper(j, 0)))
        for i in range(EX):
            out = out + fold(value(hy[1, i], hy[2, i], cy[1, i], upper(i, 1)))
        return out

    sum_a, sum_e00 = zero, zero
    for i, j in cells:
        r = R0[i, j]
        sum_a = sum_a + fold(r * r)
        sum_e00 = sum_e00 + fold(r * P0[i, j])
    sum_e00 = sum_e00 + over_ghosts(lambda r, w, c0, c1: r * c0) + fold(hz[1] * cz[1])
    a = total(sum_a)
    e00 = total(sum_e00)
    shift = jnp.where(a > 0.0, e00 / jnp.where(a > 0.0, a, 1.0), 0.0)
    volume(4)
    volume(6)
    loads[10].wait()
    LF[...] = ltb[...].astype(F32).T.astype(BF16)
    for copy in copies:
        copy.wait_recv()
    pl.semaphore_wait(know.at[2], known_3)
    ghosts(2, 1.0)
    complete(P0, W1, 2, 1.0)

    apply(W1, 2, 0)
    apply(W1, 2, 1)
    sum_b, sum_c, sum_e01, sum_e11 = zero, zero, zero, zero
    for n, (i, j) in enumerate(cells):
        for k in range(3):
            at = slice(32 * k, 32 * k + 32)
            r, w, p = R0[i, j, at, :], W1[i, j, at, :], P0[i, j, at, :]
            q = w - shift * r
            sum_b = sum_b + fold(r * q)
            sum_c = sum_c + fold(q * q)
            sum_e01 = sum_e01 + fold(q * p)
            sum_e11 = sum_e11 + fold(q * (diag(k, n) * w + gathered(i, j, k) - shift * p))
    top = upper_z()
    q = hz[2] - shift * hz[1]
    sum_e01 = sum_e01 + fold(q * cz[1]) + over_ghosts(lambda r, w, c0, c1: (w - shift * r) * c0)
    sum_e11 = sum_e11 + fold(q * (top - shift * cz[1]))
    sum_e11 = sum_e11 + over_ghosts(lambda r, w, c0, c1: (w - shift * r) * (c1 - shift * c0))
    row = lax.broadcasted_iota(jnp.int32, (8, EZ), 0)
    column = lax.broadcasted_iota(jnp.int32, (8, EZ), 1)
    tile = zero
    for n, value in [(2, sum_b), (3, sum_c), (5, sum_e01), (6, sum_e11)]:
        tile = jnp.where(row == n, jnp.sum(value, axis=0, keepdims=True), tile)
    tile = jnp.broadcast_to(jnp.sum(tile, axis=1, keepdims=True), (8, EZ))
    for n, value in [(0, shift), (1, a), (4, e00)]:
        tile = jnp.where(row == n, value, tile)
    planes, layers = sizes[0] // 2, max(sizes[1] // 2, 1)
    group = planes * sizes[2]
    place = lax.div(me[0], 2) + planes * me[2] + group * (core + 2 * lax.rem(me[1], layers))
    own[...] = jnp.where(column == place, tile, 0.0)

    def gather(k, source, landing, targets):
        for n, target in enumerate(targets):
            pltpu.make_async_remote_copy(
                src_ref=source, dst_ref=landing.at[n], send_sem=gather_send.at[k], recv_sem=gather_recv.at[k],
                device_id=target, device_id_type=MESH,
            ).start()
        out = source[...]
        pltpu.make_async_copy(landing, landing, gather_recv.at[k]).wait()
        for n in range(len(targets)):
            out = out + landing[n]
        return out

    tile = gather(0, own, ra, [
        {"gx": lax.rem(me[0] + 2 * y, sizes[0]), "gz": lax.rem(me[2] + z, sizes[2])} for y, z in across(sizes)
    ])
    low = me[1] < layers
    own_b[0:8, :] = keep(low, tile)
    own_b[8:16, :] = keep(jnp.logical_not(low), tile)
    tile = gather(1, own_b, rb, [
        {"gx": other_core if c else me[0], "gy": lax.rem(me[1] + z, sizes[1])} for c, z in along(sizes)
    ])

    moments[...] = tile
    for copy in started:
        copy.wait_send()
    pltpu.make_async_copy(ra, ra, gather_send.at[0]).wait()
    pltpu.make_async_copy(rb, rb, gather_send.at[1]).wait()


def finish(*refs):
    (moments, X, R0, W1, hx, hy, hz, BASE, LF, fi, fo_hbm, xo_hbm, GH, ON, FO, XO, new_v, new_x, new_y, new_z, out_sem) = refs
    cells = [(i, j) for i in range(EX) for j in range(EY)]
    lane = lax.broadcasted_iota(jnp.int32, (FD, EZ), 1)
    tile = moments[...]

    def summed(value):
        return jnp.sum(value(tile[0:8]) + value(tile[8:16]), axis=1, keepdims=True)

    norm0 = summed(lambda t: t[1:2])
    alpha0 = norm0 / summed(lambda t: t[4:5])

    def norm1_of(t):
        f = 1.0 - alpha0 * t[0:1]
        return f * f * t[1:2] - 2.0 * alpha0 * f * t[2:3] + alpha0 * alpha0 * t[3:4]

    norm1 = summed(norm1_of)
    beta = norm1 / norm0

    def energy_of(t):
        f = 1.0 + beta - alpha0 * t[0:1]
        return f * f * t[4:5] - 2.0 * alpha0 * f * t[5:6] + alpha0 * alpha0 * t[6:7]

    alpha1 = norm1 / summed(energy_of)
    on_r = alpha0 + alpha1 * (1.0 + beta)
    on_w = -alpha1 * alpha0

    for n, (i, j) in enumerate(cells):
        new = X[i, j] + on_r * R0[i, j] + on_w * W1[i, j]
        new_v[i, j] = new
        XO[pl.ds(n, 96, stride=CELLS), :] = new
    copies = [pltpu.make_async_copy(XO, xo_hbm, out_sem.at[0])]
    copies[0].start()
    for j in range(EY):
        new_x[j] = hx[0, j] + on_r * hx[1, j] + on_w * hx[2, j]
    for i in range(EX):
        new_y[i] = hy[0, i] + on_r * hy[1, i] + on_w * hy[2, i]
    new_z[...] = hz[0] + on_r * hz[1] + on_w * hz[2]
    for n, (i, j) in enumerate(cells):
        fine = fi[n : n + 1, :] > 0
        new_faces = faces_of(new_v, new_x, new_y, new_z, lane, i, j)
        old_faces = faces_of(X, hx.at[0], hy.at[0], hz.at[0], lane, i, j)
        for at, (new, old) in enumerate(zip(new_faces, old_faces)):
            GH[32 * at : 32 * at + 32, EZ * n : EZ * n + EZ] = jnp.where(fine, new, old).astype(BF16)
    rows = 384 // CHUNKS
    for chunk in range(CHUNKS):
        at = slice(rows * chunk, rows * chunk + rows)
        for n in range(0, CELLS, 2):
            lifted = dot(LF[at, :], GH[:, EZ * n : EZ * n + 2 * EZ])
            for m in range(2):
                ON[pl.ds(rows * CELLS * chunk + n + m, rows, stride=CELLS), :] = (
                    BASE[n + m, at, :] + TIME_STEP * lifted[:, EZ * m : EZ * m + EZ]
                )
        for n in range(rows * CELLS * chunk, rows * CELLS * (chunk + 1), 128):
            FO[n : n + 128, :] = ON[n : n + 128, :].astype(BF16)
        where = slice(rows * CELLS * chunk, rows * CELLS * (chunk + 1))
        copy = pltpu.make_async_copy(FO.at[where, :], fo_hbm.at[where, :], out_sem.at[1 + chunk])
        copy.start()
        copies.append(copy)
    for copy in copies:
        copy.wait()


def solution(mesh):
    sizes = tuple(mesh.shape[n] for n in ("gx", "gy", "gz"))

    def body(fields, trace_old, face_load, face_diag, fine_flag, coeff, volume_op, lift_op, schur_op):
        vmem = pltpu.VMEM
        field = (EX, EY, 96, EZ)
        copies = 3 + 6 + 6
        group, column = len(across(sizes)), len(along(sizes))
        scratch = [
            vmem((768, EZ), F32), vmem((768, EZ), F32), vmem((24, EZ), F32),
            vmem((8, EZ), F32), vmem((3072, EZ), BF16), vmem((384, 384), BF16), vmem((192, 384), BF16),
            vmem((192, 192), F32),
            vmem(field, F32), vmem(field, F32),
            vmem((CELLS, 192, EZ), F32), vmem((192, CELLS * EZ), BF16), vmem((192, CELLS * EZ), BF16),
            vmem((192, 192), BF16), vmem((192, 192), BF16),
            vmem((3072, EZ), F32),
            vmem((3, EY, FD, EZ), F32), vmem((3, EX, FD, EZ), F32), vmem((3, FD, EZ), F32),
            vmem((2, EY, FD, EZ), F32), vmem((2, EX, FD, EZ), F32), vmem((2, FD, EZ), F32),
            vmem((2, EY, FD, EZ), F32), vmem((2, EX, FD, EZ), F32), vmem((2, FD, EZ), F32),
            vmem((3, FD, EZ), F32),
            vmem((8, EZ), F32), vmem((group, 8, EZ), F32), vmem((16, EZ), F32), vmem((column, 16, EZ), F32),
            pltpu.SemaphoreType.DMA((11,)),
            pltpu.SemaphoreType.DMA((copies,)), pltpu.SemaphoreType.DMA((copies,)),
            pltpu.SemaphoreType.DMA((2,)), pltpu.SemaphoreType.DMA((2,)), pltpu.SemaphoreType.REGULAR((3,)),
        ]
        state = [
            ((16, EZ), F32), (field, F32), (field, F32), (field, F32),
            ((3, EY, FD, EZ), F32), ((3, EX, FD, EZ), F32), ((3, FD, EZ), F32),
            ((CELLS, 384, EZ), F32), ((384, 192), BF16), ((8, EZ), jnp.int32),
        ]
        in_vmem = pl.BlockSpec(memory_space=pltpu.VMEM)
        kept = pl.pallas_call(
            functools.partial(kernel, sizes),
            out_shape=[jax.ShapeDtypeStruct(*entry) for entry in state],
            in_specs=[pl.BlockSpec(memory_space=pltpu.HBM)] * 9,
            out_specs=[in_vmem] * len(state),
            scratch_shapes=scratch,
            compiler_params=pltpu.CompilerParams(
                collective_id=0, has_side_effects=True, vmem_limit_bytes=32 * 1024 * 1024
            ),
            name="step",
        )(
            *(
                pltpu.with_memory_space_constraint(value, pltpu.HBM)
                for value in (
                    trace_old.reshape(768, EZ), face_load.reshape(768, EZ), face_diag.reshape(24, EZ),
                    fine_flag.reshape(8, EZ), coeff.reshape(8, EZ), fields.reshape(3072, EZ), volume_op, lift_op.T,
                    schur_op,
                )
            )
        )
        out_f, out_x = pl.pallas_call(
            finish,
            out_shape=(jax.ShapeDtypeStruct((3072, EZ), BF16), jax.ShapeDtypeStruct((768, EZ), F32)),
            in_specs=[in_vmem] * len(state),
            out_specs=(pl.BlockSpec(memory_space=pltpu.HBM),) * 2,
            scratch_shapes=[
                vmem((192, CELLS * EZ), BF16), vmem((3072, EZ), F32), vmem((3072, EZ), BF16), vmem((768, EZ), F32),
                vmem(field, F32), vmem((EY, FD, EZ), F32), vmem((EX, FD, EZ), F32), vmem((FD, EZ), F32),
                pltpu.SemaphoreType.DMA((1 + CHUNKS,)),
            ],
            compiler_params=pltpu.CompilerParams(vmem_limit_bytes=24 * 1024 * 1024),
            name="finish",
        )(*kept)
        return out_f.reshape(fields.shape), out_x.reshape(trace_old.shape)

    return jax.shard_map(
        body,
        mesh=mesh,
        in_specs=(
            P(None, "gx", "gy", "gz"),
            P(None, None, "gx", "gy", "gz"),
            P(None, None, "gx", "gy", "gz"),
            P(None, "gx", "gy", "gz"),
            P("gx", "gy", "gz"),
            P("gx", "gy", "gz"),
            P(),
            P(),
            P(),
        ),
        out_specs=(P(None, "gx", "gy", "gz"), P(None, None, "gx", "gy", "gz")),
        check_vma=False,
    )
```

```python
import functools

import jax
import jax.numpy as jnp
from jax import lax
from jax.experimental import pallas as pl
from jax.experimental.pallas import tpu as pltpu
from jax.sharding import PartitionSpec as P

MESH = pl.DeviceIdType.MESH
EX, EY, EZ = 2, 4, 128
CELLS = EX * EY
FD = 32
F32, BF16 = jnp.float32, jnp.bfloat16
TIME_STEP = 0.25
CHUNKS = 3


def dot(a, b):
    return jnp.dot(a, b, preferred_element_type=F32)


def fold(value):
    return jnp.sum(value.reshape(-1, 8, 128), axis=0)


def total(value):
    return jnp.sum(jnp.sum(value, axis=0, keepdims=True), axis=1, keepdims=True)


def across(sizes):
    steps = [(y, z) for y in range(sizes[0] // 2) for z in range(sizes[2]) if y or z]
    return sorted(steps, key=lambda s: -min(s[0], sizes[0] // 2 - s[0]) - min(s[1], sizes[2] - s[1]))


def along(sizes):
    steps = [(c, z) for z in range(sizes[1]) for c in range(2) if c or z]
    return sorted(steps, key=lambda s: -min(s[1], sizes[1] - s[1]) - 0.5 * s[0])


def unpack(packed, n, at):
    return pltpu.roll(packed, (at - n) % EZ, 1)


def faces_of(v, hx, hy, hz, lane, i, j):
    n = i * EY + j
    z = v[i, j, 64:96, :]
    return [
        v[i, j, 0:32, :],
        v[i + 1, j, 0:32, :] if i + 1 < EX else hx[j],
        v[i, j, 32:64, :],
        v[i, j + 1, 32:64, :] if j + 1 < EY else hy[i],
        z,
        jnp.where(lane == EZ - 1, unpack(hz[...], n, EZ - 1), pltpu.roll(z, EZ - 1, 1)),
    ]


def kernel(sizes, *refs):
    (x_hbm, b_hbm, diag_hbm, fine_hbm, coeff_hbm, f_hbm, v_hbm, lt_hbm, s_hbm) = refs[:9]
    (moments, X, R0, W1, hx, hy, hz, BASE, LF, fi) = refs[9:19]
    (xn, bn, dg, co, fb, vb, ltb, sf, PR, P0, T, GH, GL, SH, SL, FN,
     gx, gy, gz, ux, uy, uz, cx, cy, cz, zs, own, ra, own_b, rb,
     wt, px, py, near_w, edge, pair_xy, corner, CH, CL,
     load_sem, send_sem, recv_sem, gather_send, gather_recv, know) = refs[19:]
    names = ("gx", "gy", "gz")
    me = [lax.axis_index(n) for n in names]
    has_up = [m < n - 1 for m, n in zip(me, sizes)]
    has_down = [m > 0 for m in me]

    barrier = pltpu.get_barrier_semaphore()

    ring = [[m] + [lax.rem(m + k, n) for k in range(1, n)] for m, n in zip(me, sizes)]

    def at(*steps):
        return {
            names[axis]: ring[axis][step % sizes[axis]] for axis, step in enumerate(steps) if step
        }

    def announce(sem, steps):
        count = 0
        for each in steps:
            if any(step % n for step, n in zip(each, sizes)):
                pl.semaphore_signal(sem, inc=1, device_id=at(*each), device_id_type=MESH)
                count += 1
        return count

    near = [(1, 0, 0), (-1, 0, 0), (0, 1, 0), (0, -1, 0), (0, 0, 1), (0, 0, -1)]
    both = [(p, q) for p in (1, -1) for q in (1, -1)]
    diagonal = [(p, q, 0) for p, q in both] + [(p, 0, q) for p, q in both] + [(0, p, q) for p, q in both]
    loads = [
        pltpu.make_async_copy(src, dst, load_sem.at[k])
        for k, (src, dst) in enumerate(
            [(x_hbm.at[256 * a : 256 * a + 256, :], xn.at[256 * a : 256 * a + 256, :]) for a in range(3)]
            + [(fine_hbm, fi), (coeff_hbm, co), (s_hbm, sf), (diag_hbm, dg), (b_hbm, bn),
               (f_hbm, fb), (v_hbm, vb), (lt_hbm, ltb)]
        )
    ]
    for copy in loads[:3]:
        copy.start()
    partners = announce(barrier, near + diagonal)
    for copy in loads[3:8]:
        copy.start()
    core = lax.rem(me[0], 2)
    other_core = me[0] + 1 - 2 * core

    started = []

    def send(src, dst, *steps):
        k = len(started)
        copy = pltpu.make_async_remote_copy(
            src_ref=src, dst_ref=dst, send_sem=send_sem.at[k], recv_sem=recv_sem.at[k],
            device_id=at(*steps), device_id_type=MESH,
        )
        copy.start()
        started.append(copy)
        return copy

    lane = lax.broadcasted_iota(jnp.int32, (FD, EZ), 1)
    cells = [(i, j) for i in range(EX) for j in range(EY)]

    def keep(flag, value):
        return jnp.where(flag, value, 0.0)

    def pack(pieces, lane_of, first=0, out=None):
        out = jnp.zeros((FD, EZ), F32) if out is None else out
        for n, piece in enumerate(pieces, first):
            out = jnp.where(lane == n, pltpu.roll(piece, (n - lane_of) % EZ, 1), out)
        return out

    def faces(v, k, i, j):
        return faces_of(v, hx.at[k], hy.at[k], hz.at[k], lane, i, j)

    def apply(v, k, half):
        for n, (i, j) in enumerate(cells):
            if i != half:
                continue
            for at, block in enumerate(faces(v, k, i, j)):
                high = block.astype(BF16)
                low = (block - high.astype(F32)).astype(BF16)
                GH[32 * at : 32 * at + 32, EZ * n : EZ * n + EZ] = high
                GL[32 * at : 32 * at + 32, EZ * n : EZ * n + EZ] = low
        for n in range(EY * half, EY * half + EY, 2):
            cols = slice(EZ * n, EZ * n + 2 * EZ)
            high = GH[:, cols]
            product = dot(SH[...], high) + (dot(SH[...], GL[:, cols]) + dot(SL[...], high))
            for m in range(2):
                T[n + m] = product[:, EZ * m : EZ * m + EZ] * weight(n + m)

    def weight(n):
        return wt[n : n + 1, :]

    def gathered(i, j, a):
        n = i * EY + j
        at = 64 * a
        value = T[n, at : at + 32, :]
        if a == 0 and i > 0:
            value = value + T[n - EY, at + 32 : at + 64, :]
        if a == 1 and j > 0:
            value = value + T[n - 1, at + 32 : at + 64, :]
        if a == 2:
            value = value + jnp.where(lane == 0, 0.0, pltpu.roll(T[n, at + 32 : at + 64, :], 1, 1))
        return value

    def upper(i_or_j, axis):
        if axis == 0:
            return T[(EX - 1) * EY + i_or_j, 32:64, :]
        return T[i_or_j * EY + EY - 1, 96:128, :]

    def upper_z():
        return pack([T[n, 160:192, :] for n in range(CELLS)], EZ - 1)

    def diag(a, n):
        return dg[a * CELLS + n : a * CELLS + n + 1, :]

    def round_trip(v, p, k, partial):
        out = []
        done = set()

        def put(i, j, a):
            p[i, j, 32 * a : 32 * a + 32, :] = partial(i, j, a)
            done.add((i, j, a))

        apply(v, k - 1, 0)
        for j in range(EY):
            put(0, j, 0)
        out.append(send(p.at[0, :, 0:32, :], gx.at[k], -1, 0, 0))
        apply(v, k - 1, 1)
        for j in range(EY):
            cx[k - 1, j] = upper(j, 0)
        out.append(send(cx.at[k - 1], ux.at[k - 1], 1, 0, 0))
        for i in range(EX):
            put(i, 0, 1)
        out.append(send(p.at[:, 0, 32:64, :], gy.at[k], 0, -1, 0))
        for i in range(EX):
            cy[k - 1, i] = upper(i, 1)
        out.append(send(cy.at[k - 1], uy.at[k - 1], 0, 1, 0))
        for i, j in cells:
            put(i, j, 2)
        zs[k] = pack([p[i, j, 64:96, :] for i, j in cells], 0)
        out.append(send(zs.at[k], gz.at[k], 0, 0, -1))
        cz[k - 1] = upper_z()
        out.append(send(cz.at[k - 1], uz.at[k - 1], 0, 0, 1))
        for i, j in cells:
            for a in range(3):
                if (i, j, a) not in done:
                    put(i, j, a)
        return out

    def ghosts(k, own_x, own_y, own_z):
        for j in range(EY):
            hx[k, j] = keep(has_up[0], gx[k, j] + own_x(j))
        for i in range(EX):
            hy[k, i] = keep(has_up[1], gy[k, i] + own_y(i))
        hz[k] = keep(has_up[2], gz[k] + own_z())

    def complete(p, out, k, sign):
        for n, (i, j) in enumerate(cells):
            along_x, along_y, along_z = p[i, j, 0:32, :], p[i, j, 32:64, :], p[i, j, 64:96, :]
            if i == 0:
                along_x = along_x + sign * keep(has_down[0], ux[k - 1, j])
            if j == 0:
                along_y = along_y + sign * keep(has_down[1], uy[k - 1, i])
            below = jnp.where(lane == 0, unpack(uz[k - 1], n, 0), 0.0)
            along_z = along_z + sign * keep(has_down[2], below)
            out[i, j, 0:32, :] = along_x
            out[i, j, 32:64, :] = along_y
            out[i, j, 64:96, :] = along_z

    for a in range(3):
        loads[a].wait()
        for n, (i, j) in enumerate(cells):
            X[i, j, 32 * a : 32 * a + 32, :] = xn[pl.ds(256 * a + n, FD, stride=CELLS), :]
    low_x = [X[0, j, 0:32, :] for j in range(EY)]
    low_y = [X[i, 0, 32:64, :] for i in range(EX)]
    low_z = [X[i, j, 64:96, :] for i, j in cells]
    zs[0] = pack(low_y, 0, 12, pack(low_x, 0, 8, pack(low_z, 0)))
    edge[...] = pack(low_y, EZ - 1, 12, pack(low_x, EZ - 1, 8))
    pl.semaphore_wait(barrier, partners)
    copies = [
        send(X.at[0, 0, 0:64, :], pair_xy, -1, -1, 0),
        send(X.at[1, 0, 32:64, :], corner.at[0], 1, -1, 0),
        send(X.at[0, EY - 1, 0:32, :], corner.at[1], -1, 1, 0),
        send(zs.at[0], corner.at[2], -1, 0, -1),
        send(zs.at[0], corner.at[3], 1, 0, -1),
        send(edge, corner.at[4], -1, 0, 1),
        send(zs.at[0], corner.at[5], 0, -1, -1),
        send(zs.at[0], corner.at[6], 0, 1, -1),
        send(edge, corner.at[7], 0, -1, 1),
        send(X.at[0, :, 0:32, :], gx.at[0], -1, 0, 0),
        send(X.at[:, 0, 32:64, :], gy.at[0], 0, -1, 0),
        send(zs.at[0], gz.at[0], 0, 0, -1),
    ]
    for copy in loads[8:]:
        copy.start()
    for copy in loads[3:8]:
        copy.wait()
    wt[...] = fi[...].astype(F32) * co[...]
    s = sf[...]
    high = s.astype(BF16)
    SH[...] = high
    SL[...] = (s - high.astype(F32)).astype(BF16)
    hx[0] = jnp.zeros((EY, FD, EZ), F32)
    hy[0] = jnp.zeros((EX, FD, EZ), F32)
    hz[0] = jnp.zeros((FD, EZ), F32)

    def residual(i, j, a):
        n = i * EY + j
        load = bn[pl.ds(a * FD * CELLS + n, FD, stride=CELLS), :]
        return load - diag(a, n) * X[i, j, 32 * a : 32 * a + 32, :] - gathered(i, j, a)

    apply(X, 0, 0)
    for j in range(EY):
        px[j] = residual(0, j, 0)
    copies.append(send(px, gx.at[1], -1, 0, 0))
    apply(X, 0, 1)
    for j in range(EY):
        cx[0, j] = upper(j, 0)
    copies.append(send(cx.at[0], ux.at[0], 1, 0, 0))
    for i in range(EX):
        py[i] = residual(i, 0, 1)
        cy[0, i] = upper(i, 1)
    copies.append(send(py, gy.at[1], 0, -1, 0))
    copies.append(send(cy.at[0], uy.at[0], 0, 1, 0))
    zs[1] = pack([residual(i, j, 2) for i, j in cells], 0)
    cz[0] = upper_z()
    copies.append(send(zs.at[1], gz.at[1], 0, 0, -1))
    copies.append(send(cz.at[0], uz.at[0], 0, 0, 1))
    for n, step in enumerate(near):
        copies.append(send(wt, near_w.at[n], *step))
    known_1 = announce(know.at[0], near)

    def put(block, first, value):
        cols = slice(first, first + value.shape[1])
        high = value.astype(BF16)
        CH[32 * block : 32 * block + 32, cols] = high
        CL[32 * block : 32 * block + 32, cols] = (value - high.astype(F32)).astype(BF16)

    CH[...] = jnp.zeros(CH.shape, BF16)
    CL[...] = jnp.zeros(CL.shape, BF16)
    for j in range(EY):
        put(1, EZ * j, low_x[j])
    for i in range(EX):
        put(3, 1024 + EZ * i, low_y[i])
    put(5, 1536, zs[0])

    def volume(n):
        pair = [FN[pl.ds(n + m, 384, stride=CELLS), :] for m in range(2)]
        moved = dot(vb[...], jnp.concatenate([p.astype(BF16) for p in pair], axis=1))
        for m in range(2):
            coarse = 1.0 - fi[n + m : n + m + 1, :].astype(F32)
            BASE[n + m] = pair[m] + TIME_STEP * (coarse * moved[:, EZ * m : EZ * m + EZ])

    loads[8].wait()
    for n in range(0, 3072, 128):
        FN[n : n + 128, :] = fb[n : n + 128, :].astype(F32)
    loads[9].wait()
    volume(0)
    volume(2)
    for copy in copies[:12]:
        copy.wait_recv()
    ghosts(0, lambda j: 0.0, lambda i: 0.0, lambda: 0.0)

    def last(packed, n):
        return jnp.where(lane == EZ - 1, unpack(packed, n, EZ - 1), 0.0)

    def moved(packed, n, to):
        return jnp.where(lane == to, unpack(packed, n, to), 0.0)

    def over(axis, value):
        return keep(has_up[axis], value)

    put(3, 384, over(1, corner[0]))
    put(3, 896, over(1, pair_xy[32:64, :]))
    put(1, 1152, over(0, corner[1]))
    put(1, 1408, over(0, pair_xy[0:32, :]))
    for j in range(EY):
        put(5, EZ * j, over(2, last(corner[3], EY + j)))
        put(5, 512 + EZ * j, over(2, last(corner[2], j)))
    for i in range(EX):
        put(5, 1024 + EZ * i, over(2, last(corner[6], i * EY + EY - 1)))
        put(5, 1280 + EZ * i, over(2, last(corner[5], i * EY)))
    second = jnp.logical_and(lane >= EY, lane < 2 * EY)
    put(1, 1536, over(0, jnp.where(second, pltpu.roll(corner[4], EZ - 4, 1), 0.0)))
    put(1, 1664, over(0, jnp.where(second, pltpu.roll(corner[2], EZ - 4, 1), 0.0)))
    put(3, 1536, over(1, moved(corner[7], 12, EY - 1) + moved(corner[7], 13, 2 * EY - 1)))
    put(3, 1664, over(1, moved(corner[5], 12, EY - 1) + moved(corner[5], 13, 2 * EY - 1)))

    def correction(block, first, size):
        rows, cols = slice(32 * block, 32 * block + 32), slice(first, first + size)
        high = CH[:, cols]
        return dot(SH[rows, :], high) + (dot(SH[rows, :], CL[:, cols]) + dot(SL[rows, :], high))

    def ends(n, at):
        out = jnp.zeros((1, EZ), F32)
        for c in range(CELLS):
            out = jnp.where(lane[0:1] == c, jnp.broadcast_to(near_w[n, c : c + 1, at : at + 1], (1, EZ)), out)
        return out

    def cut(value, n):
        return value[:, EZ * n : EZ * n + EZ]

    xl, xh = correction(1, 0, 512), correction(0, 512, 512)
    yl, yh = correction(3, 1024, 256), correction(2, 1280, 256)
    zl, zh = correction(5, 1536, 128), correction(4, 1664, 128)
    apply(X, 0, 0)
    apply(X, 0, 1)
    for i, j in cells:
        for a in range(3):
            PR[i, j, 32 * a : 32 * a + 32, :] = residual(i, j, a)
    for copy in copies[12:]:
        copy.wait_recv()
    pl.semaphore_wait(know.at[0], known_1)

    xl = [cut(xl, j) * near_w[0, EY + j : EY + j + 1, :] for j in range(EY)]
    xh = [cut(xh, j) * near_w[1, j : j + 1, :] for j in range(EY)]
    yl = [cut(yl, i) * near_w[2, i * EY + EY - 1 : i * EY + EY, :] for i in range(EX)]
    yh = [cut(yh, i) * near_w[3, i * EY : i * EY + 1, :] for i in range(EX)]
    zl = zl * ends(4, EZ - 1)
    zh = zh * ends(5, 0)

    for n, (i, j) in enumerate(cells):
        along_x, along_y, along_z = PR[i, j, 0:32, :], PR[i, j, 32:64, :], PR[i, j, 64:96, :]
        if i == 0:
            along_x = along_x - keep(has_down[0], ux[0, j] + xl[j])
        if j == 0:
            along_y = along_y - keep(has_down[1], uy[0, i] + yl[i])
        below = jnp.where(lane == 0, unpack(uz[0] + zl, n, 0), 0.0)
        R0[i, j, 0:32, :] = along_x
        R0[i, j, 32:64, :] = along_y
        R0[i, j, 64:96, :] = along_z - keep(has_down[2], below)
    ghosts(1, lambda j: -xh[j] - upper(j, 0), lambda i: -yh[i] - upper(i, 1), lambda: -zh - upper_z())

    def image(i, j, a):
        return diag(a, i * EY + j) * R0[i, j, 32 * a : 32 * a + 32, :] + gathered(i, j, a)

    early = list(started)
    copies = round_trip(R0, P0, 2, image)
    known_2 = announce(know.at[1], [(2, 0, 0), (-2, 0, 0), (0, 2, 0), (0, -2, 0), (2, 0, 1), (-2, 0, -1)])
    for copy in early:
        copy.wait_send()
    zero = jnp.zeros((8, EZ), F32)

    def over_ghosts(value):
        out = zero
        for j in range(EY):
            out = out + fold(value(hx[1, j], hx[2, j], cx[1, j], upper(j, 0)))
        for i in range(EX):
            out = out + fold(value(hy[1, i], hy[2, i], cy[1, i], upper(i, 1)))
        return out

    sum_a, sum_e00 = zero, zero
    for i, j in cells:
        r = R0[i, j]
        sum_a = sum_a + fold(r * r)
        sum_e00 = sum_e00 + fold(r * P0[i, j])
    sum_e00 = sum_e00 + over_ghosts(lambda r, w, c0, c1: r * c0) + fold(hz[1] * cz[1])
    a = total(sum_a)
    e00 = total(sum_e00)
    shift = jnp.where(a > 0.0, e00 / jnp.where(a > 0.0, a, 1.0), 0.0)
    volume(4)
    volume(6)
    loads[10].wait()
    LF[...] = ltb[...].astype(F32).T.astype(BF16)
    for copy in copies:
        copy.wait_recv()
    if known_2:
        pl.semaphore_wait(know.at[1], known_2)
    ghosts(2, lambda j: cx[1, j], lambda i: cy[1, i], lambda: cz[1])
    complete(P0, W1, 2, 1.0)

    apply(W1, 2, 0)
    apply(W1, 2, 1)
    sum_b, sum_c, sum_e01, sum_e11 = zero, zero, zero, zero
    for n, (i, j) in enumerate(cells):
        for k in range(3):
            at = slice(32 * k, 32 * k + 32)
            r, w, p = R0[i, j, at, :], W1[i, j, at, :], P0[i, j, at, :]
            q = w - shift * r
            sum_b = sum_b + fold(r * q)
            sum_c = sum_c + fold(q * q)
            sum_e01 = sum_e01 + fold(q * p)
            sum_e11 = sum_e11 + fold(q * (diag(k, n) * w + gathered(i, j, k) - shift * p))
    top = upper_z()
    q = hz[2] - shift * hz[1]
    sum_e01 = sum_e01 + fold(q * cz[1]) + over_ghosts(lambda r, w, c0, c1: (w - shift * r) * c0)
    sum_e11 = sum_e11 + fold(q * (top - shift * cz[1]))
    sum_e11 = sum_e11 + over_ghosts(lambda r, w, c0, c1: (w - shift * r) * (c1 - shift * c0))
    row = lax.broadcasted_iota(jnp.int32, (8, EZ), 0)
    column = lax.broadcasted_iota(jnp.int32, (1, EZ), 1)
    tile = zero
    for n, value in [(2, sum_b), (3, sum_c), (5, sum_e01), (6, sum_e11)]:
        tile = jnp.where(row == n, jnp.sum(value, axis=0, keepdims=True), tile)
    tile = jnp.broadcast_to(jnp.sum(tile, axis=1, keepdims=True), (8, EZ))
    for n, value in [(0, shift), (1, a), (4, e00)]:
        tile = jnp.where(row == n, value, tile)
    place = lax.div(me[0], 2) + sizes[0] // 2 * me[2]
    mine = lax.broadcasted_iota(jnp.int32, (8, EZ), 1) == 16 * row + place
    own[...] = jnp.sum(jnp.where(mine, tile, 0.0), axis=0, keepdims=True)

    def gather(k, source, landing, targets, sent):
        for n, target in enumerate(targets):
            pltpu.make_async_remote_copy(
                src_ref=source, dst_ref=landing.at[n], send_sem=gather_send.at[k], recv_sem=gather_recv.at[k],
                device_id=target, device_id_type=MESH,
            ).start()
        sent()
        pltpu.make_async_copy(landing, landing, gather_recv.at[k]).wait()

    gather(0, own, ra, [
        {"gx": ring[0][2 * y], "gz": ring[2][z]} for y, z in across(sizes)
    ], lambda: [copy.wait_send() for copy in copies])
    total_row = own[...]
    for n in range(ra.shape[0]):
        total_row = total_row + ra[n]
    own_b[...] = total_row
    gather(1, own_b, rb, [
        {"gx": other_core if c else me[0], "gy": ring[1][z]} for c, z in along(sizes)
    ], lambda: pltpu.make_async_copy(ra, ra, gather_send.at[0]).wait())
    rows = lax.broadcasted_iota(jnp.int32, (16, EZ), 0)
    tile = jnp.where(rows == 0, total_row, 0.0)
    for n in range(rb.shape[0]):
        tile = jnp.where(rows == n + 1, rb[n], tile)
    moments[...] = tile
    pltpu.make_async_copy(rb, rb, gather_send.at[1]).wait()


def finish(*refs):
    (moments, X, R0, W1, hx, hy, hz, BASE, LF, fi, fo_hbm, xo_hbm, GH, ON, FO, XO, new_v, new_x, new_y, new_z, out_sem) = refs
    cells = [(i, j) for i in range(EX) for j in range(EY)]
    lane = lax.broadcasted_iota(jnp.int32, (FD, EZ), 1)
    tile = moments[...]

    held = lax.broadcasted_iota(jnp.int32, (16, EZ), 1) < 16

    def number(n):
        return jnp.where(held, pltpu.roll(tile, EZ - 16 * n, 1) if n else tile, 0.0)

    shift, a, b, c, e00, e01, e11 = [number(n) for n in range(7)]

    def summed(value):
        return jnp.sum(jnp.sum(value, axis=0, keepdims=True), axis=1, keepdims=True)

    norm0, energy0 = summed(a), summed(e00)
    alpha0 = norm0 / energy0
    f = 1.0 - alpha0 * shift
    norm1 = summed(f * f * a - 2.0 * alpha0 * f * b + alpha0 * alpha0 * c)
    energy1 = summed(f * f * e00 - 2.0 * alpha0 * f * e01 + alpha0 * alpha0 * e11)
    mixed = summed(f * e00 - alpha0 * e01)
    beta = norm1 / norm0
    alpha1 = norm1 / (energy1 + 2.0 * beta * mixed + beta * beta * energy0)
    on_r = alpha0 + alpha1 * (1.0 + beta)
    on_w = -alpha1 * alpha0

    for n, (i, j) in enumerate(cells):
        new = X[i, j] + on_r * R0[i, j] + on_w * W1[i, j]
        new_v[i, j] = new
        XO[pl.ds(n, 96, stride=CELLS), :] = new
    copies = [pltpu.make_async_copy(XO, xo_hbm, out_sem.at[0])]
    copies[0].start()
    for j in range(EY):
        new_x[j] = hx[0, j] + on_r * hx[1, j] + on_w * hx[2, j]
    for i in range(EX):
        new_y[i] = hy[0, i] + on_r * hy[1, i] + on_w * hy[2, i]
    new_z[...] = hz[0] + on_r * hz[1] + on_w * hz[2]
    for n, (i, j) in enumerate(cells):
        fine = fi[n : n + 1, :] > 0
        new_faces = faces_of(new_v, new_x, new_y, new_z, lane, i, j)
        old_faces = faces_of(X, hx.at[0], hy.at[0], hz.at[0], lane, i, j)
        for at, (new, old) in enumerate(zip(new_faces, old_faces)):
            GH[32 * at : 32 * at + 32, EZ * n : EZ * n + EZ] = jnp.where(fine, new, old).astype(BF16)
    rows = 384 // CHUNKS
    for chunk in range(CHUNKS):
        at = slice(rows * chunk, rows * chunk + rows)
        for n in range(0, CELLS, 2):
            lifted = dot(LF[at, :], GH[:, EZ * n : EZ * n + 2 * EZ])
            for m in range(2):
                ON[pl.ds(rows * CELLS * chunk + n + m, rows, stride=CELLS), :] = (
                    BASE[n + m, at, :] + TIME_STEP * lifted[:, EZ * m : EZ * m + EZ]
                )
        for n in range(rows * CELLS * chunk, rows * CELLS * (chunk + 1), 128):
            FO[n : n + 128, :] = ON[n : n + 128, :].astype(BF16)
        where = slice(rows * CELLS * chunk, rows * CELLS * (chunk + 1))
        copy = pltpu.make_async_copy(FO.at[where, :], fo_hbm.at[where, :], out_sem.at[1 + chunk])
        copy.start()
        copies.append(copy)
    for copy in copies:
        copy.wait()


def solution(mesh):
    sizes = tuple(mesh.shape[n] for n in ("gx", "gy", "gz"))

    def body(fields, trace_old, face_load, face_diag, fine_flag, coeff, volume_op, lift_op, schur_op):
        vmem = pltpu.VMEM
        field = (EX, EY, 96, EZ)
        copies = 12 + 6 + 6 + 6
        group, column = len(across(sizes)), len(along(sizes))
        scratch = [
            vmem((768, EZ), F32), vmem((768, EZ), F32), vmem((24, EZ), F32),
            vmem((8, EZ), F32), vmem((3072, EZ), BF16), vmem((384, 384), BF16), vmem((192, 384), BF16),
            vmem((192, 192), F32),
            vmem(field, F32), vmem(field, F32),
            vmem((CELLS, 192, EZ), F32), vmem((192, CELLS * EZ), BF16), vmem((192, CELLS * EZ), BF16),
            vmem((192, 192), BF16), vmem((192, 192), BF16),
            vmem((3072, EZ), F32),
            vmem((3, EY, FD, EZ), F32), vmem((3, EX, FD, EZ), F32), vmem((3, FD, EZ), F32),
            vmem((2, EY, FD, EZ), F32), vmem((2, EX, FD, EZ), F32), vmem((2, FD, EZ), F32),
            vmem((2, EY, FD, EZ), F32), vmem((2, EX, FD, EZ), F32), vmem((2, FD, EZ), F32),
            vmem((3, FD, EZ), F32),
            vmem((1, EZ), F32), vmem((group, 1, EZ), F32), vmem((1, EZ), F32), vmem((column, 1, EZ), F32),
            vmem((8, EZ), F32), vmem((EY, FD, EZ), F32), vmem((EX, FD, EZ), F32), vmem((6, 8, EZ), F32), vmem((FD, EZ), F32), vmem((64, EZ), F32), vmem((8, FD, EZ), F32),
            vmem((192, 1792), BF16), vmem((192, 1792), BF16),
            pltpu.SemaphoreType.DMA((11,)),
            pltpu.SemaphoreType.DMA((copies,)), pltpu.SemaphoreType.DMA((copies,)),
            pltpu.SemaphoreType.DMA((2,)), pltpu.SemaphoreType.DMA((2,)), pltpu.SemaphoreType.REGULAR((2,)),
        ]
        state = [
            ((16, EZ), F32), (field, F32), (field, F32), (field, F32),
            ((3, EY, FD, EZ), F32), ((3, EX, FD, EZ), F32), ((3, FD, EZ), F32),
            ((CELLS, 384, EZ), F32), ((384, 192), BF16), ((8, EZ), jnp.int32),
        ]
        in_vmem = pl.BlockSpec(memory_space=pltpu.VMEM)
        kept = pl.pallas_call(
            functools.partial(kernel, sizes),
            out_shape=[jax.ShapeDtypeStruct(*entry) for entry in state],
            in_specs=[pl.BlockSpec(memory_space=pltpu.HBM)] * 9,
            out_specs=[in_vmem] * len(state),
            scratch_shapes=scratch,
            compiler_params=pltpu.CompilerParams(
                collective_id=0, has_side_effects=True, vmem_limit_bytes=32 * 1024 * 1024
            ),
            name="step",
        )(
            *(
                pltpu.with_memory_space_constraint(value, pltpu.HBM)
                for value in (
                    trace_old.reshape(768, EZ), face_load.reshape(768, EZ), face_diag.reshape(24, EZ),
                    fine_flag.reshape(8, EZ), coeff.reshape(8, EZ), fields.reshape(3072, EZ), volume_op, lift_op.T,
                    schur_op,
                )
            )
        )
        out_f, out_x = pl.pallas_call(
            finish,
            out_shape=(jax.ShapeDtypeStruct((3072, EZ), BF16), jax.ShapeDtypeStruct((768, EZ), F32)),
            in_specs=[in_vmem] * len(state),
            out_specs=(pl.BlockSpec(memory_space=pltpu.HBM),) * 2,
            scratch_shapes=[
                vmem((192, CELLS * EZ), BF16), vmem((3072, EZ), F32), vmem((3072, EZ), BF16), vmem((768, EZ), F32),
                vmem(field, F32), vmem((EY, FD, EZ), F32), vmem((EX, FD, EZ), F32), vmem((FD, EZ), F32),
                pltpu.SemaphoreType.DMA((1 + CHUNKS,)),
            ],
            compiler_params=pltpu.CompilerParams(vmem_limit_bytes=24 * 1024 * 1024),
            name="finish",
        )(*kept)
        return out_f.reshape(fields.shape), out_x.reshape(trace_old.shape)

    return jax.shard_map(
        body,
        mesh=mesh,
        in_specs=(
            P(None, "gx", "gy", "gz"),
            P(None, None, "gx", "gy", "gz"),
            P(None, None, "gx", "gy", "gz"),
            P(None, "gx", "gy", "gz"),
            P("gx", "gy", "gz"),
            P("gx", "gy", "gz"),
            P(),
            P(),
            P(),
        ),
        out_specs=(P(None, "gx", "gy", "gz"), P(None, None, "gx", "gy", "gz")),
        check_vma=False,
    )
```

```python
import functools

import jax
import jax.numpy as jnp
from jax import lax
from jax.experimental import pallas as pl
from jax.experimental.pallas import tpu as pltpu
from jax.sharding import PartitionSpec as P

MESH = pl.DeviceIdType.MESH
EX, EY, EZ = 2, 4, 128
CELLS = EX * EY
FD = 32
F32, BF16 = jnp.float32, jnp.bfloat16
TIME_STEP = 0.25
CHUNKS = 3


def dot(a, b):
    return jnp.dot(a, b, preferred_element_type=F32)


def fold(value):
    return jnp.sum(value.reshape(-1, 8, 128), axis=0)


def total(value):
    return jnp.sum(jnp.sum(value, axis=0, keepdims=True), axis=1, keepdims=True)


def across(sizes):
    steps = [(y, z) for y in range(sizes[0] // 2) for z in range(sizes[2]) if y or z]
    return sorted(steps, key=lambda s: -min(s[0], sizes[0] // 2 - s[0]) - min(s[1], sizes[2] - s[1]))


def along(sizes):
    steps = [(c, z) for z in range(sizes[1]) for c in range(2) if c or z]
    return sorted(steps, key=lambda s: -min(s[1], sizes[1] - s[1]) - 0.5 * s[0])


def unpack(packed, n, at):
    return pltpu.roll(packed, (at - n) % EZ, 1)


def squeeze(value):
    out = value[0:8, :]
    for n in range(1, 4):
        out = out + pltpu.roll(value[8 * n : 8 * n + 8, :], 16 * n, 1)
    return out


def spread(value):
    wide = jnp.concatenate([value] + [pltpu.roll(value, EZ - 16 * n, 1) for n in range(1, 4)], axis=0)
    return jnp.where(lax.broadcasted_iota(jnp.int32, wide.shape, 1) < 16, wide, 0.0)


def faces_of(v, hx, hy, hz, lane, i, j):
    n = i * EY + j
    z = v[i, j, 64:96, :]
    return [
        v[i, j, 0:32, :],
        v[i + 1, j, 0:32, :] if i + 1 < EX else hx[j],
        v[i, j, 32:64, :],
        v[i, j + 1, 32:64, :] if j + 1 < EY else hy[i],
        z,
        jnp.where(lane == EZ - 1, unpack(hz[...], n, EZ - 1), pltpu.roll(z, EZ - 1, 1)),
    ]


def kernel(sizes, *refs):
    (x_hbm, b_hbm, diag_hbm, fine_hbm, coeff_hbm, f_hbm, v_hbm, lt_hbm, s_hbm) = refs[:9]
    (moments, X, R0, W1, hx, hy, hz, BASE, LF, fi) = refs[9:19]
    (xn, bn, dg, co, fb, vb, ltb, sf, PR, P0, T, GH, GL, SX, FN,
     gx, gy, gz, ux, uy, uz, cx, cy, cz, cs, zs, own, ra, own_b, rb,
     wt, px, py, near_w, edge, pair_xy, corner, packed, CH, CL,
     load_sem, send_sem, recv_sem, gather_send, gather_recv, know) = refs[19:]
    names = ("gx", "gy", "gz")
    me = [lax.axis_index(n) for n in names]
    has_up = [m < n - 1 for m, n in zip(me, sizes)]
    has_down = [m > 0 for m in me]

    barrier = pltpu.get_barrier_semaphore()

    ring = [[m] + [lax.rem(m + k, n) for k in range(1, n)] for m, n in zip(me, sizes)]

    def at(*steps):
        return {
            names[axis]: ring[axis][step % sizes[axis]] for axis, step in enumerate(steps) if step
        }

    def announce(sem, steps):
        count = 0
        for each in steps:
            if any(step % n for step, n in zip(each, sizes)):
                pl.semaphore_signal(sem, inc=1, device_id=at(*each), device_id_type=MESH)
                count += 1
        return count

    near = [(1, 0, 0), (-1, 0, 0), (0, 1, 0), (0, -1, 0), (0, 0, 1), (0, 0, -1)]
    both = [(p, q) for p in (1, -1) for q in (1, -1)]
    diagonal = [(p, q, 0) for p, q in both] + [(p, 0, q) for p, q in both] + [(0, p, q) for p, q in both]
    loads = [
        pltpu.make_async_copy(src, dst, load_sem.at[k])
        for k, (src, dst) in enumerate(
            [(x_hbm.at[256 * a : 256 * a + 256, :], xn.at[256 * a : 256 * a + 256, :]) for a in range(3)]
            + [(fine_hbm, fi), (coeff_hbm, co), (s_hbm, sf), (diag_hbm, dg), (b_hbm, bn),
               (f_hbm, fb), (v_hbm, vb), (lt_hbm, ltb)]
        )
    ]
    for copy in loads[:3]:
        copy.start()
    partners = announce(barrier, near + diagonal)
    for copy in loads[3:8]:
        copy.start()
    core = lax.rem(me[0], 2)
    other_core = me[0] + 1 - 2 * core

    started = []

    def send(src, dst, *steps):
        k = len(started)
        copy = pltpu.make_async_remote_copy(
            src_ref=src, dst_ref=dst, send_sem=send_sem.at[k], recv_sem=recv_sem.at[k],
            device_id=at(*steps), device_id_type=MESH,
        )
        copy.start()
        started.append(copy)
        return copy

    lane = lax.broadcasted_iota(jnp.int32, (FD, EZ), 1)
    cells = [(i, j) for i in range(EX) for j in range(EY)]

    def keep(flag, value):
        return jnp.where(flag, value, 0.0)

    def pack(pieces, lane_of, first=0, out=None):
        out = jnp.zeros((FD, EZ), F32) if out is None else out
        for n, piece in enumerate(pieces, first):
            out = jnp.where(lane == n, pltpu.roll(piece, (n - lane_of) % EZ, 1), out)
        return out

    def faces(v, k, i, j):
        return faces_of(v, hx.at[k], hy.at[k], hz.at[k], lane, i, j)

    def convert(v, k, half, upper_only=False):
        for n, (i, j) in enumerate(cells):
            if i != half:
                continue
            fresh = (1,) * (i == EX - 1) + (3,) * (j == EY - 1) + (5,) if upper_only else range(6)
            for at, block in enumerate(faces(v, k, i, j)):
                if at not in fresh:
                    continue
                high = block.astype(BF16)
                low = (block - high.astype(F32)).astype(BF16)
                GH[32 * at : 32 * at + 32, EZ * n : EZ * n + EZ] = high
                GL[32 * at : 32 * at + 32, EZ * n : EZ * n + EZ] = low
    def multiply(half):
        for n in range(EY * half, EY * half + EY, 2):
            cols = slice(EZ * n, EZ * n + 2 * EZ)
            both = dot(SX[...], GH[:, cols])
            product = both[0:192, :] + (dot(SX[0:192, :], GL[:, cols]) + both[192:384, :])
            for m in range(2):
                T[n + m] = product[:, EZ * m : EZ * m + EZ] * weight(n + m)

    def apply(v, k, half):
        convert(v, k, half)
        multiply(half)

    def weight(n):
        return wt[n : n + 1, :]

    def gathered(i, j, a):
        n = i * EY + j
        at = 64 * a
        value = T[n, at : at + 32, :]
        if a == 0 and i > 0:
            value = value + T[n - EY, at + 32 : at + 64, :]
        if a == 1 and j > 0:
            value = value + T[n - 1, at + 32 : at + 64, :]
        if a == 2:
            value = value + jnp.where(lane == 0, 0.0, pltpu.roll(T[n, at + 32 : at + 64, :], 1, 1))
        return value

    def upper(i_or_j, axis):
        if axis == 0:
            return T[(EX - 1) * EY + i_or_j, 32:64, :]
        return T[i_or_j * EY + EY - 1, 96:128, :]

    def upper_z():
        return pack([T[n, 160:192, :] for n in range(CELLS)], EZ - 1)

    def diag(a, n):
        return dg[a * CELLS + n : a * CELLS + n + 1, :]

    def round_trip(v, p, k, partial):
        out = []
        done = set()

        def put(i, j, a):
            p[i, j, 32 * a : 32 * a + 32, :] = partial(i, j, a)
            done.add((i, j, a))

        apply(v, k - 1, 0)
        for j in range(EY):
            put(0, j, 0)
        out.append(send(p.at[0, :, 0:32, :], gx.at[k], -1, 0, 0))
        apply(v, k - 1, 1)
        for j in range(EY):
            cx[k - 1, j] = upper(j, 0)
        out.append(send(cx.at[k - 1], ux.at[k - 1], 1, 0, 0))
        for i in range(EX):
            put(i, 0, 1)
        out.append(send(p.at[:, 0, 32:64, :], gy.at[k], 0, -1, 0))
        for i in range(EX):
            cy[k - 1, i] = upper(i, 1)
        out.append(send(cy.at[k - 1], uy.at[k - 1], 0, 1, 0))
        for i, j in cells:
            put(i, j, 2)
        zs[k] = squeeze(pack([p[i, j, 64:96, :] for i, j in cells], 0))
        out.append(send(zs.at[k], gz.at[k], 0, 0, -1))
        cz[...] = upper_z()
        cs[k - 1] = squeeze(cz[...])
        out.append(send(cs.at[k - 1], uz.at[k - 1], 0, 0, 1))
        for i, j in cells:
            for a in range(3):
                if (i, j, a) not in done:
                    put(i, j, a)
        return out

    def ghosts(k, own_x, own_y, own_z):
        for j in range(EY):
            hx[k, j] = keep(has_up[0], gx[k, j] + own_x(j))
        for i in range(EX):
            hy[k, i] = keep(has_up[1], gy[k, i] + own_y(i))
        hz[k] = keep(has_up[2], spread(gz[k]) + own_z())

    def complete(p, out, k, sign):
        from_z = spread(uz[k - 1])
        for n, (i, j) in enumerate(cells):
            along_x, along_y, along_z = p[i, j, 0:32, :], p[i, j, 32:64, :], p[i, j, 64:96, :]
            if i == 0:
                along_x = along_x + sign * keep(has_down[0], ux[k - 1, j])
            if j == 0:
                along_y = along_y + sign * keep(has_down[1], uy[k - 1, i])
            below = jnp.where(lane == 0, unpack(from_z, n, 0), 0.0)
            along_z = along_z + sign * keep(has_down[2], below)
            out[i, j, 0:32, :] = along_x
            out[i, j, 32:64, :] = along_y
            out[i, j, 64:96, :] = along_z

    for a in range(3):
        loads[a].wait()
        for n, (i, j) in enumerate(cells):
            X[i, j, 32 * a : 32 * a + 32, :] = xn[pl.ds(256 * a + n, FD, stride=CELLS), :]
    low_x = [X[0, j, 0:32, :] for j in range(EY)]
    low_y = [X[i, 0, 32:64, :] for i in range(EX)]
    low_z = [X[i, j, 64:96, :] for i, j in cells]
    low = pack(low_y, 0, 12, pack(low_x, 0, 8, pack(low_z, 0)))
    zs[0] = squeeze(low)
    edge[...] = squeeze(pack(low_y, EZ - 1, 12, pack(low_x, EZ - 1, 8)))
    pl.semaphore_wait(barrier, partners)
    copies = [
        send(X.at[0, :, 0:32, :], gx.at[0], -1, 0, 0),
        send(X.at[0, 0, 0:64, :], pair_xy, -1, -1, 0),
        send(X.at[1, 0, 32:64, :], corner.at[0], 1, -1, 0),
        send(X.at[0, EY - 1, 0:32, :], corner.at[1], -1, 1, 0),
        send(zs.at[0], packed.at[0], -1, 0, -1),
        send(zs.at[0], packed.at[1], 1, 0, -1),
        send(edge, packed.at[2], -1, 0, 1),
        send(zs.at[0], packed.at[3], 0, -1, -1),
        send(zs.at[0], packed.at[4], 0, 1, -1),
        send(edge, packed.at[5], 0, -1, 1),
        send(X.at[:, 0, 32:64, :], gy.at[0], 0, -1, 0),
        send(zs.at[0], gz.at[0], 0, 0, -1),
    ]
    for copy in loads[8:]:
        copy.start()
    for copy in loads[3:8]:
        copy.wait()
    wt[...] = fi[...].astype(F32) * co[...]
    s = sf[...]
    high = s.astype(BF16)
    SX[0:192, :] = high
    SX[192:384, :] = (s - high.astype(F32)).astype(BF16)
    hx[0] = jnp.zeros((EY, FD, EZ), F32)
    hy[0] = jnp.zeros((EX, FD, EZ), F32)
    hz[0] = jnp.zeros((FD, EZ), F32)

    def residual(i, j, a):
        n = i * EY + j
        load = bn[pl.ds(a * FD * CELLS + n, FD, stride=CELLS), :]
        return load - diag(a, n) * X[i, j, 32 * a : 32 * a + 32, :] - gathered(i, j, a)

    apply(X, 0, 0)
    for j in range(EY):
        px[j] = residual(0, j, 0)
    copies.append(send(px, gx.at[1], -1, 0, 0))
    apply(X, 0, 1)
    for j in range(EY):
        cx[0, j] = upper(j, 0)
    copies.append(send(cx.at[0], ux.at[0], 1, 0, 0))
    for i in range(EX):
        py[i] = residual(i, 0, 1)
        cy[0, i] = upper(i, 1)
    copies.append(send(py, gy.at[1], 0, -1, 0))
    copies.append(send(cy.at[0], uy.at[0], 0, 1, 0))
    zs[1] = squeeze(pack([residual(i, j, 2) for i, j in cells], 0))
    cs[0] = squeeze(upper_z())
    copies.append(send(zs.at[1], gz.at[1], 0, 0, -1))
    copies.append(send(cs.at[0], uz.at[0], 0, 0, 1))
    for n, step in enumerate(near):
        copies.append(send(wt, near_w.at[n], *step))
    known_1 = announce(know.at[0], near)

    def put(block, first, value):
        cols = slice(first, first + value.shape[1])
        high = value.astype(BF16)
        CH[32 * block : 32 * block + 32, cols] = high
        CL[32 * block : 32 * block + 32, cols] = (value - high.astype(F32)).astype(BF16)

    CH[...] = jnp.zeros(CH.shape, BF16)
    CL[...] = jnp.zeros(CL.shape, BF16)
    for j in range(EY):
        put(1, EZ * j, low_x[j])
    for i in range(EX):
        put(3, 1024 + EZ * i, low_y[i])
    put(5, 1536, low)

    def volume(n):
        pair = [FN[pl.ds(n + m, 384, stride=CELLS), :] for m in range(2)]
        moved = dot(vb[...], jnp.concatenate([p.astype(BF16) for p in pair], axis=1))
        for m in range(2):
            coarse = 1.0 - fi[n + m : n + m + 1, :].astype(F32)
            BASE[n + m] = pair[m] + TIME_STEP * (coarse * moved[:, EZ * m : EZ * m + EZ])

    loads[8].wait()
    for n in range(0, 3072, 128):
        FN[n : n + 128, :] = fb[n : n + 128, :].astype(F32)
    loads[9].wait()
    volume(0)
    volume(2)
    for copy in copies[:12]:
        copy.wait_recv()
    ghosts(0, lambda j: 0.0, lambda i: 0.0, lambda: 0.0)

    def last(packed, n):
        return jnp.where(lane == EZ - 1, unpack(packed, n, EZ - 1), 0.0)

    def moved(packed, n, to):
        return jnp.where(lane == to, unpack(packed, n, to), 0.0)

    def over(axis, value):
        return keep(has_up[axis], value)

    apart = [spread(packed[n]) for n in range(6)]
    put(3, 384, over(1, corner[0]))
    put(3, 896, over(1, pair_xy[32:64, :]))
    put(1, 1152, over(0, corner[1]))
    put(1, 1408, over(0, pair_xy[0:32, :]))
    for j in range(EY):
        put(5, EZ * j, over(2, last(apart[1], EY + j)))
        put(5, 512 + EZ * j, over(2, last(apart[0], j)))
    for i in range(EX):
        put(5, 1024 + EZ * i, over(2, last(apart[4], i * EY + EY - 1)))
        put(5, 1280 + EZ * i, over(2, last(apart[3], i * EY)))
    second = jnp.logical_and(lane >= EY, lane < 2 * EY)
    put(1, 1536, over(0, jnp.where(second, pltpu.roll(apart[2], EZ - 4, 1), 0.0)))
    put(1, 1664, over(0, jnp.where(second, pltpu.roll(apart[0], EZ - 4, 1), 0.0)))
    put(3, 1536, over(1, moved(apart[5], 12, EY - 1) + moved(apart[5], 13, 2 * EY - 1)))
    put(3, 1664, over(1, moved(apart[3], 12, EY - 1) + moved(apart[3], 13, 2 * EY - 1)))

    def correction(pair, first, size):
        rows, lower = slice(64 * pair, 64 * pair + 64), slice(192 + 64 * pair, 256 + 64 * pair)
        cols = slice(first, first + 2 * size)
        both = dot(jnp.concatenate([SX[rows, :], SX[lower, :]], axis=0), CH[:, cols])
        out = both[0:64, :] + (dot(SX[rows, :], CL[:, cols]) + both[64:128, :])
        return out[32:64, 0:size], out[0:32, size : 2 * size]

    def ends(n, at):
        out = jnp.zeros((1, EZ), F32)
        for c in range(CELLS):
            out = jnp.where(lane[0:1] == c, jnp.broadcast_to(near_w[n, c : c + 1, at : at + 1], (1, EZ)), out)
        return out

    def cut(value, n):
        return value[:, EZ * n : EZ * n + EZ]

    xl, xh = correction(0, 0, 512)
    yl, yh = correction(1, 1024, 256)
    zl, zh = correction(2, 1536, 128)
    convert(X, 0, 0, True)
    convert(X, 0, 1, True)
    multiply(0)
    multiply(1)
    for i, j in cells:
        for a in range(3):
            PR[i, j, 32 * a : 32 * a + 32, :] = residual(i, j, a)
    for copy in copies[12:]:
        copy.wait_recv()
    pl.semaphore_wait(know.at[0], known_1)

    xl = [cut(xl, j) * near_w[0, EY + j : EY + j + 1, :] for j in range(EY)]
    xh = [cut(xh, j) * near_w[1, j : j + 1, :] for j in range(EY)]
    yl = [cut(yl, i) * near_w[2, i * EY + EY - 1 : i * EY + EY, :] for i in range(EX)]
    yh = [cut(yh, i) * near_w[3, i * EY : i * EY + 1, :] for i in range(EX)]
    zl = zl * ends(4, EZ - 1)
    zh = zh * ends(5, 0)

    from_z = spread(uz[0]) + zl
    for n, (i, j) in enumerate(cells):
        along_x, along_y, along_z = PR[i, j, 0:32, :], PR[i, j, 32:64, :], PR[i, j, 64:96, :]
        if i == 0:
            along_x = along_x - keep(has_down[0], ux[0, j] + xl[j])
        if j == 0:
            along_y = along_y - keep(has_down[1], uy[0, i] + yl[i])
        below = jnp.where(lane == 0, unpack(from_z, n, 0), 0.0)
        R0[i, j, 0:32, :] = along_x
        R0[i, j, 32:64, :] = along_y
        R0[i, j, 64:96, :] = along_z - keep(has_down[2], below)
    ghosts(1, lambda j: -xh[j] - upper(j, 0), lambda i: -yh[i] - upper(i, 1), lambda: -zh - upper_z())

    def image(i, j, a):
        return diag(a, i * EY + j) * R0[i, j, 32 * a : 32 * a + 32, :] + gathered(i, j, a)

    early = list(started)
    copies = round_trip(R0, P0, 2, image)
    known_2 = announce(know.at[1], [(2, 0, 0), (-2, 0, 0), (0, 2, 0), (0, -2, 0), (2, 0, 1), (-2, 0, -1)])
    for copy in early:
        copy.wait_send()
    zero = jnp.zeros((8, EZ), F32)

    def over_ghosts(value):
        out = zero
        for j in range(EY):
            out = out + fold(value(hx[1, j], hx[2, j], cx[1, j], upper(j, 0)))
        for i in range(EX):
            out = out + fold(value(hy[1, i], hy[2, i], cy[1, i], upper(i, 1)))
        return out

    sum_a, sum_e00 = zero, zero
    for i, j in cells:
        r = R0[i, j]
        sum_a = sum_a + fold(r * r)
        sum_e00 = sum_e00 + fold(r * P0[i, j])
    sum_e00 = sum_e00 + over_ghosts(lambda r, w, c0, c1: r * c0) + fold(hz[1] * cz[...])
    a = total(sum_a)
    e00 = total(sum_e00)
    shift = jnp.where(a > 0.0, e00 / jnp.where(a > 0.0, a, 1.0), 0.0)
    volume(4)
    volume(6)
    loads[10].wait()
    LF[...] = ltb[...].astype(F32).T.astype(BF16)
    for copy in copies:
        copy.wait_recv()
    if known_2:
        pl.semaphore_wait(know.at[1], known_2)
    ghosts(2, lambda j: cx[1, j], lambda i: cy[1, i], lambda: cz[...])
    complete(P0, W1, 2, 1.0)

    apply(W1, 2, 0)
    apply(W1, 2, 1)
    sum_b, sum_c, sum_e01, sum_e11 = zero, zero, zero, zero
    for n, (i, j) in enumerate(cells):
        for k in range(3):
            at = slice(32 * k, 32 * k + 32)
            r, w, p = R0[i, j, at, :], W1[i, j, at, :], P0[i, j, at, :]
            q = w - shift * r
            sum_b = sum_b + fold(r * q)
            sum_c = sum_c + fold(q * q)
            sum_e01 = sum_e01 + fold(q * p)
            sum_e11 = sum_e11 + fold(q * (diag(k, n) * w + gathered(i, j, k) - shift * p))
    top = upper_z()
    q = hz[2] - shift * hz[1]
    sum_e01 = sum_e01 + fold(q * cz[...]) + over_ghosts(lambda r, w, c0, c1: (w - shift * r) * c0)
    sum_e11 = sum_e11 + fold(q * (top - shift * cz[...]))
    sum_e11 = sum_e11 + over_ghosts(lambda r, w, c0, c1: (w - shift * r) * (c1 - shift * c0))
    row = lax.broadcasted_iota(jnp.int32, (8, EZ), 0)
    column = lax.broadcasted_iota(jnp.int32, (1, EZ), 1)
    tile = zero
    for n, value in [(2, sum_b), (3, sum_c), (5, sum_e01), (6, sum_e11)]:
        tile = jnp.where(row == n, jnp.sum(value, axis=0, keepdims=True), tile)
    tile = jnp.broadcast_to(jnp.sum(tile, axis=1, keepdims=True), (8, EZ))
    for n, value in [(0, shift), (1, a), (4, e00)]:
        tile = jnp.where(row == n, value, tile)
    place = lax.div(me[0], 2) + sizes[0] // 2 * me[2]
    mine = lax.broadcasted_iota(jnp.int32, (8, EZ), 1) == 16 * row + place
    own[...] = jnp.sum(jnp.where(mine, tile, 0.0), axis=0, keepdims=True)

    def gather(k, source, landing, targets, sent):
        for n, target in enumerate(targets):
            pltpu.make_async_remote_copy(
                src_ref=source, dst_ref=landing.at[n], send_sem=gather_send.at[k], recv_sem=gather_recv.at[k],
                device_id=target, device_id_type=MESH,
            ).start()
        sent()
        pltpu.make_async_copy(landing, landing, gather_recv.at[k]).wait()

    gather(0, own, ra, [
        {"gx": ring[0][2 * y], "gz": ring[2][z]} for y, z in across(sizes)
    ], lambda: [copy.wait_send() for copy in copies])
    total_row = own[...]
    for n in range(ra.shape[0]):
        total_row = total_row + ra[n]
    own_b[...] = total_row
    gather(1, own_b, rb, [
        {"gx": other_core if c else me[0], "gy": ring[1][z]} for c, z in along(sizes)
    ], lambda: pltpu.make_async_copy(ra, ra, gather_send.at[0]).wait())
    rows = lax.broadcasted_iota(jnp.int32, (16, EZ), 0)
    tile = jnp.where(rows == 0, total_row, 0.0)
    for n in range(rb.shape[0]):
        tile = jnp.where(rows == n + 1, rb[n], tile)
    moments[...] = tile
    pltpu.make_async_copy(rb, rb, gather_send.at[1]).wait()


def finish(*refs):
    (moments, X, R0, W1, hx, hy, hz, BASE, LF, fi, fo_hbm, xo_hbm, GH, ON, FO, XO, new_v, new_x, new_y, new_z, out_sem) = refs
    cells = [(i, j) for i in range(EX) for j in range(EY)]
    lane = lax.broadcasted_iota(jnp.int32, (FD, EZ), 1)
    tile = moments[...]

    held = lax.broadcasted_iota(jnp.int32, (16, EZ), 1) < 16

    def number(n):
        return jnp.where(held, pltpu.roll(tile, EZ - 16 * n, 1) if n else tile, 0.0)

    shift, a, b, c, e00, e01, e11 = [number(n) for n in range(7)]

    def summed(value):
        return jnp.sum(jnp.sum(value, axis=0, keepdims=True), axis=1, keepdims=True)

    norm0, energy0 = summed(a), summed(e00)
    alpha0 = norm0 / energy0
    f = 1.0 - alpha0 * shift
    norm1 = summed(f * f * a - 2.0 * alpha0 * f * b + alpha0 * alpha0 * c)
    energy1 = summed(f * f * e00 - 2.0 * alpha0 * f * e01 + alpha0 * alpha0 * e11)
    mixed = summed(f * e00 - alpha0 * e01)
    beta = norm1 / norm0
    alpha1 = norm1 / (energy1 + 2.0 * beta * mixed + beta * beta * energy0)
    on_r = alpha0 + alpha1 * (1.0 + beta)
    on_w = -alpha1 * alpha0

    for n, (i, j) in enumerate(cells):
        new = X[i, j] + on_r * R0[i, j] + on_w * W1[i, j]
        new_v[i, j] = new
        XO[pl.ds(n, 96, stride=CELLS), :] = new
    copies = [pltpu.make_async_copy(XO, xo_hbm, out_sem.at[0])]
    copies[0].start()
    for j in range(EY):
        new_x[j] = hx[0, j] + on_r * hx[1, j] + on_w * hx[2, j]
    for i in range(EX):
        new_y[i] = hy[0, i] + on_r * hy[1, i] + on_w * hy[2, i]
    new_z[...] = hz[0] + on_r * hz[1] + on_w * hz[2]
    for n, (i, j) in enumerate(cells):
        fine = fi[n : n + 1, :] > 0
        new_faces = faces_of(new_v, new_x, new_y, new_z, lane, i, j)
        old_faces = faces_of(X, hx.at[0], hy.at[0], hz.at[0], lane, i, j)
        for at, (new, old) in enumerate(zip(new_faces, old_faces)):
            GH[32 * at : 32 * at + 32, EZ * n : EZ * n + EZ] = jnp.where(fine, new, old).astype(BF16)
    rows = 384 // CHUNKS
    for chunk in range(CHUNKS):
        at = slice(rows * chunk, rows * chunk + rows)
        for n in range(0, CELLS, 2):
            lifted = dot(LF[at, :], GH[:, EZ * n : EZ * n + 2 * EZ])
            for m in range(2):
                ON[pl.ds(rows * CELLS * chunk + n + m, rows, stride=CELLS), :] = (
                    BASE[n + m, at, :] + TIME_STEP * lifted[:, EZ * m : EZ * m + EZ]
                )
        for n in range(rows * CELLS * chunk, rows * CELLS * (chunk + 1), 128):
            FO[n : n + 128, :] = ON[n : n + 128, :].astype(BF16)
        where = slice(rows * CELLS * chunk, rows * CELLS * (chunk + 1))
        copy = pltpu.make_async_copy(FO.at[where, :], fo_hbm.at[where, :], out_sem.at[1 + chunk])
        copy.start()
        copies.append(copy)
    for copy in copies:
        copy.wait()


def solution(mesh):
    sizes = tuple(mesh.shape[n] for n in ("gx", "gy", "gz"))

    def body(fields, trace_old, face_load, face_diag, fine_flag, coeff, volume_op, lift_op, schur_op):
        vmem = pltpu.VMEM
        field = (EX, EY, 96, EZ)
        copies = 12 + 6 + 6 + 6
        group, column = len(across(sizes)), len(along(sizes))
        scratch = [
            vmem((768, EZ), F32), vmem((768, EZ), F32), vmem((24, EZ), F32),
            vmem((8, EZ), F32), vmem((3072, EZ), BF16), vmem((384, 384), BF16), vmem((192, 384), BF16),
            vmem((192, 192), F32),
            vmem(field, F32), vmem(field, F32),
            vmem((CELLS, 192, EZ), F32), vmem((192, CELLS * EZ), BF16), vmem((192, CELLS * EZ), BF16),
            vmem((384, 192), BF16),
            vmem((3072, EZ), F32),
            vmem((3, EY, FD, EZ), F32), vmem((3, EX, FD, EZ), F32), vmem((3, 8, EZ), F32),
            vmem((2, EY, FD, EZ), F32), vmem((2, EX, FD, EZ), F32), vmem((2, 8, EZ), F32),
            vmem((2, EY, FD, EZ), F32), vmem((2, EX, FD, EZ), F32), vmem((FD, EZ), F32), vmem((2, 8, EZ), F32),
            vmem((3, 8, EZ), F32),
            vmem((1, EZ), F32), vmem((group, 1, EZ), F32), vmem((1, EZ), F32), vmem((column, 1, EZ), F32),
            vmem((8, EZ), F32), vmem((EY, FD, EZ), F32), vmem((EX, FD, EZ), F32), vmem((6, 8, EZ), F32), vmem((8, EZ), F32), vmem((64, EZ), F32), vmem((2, FD, EZ), F32),
            vmem((6, 8, EZ), F32),
            vmem((192, 1792), BF16), vmem((192, 1792), BF16),
            pltpu.SemaphoreType.DMA((11,)),
            pltpu.SemaphoreType.DMA((copies,)), pltpu.SemaphoreType.DMA((copies,)),
            pltpu.SemaphoreType.DMA((2,)), pltpu.SemaphoreType.DMA((2,)), pltpu.SemaphoreType.REGULAR((2,)),
        ]
        state = [
            ((16, EZ), F32), (field, F32), (field, F32), (field, F32),
            ((3, EY, FD, EZ), F32), ((3, EX, FD, EZ), F32), ((3, FD, EZ), F32),
            ((CELLS, 384, EZ), F32), ((384, 192), BF16), ((8, EZ), jnp.int32),
        ]
        in_vmem = pl.BlockSpec(memory_space=pltpu.VMEM)
        kept = pl.pallas_call(
            functools.partial(kernel, sizes),
            out_shape=[jax.ShapeDtypeStruct(*entry) for entry in state],
            in_specs=[pl.BlockSpec(memory_space=pltpu.HBM)] * 9,
            out_specs=[in_vmem] * len(state),
            scratch_shapes=scratch,
            compiler_params=pltpu.CompilerParams(
                collective_id=0, has_side_effects=True, vmem_limit_bytes=32 * 1024 * 1024
            ),
            name="step",
        )(
            *(
                pltpu.with_memory_space_constraint(value, pltpu.HBM)
                for value in (
                    trace_old.reshape(768, EZ), face_load.reshape(768, EZ), face_diag.reshape(24, EZ),
                    fine_flag.reshape(8, EZ), coeff.reshape(8, EZ), fields.reshape(3072, EZ), volume_op, lift_op.T,
                    schur_op,
                )
            )
        )
        out_f, out_x = pl.pallas_call(
            finish,
            out_shape=(jax.ShapeDtypeStruct((3072, EZ), BF16), jax.ShapeDtypeStruct((768, EZ), F32)),
            in_specs=[in_vmem] * len(state),
            out_specs=(pl.BlockSpec(memory_space=pltpu.HBM),) * 2,
            scratch_shapes=[
                vmem((192, CELLS * EZ), BF16), vmem((3072, EZ), F32), vmem((3072, EZ), BF16), vmem((768, EZ), F32),
                vmem(field, F32), vmem((EY, FD, EZ), F32), vmem((EX, FD, EZ), F32), vmem((FD, EZ), F32),
                pltpu.SemaphoreType.DMA((1 + CHUNKS,)),
            ],
            compiler_params=pltpu.CompilerParams(vmem_limit_bytes=24 * 1024 * 1024),
            name="finish",
        )(*kept)
        return out_f.reshape(fields.shape), out_x.reshape(trace_old.shape)

    return jax.shard_map(
        body,
        mesh=mesh,
        in_specs=(
            P(None, "gx", "gy", "gz"),
            P(None, None, "gx", "gy", "gz"),
            P(None, None, "gx", "gy", "gz"),
            P(None, "gx", "gy", "gz"),
            P("gx", "gy", "gz"),
            P("gx", "gy", "gz"),
            P(),
            P(),
            P(),
        ),
        out_specs=(P(None, "gx", "gy", "gz"), P(None, None, "gx", "gy", "gz")),
        check_vma=False,
    )
```

```python
import functools

import jax
import jax.numpy as jnp
from jax import lax
from jax.experimental import pallas as pl
from jax.experimental.pallas import tpu as pltpu
from jax.sharding import PartitionSpec as P

MESH = pl.DeviceIdType.MESH
EX, EY, EZ = 2, 4, 128
CELLS = EX * EY
FD = 32
F32, BF16 = jnp.float32, jnp.bfloat16
TIME_STEP = 0.25
CHUNKS = 3


def dot(a, b):
    return jnp.dot(a, b, preferred_element_type=F32)


def fold(value):
    return jnp.sum(value.reshape(-1, 8, 128), axis=0)


def total(value):
    return jnp.sum(jnp.sum(value, axis=0, keepdims=True), axis=1, keepdims=True)


def across(sizes):
    steps = [(y, z) for y in range(sizes[0] // 2) for z in range(sizes[2]) if y or z]
    return sorted(steps, key=lambda s: -min(s[0], sizes[0] // 2 - s[0]) - min(s[1], sizes[2] - s[1]))


def along(sizes):
    steps = [(c, z) for z in range(sizes[1]) for c in range(2) if c or z]
    return sorted(steps, key=lambda s: -min(s[1], sizes[1] - s[1]) - 0.5 * s[0])


def unpack(packed, n, at):
    return pltpu.roll(packed, (at - n) % EZ, 1)


def squeeze(value):
    out = value[0:8, :]
    for n in range(1, 4):
        out = out + pltpu.roll(value[8 * n : 8 * n + 8, :], 16 * n, 1)
    return out


def spread(value):
    wide = jnp.concatenate([value] + [pltpu.roll(value, EZ - 16 * n, 1) for n in range(1, 4)], axis=0)
    return jnp.where(lax.broadcasted_iota(jnp.int32, wide.shape, 1) < 16, wide, 0.0)


def faces_of(v, hx, hy, hz, lane, i, j):
    n = i * EY + j
    z = v[i, j, 64:96, :]
    return [
        v[i, j, 0:32, :],
        v[i + 1, j, 0:32, :] if i + 1 < EX else hx[j],
        v[i, j, 32:64, :],
        v[i, j + 1, 32:64, :] if j + 1 < EY else hy[i],
        z,
        jnp.where(lane == EZ - 1, unpack(hz[...], n, EZ - 1), pltpu.roll(z, EZ - 1, 1)),
    ]


def kernel(sizes, *refs):
    (x_hbm, b_hbm, diag_hbm, fine_hbm, coeff_hbm, f_hbm, v_hbm, lt_hbm, s_hbm) = refs[:9]
    (moments, X, R0, W1, hx, hy, hz, BASE, LF, fi) = refs[9:19]
    (xn, bn, dg, co, fb, vb, ltb, sf, PR, P0, T, GH, GL, SX, FN,
     gx, gy, gz, ux, uy, uz, cx, cy, cz, cs, zs, own, ra, own_b, rb,
     wt, px, py, near_w, edge, pair_xy, corner, packed, CH, CL,
     load_sem, send_sem, recv_sem, gather_send, gather_recv, know) = refs[19:]
    names = ("gx", "gy", "gz")
    me = [lax.axis_index(n) for n in names]
    has_up = [m < n - 1 for m, n in zip(me, sizes)]
    has_down = [m > 0 for m in me]

    barrier = pltpu.get_barrier_semaphore()

    ring = [[m] + [lax.rem(m + k, n) for k in range(1, n)] for m, n in zip(me, sizes)]

    def at(*steps):
        return {
            names[axis]: ring[axis][step % sizes[axis]] for axis, step in enumerate(steps) if step
        }

    def announce(sem, steps):
        count = 0
        for each in steps:
            if any(step % n for step, n in zip(each, sizes)):
                pl.semaphore_signal(sem, inc=1, device_id=at(*each), device_id_type=MESH)
                count += 1
        return count

    near = [(1, 0, 0), (-1, 0, 0), (0, 1, 0), (0, -1, 0), (0, 0, 1), (0, 0, -1)]
    both = [(p, q) for p in (1, -1) for q in (1, -1)]
    diagonal = [(p, q, 0) for p, q in both] + [(p, 0, q) for p, q in both] + [(0, p, q) for p, q in both]
    loads = [
        pltpu.make_async_copy(src, dst, load_sem.at[k])
        for k, (src, dst) in enumerate(
            [(x_hbm.at[256 * a : 256 * a + 256, :], xn.at[256 * a : 256 * a + 256, :]) for a in range(3)]
            + [(fine_hbm, fi), (coeff_hbm, co), (s_hbm, sf), (diag_hbm, dg), (b_hbm, bn),
               (f_hbm, fb), (v_hbm, vb), (lt_hbm, ltb)]
        )
    ]
    for copy in loads[:3]:
        copy.start()
    partners = announce(barrier, near + diagonal)
    for copy in loads[3:8]:
        copy.start()
    core = lax.rem(me[0], 2)
    other_core = me[0] + 1 - 2 * core

    started = []

    def send(src, dst, *steps):
        k = len(started)
        copy = pltpu.make_async_remote_copy(
            src_ref=src, dst_ref=dst, send_sem=send_sem.at[k], recv_sem=recv_sem.at[k],
            device_id=at(*steps), device_id_type=MESH,
        )
        copy.start()
        started.append(copy)
        return copy

    lane = lax.broadcasted_iota(jnp.int32, (FD, EZ), 1)
    cells = [(i, j) for i in range(EX) for j in range(EY)]

    def keep(flag, value):
        return jnp.where(flag, value, 0.0)

    def pack(pieces, lane_of, first=0, out=None):
        out = jnp.zeros((FD, EZ), F32) if out is None else out
        for n, piece in enumerate(pieces, first):
            out = jnp.where(lane == n, pltpu.roll(piece, (n - lane_of) % EZ, 1), out)
        return out

    def faces(v, k, i, j):
        return faces_of(v, hx.at[k], hy.at[k], hz.at[k], lane, i, j)

    def convert(v, k, half, upper_only=False):
        for n, (i, j) in enumerate(cells):
            if i != half:
                continue
            fresh = (1,) * (i == EX - 1) + (3,) * (j == EY - 1) + (5,) if upper_only else range(6)
            for at, block in enumerate(faces(v, k, i, j)):
                if at not in fresh:
                    continue
                high = block.astype(BF16)
                low = (block - high.astype(F32)).astype(BF16)
                GH[32 * at : 32 * at + 32, EZ * n : EZ * n + EZ] = high
                GL[32 * at : 32 * at + 32, EZ * n : EZ * n + EZ] = low
    def multiply(half):
        for n in range(EY * half, EY * half + EY, 2):
            cols = slice(EZ * n, EZ * n + 2 * EZ)
            both = dot(SX[...], GH[:, cols])
            product = both[0:192, :] + (dot(SX[0:192, :], GL[:, cols]) + both[192:384, :])
            for m in range(2):
                T[n + m] = product[:, EZ * m : EZ * m + EZ] * weight(n + m)

    def apply(v, k, half):
        convert(v, k, half)
        multiply(half)

    def weight(n):
        return wt[n : n + 1, :]

    def gathered(i, j, a):
        n = i * EY + j
        at = 64 * a
        value = T[n, at : at + 32, :]
        if a == 0 and i > 0:
            value = value + T[n - EY, at + 32 : at + 64, :]
        if a == 1 and j > 0:
            value = value + T[n - 1, at + 32 : at + 64, :]
        if a == 2:
            value = value + jnp.where(lane == 0, 0.0, pltpu.roll(T[n, at + 32 : at + 64, :], 1, 1))
        return value

    def upper(i_or_j, axis):
        if axis == 0:
            return T[(EX - 1) * EY + i_or_j, 32:64, :]
        return T[i_or_j * EY + EY - 1, 96:128, :]

    def upper_z():
        return pack([T[n, 160:192, :] for n in range(CELLS)], EZ - 1)

    def diag(a, n):
        return dg[a * CELLS + n : a * CELLS + n + 1, :]

    def round_trip(v, p, k, partial):
        out = []
        done = set()

        def put(i, j, a):
            p[i, j, 32 * a : 32 * a + 32, :] = partial(i, j, a)
            done.add((i, j, a))

        apply(v, k - 1, 0)
        for j in range(EY):
            put(0, j, 0)
        out.append(send(p.at[0, :, 0:32, :], gx.at[k], -1, 0, 0))
        apply(v, k - 1, 1)
        for j in range(EY):
            cx[k - 1, j] = upper(j, 0)
        out.append(send(cx.at[k - 1], ux.at[k - 1], 1, 0, 0))
        for i in range(EX):
            put(i, 0, 1)
        out.append(send(p.at[:, 0, 32:64, :], gy.at[k], 0, -1, 0))
        for i in range(EX):
            cy[k - 1, i] = upper(i, 1)
        out.append(send(cy.at[k - 1], uy.at[k - 1], 0, 1, 0))
        for i, j in cells:
            put(i, j, 2)
        zs[k] = squeeze(pack([p[i, j, 64:96, :] for i, j in cells], 0))
        out.append(send(zs.at[k], gz.at[k], 0, 0, -1))
        cz[...] = upper_z()
        cs[k - 1] = squeeze(cz[...])
        out.append(send(cs.at[k - 1], uz.at[k - 1], 0, 0, 1))
        for i, j in cells:
            for a in range(3):
                if (i, j, a) not in done:
                    put(i, j, a)
        return out

    def ghosts(k, own_x, own_y, own_z):
        for j in range(EY):
            hx[k, j] = keep(has_up[0], gx[k, j] + own_x(j))
        for i in range(EX):
            hy[k, i] = keep(has_up[1], gy[k, i] + own_y(i))
        hz[k] = keep(has_up[2], spread(gz[k]) + own_z())

    def complete(p, out, k, sign):
        from_z = spread(uz[k - 1])
        for n, (i, j) in enumerate(cells):
            along_x, along_y, along_z = p[i, j, 0:32, :], p[i, j, 32:64, :], p[i, j, 64:96, :]
            if i == 0:
                along_x = along_x + sign * keep(has_down[0], ux[k - 1, j])
            if j == 0:
                along_y = along_y + sign * keep(has_down[1], uy[k - 1, i])
            below = jnp.where(lane == 0, unpack(from_z, n, 0), 0.0)
            along_z = along_z + sign * keep(has_down[2], below)
            out[i, j, 0:32, :] = along_x
            out[i, j, 32:64, :] = along_y
            out[i, j, 64:96, :] = along_z

    for a in range(3):
        loads[a].wait()
        for n, (i, j) in enumerate(cells):
            X[i, j, 32 * a : 32 * a + 32, :] = xn[pl.ds(256 * a + n, FD, stride=CELLS), :]
    low_x = [X[0, j, 0:32, :] for j in range(EY)]
    low_y = [X[i, 0, 32:64, :] for i in range(EX)]
    low_z = [X[i, j, 64:96, :] for i, j in cells]
    low = pack(low_y, 0, 12, pack(low_x, 0, 8, pack(low_z, 0)))
    zs[0] = squeeze(low)
    edge[...] = squeeze(pack(low_y, EZ - 1, 12, pack(low_x, EZ - 1, 8)))
    pl.semaphore_wait(barrier, partners)
    copies = [
        send(X.at[0, :, 0:32, :], gx.at[0], -1, 0, 0),
        send(X.at[0, 0, 0:64, :], pair_xy, -1, -1, 0),
        send(X.at[1, 0, 32:64, :], corner.at[0], 1, -1, 0),
        send(X.at[0, EY - 1, 0:32, :], corner.at[1], -1, 1, 0),
        send(zs.at[0], packed.at[0], -1, 0, -1),
        send(zs.at[0], packed.at[1], 1, 0, -1),
        send(edge, packed.at[2], -1, 0, 1),
        send(zs.at[0], packed.at[3], 0, -1, -1),
        send(zs.at[0], packed.at[4], 0, 1, -1),
        send(edge, packed.at[5], 0, -1, 1),
        send(X.at[:, 0, 32:64, :], gy.at[0], 0, -1, 0),
        send(zs.at[0], gz.at[0], 0, 0, -1),
    ]
    for copy in loads[8:]:
        copy.start()
    for copy in loads[3:8]:
        copy.wait()
    wt[...] = fi[...].astype(F32) * co[...]
    s = sf[...]
    high = s.astype(BF16)
    SX[0:192, :] = high
    SX[192:384, :] = (s - high.astype(F32)).astype(BF16)
    hx[0] = jnp.zeros((EY, FD, EZ), F32)
    hy[0] = jnp.zeros((EX, FD, EZ), F32)
    hz[0] = jnp.zeros((FD, EZ), F32)

    def residual(i, j, a):
        n = i * EY + j
        load = bn[pl.ds(a * FD * CELLS + n, FD, stride=CELLS), :]
        return load - diag(a, n) * X[i, j, 32 * a : 32 * a + 32, :] - gathered(i, j, a)

    apply(X, 0, 0)
    for j in range(EY):
        px[j] = residual(0, j, 0)
    copies.append(send(px, gx.at[1], -1, 0, 0))
    apply(X, 0, 1)
    for j in range(EY):
        cx[0, j] = upper(j, 0)
    copies.append(send(cx.at[0], ux.at[0], 1, 0, 0))
    for i in range(EX):
        py[i] = residual(i, 0, 1)
        cy[0, i] = upper(i, 1)
    copies.append(send(py, gy.at[1], 0, -1, 0))
    copies.append(send(cy.at[0], uy.at[0], 0, 1, 0))
    zs[1] = squeeze(pack([residual(i, j, 2) for i, j in cells], 0))
    cs[0] = squeeze(upper_z())
    copies.append(send(zs.at[1], gz.at[1], 0, 0, -1))
    copies.append(send(cs.at[0], uz.at[0], 0, 0, 1))
    for n, step in enumerate(near):
        copies.append(send(wt, near_w.at[n], *step))
    known_1 = announce(know.at[0], near)

    def put(block, first, value):
        cols = slice(first, first + value.shape[1])
        high = value.astype(BF16)
        CH[32 * block : 32 * block + 32, cols] = high
        CL[32 * block : 32 * block + 32, cols] = (value - high.astype(F32)).astype(BF16)

    CH[...] = jnp.zeros(CH.shape, BF16)
    CL[...] = jnp.zeros(CL.shape, BF16)
    for j in range(EY):
        put(1, EZ * j, low_x[j])
    for i in range(EX):
        put(3, 1024 + EZ * i, low_y[i])
    put(5, 1536, low)

    def volume(n):
        pair = [FN[pl.ds(n + m, 384, stride=CELLS), :] for m in range(2)]
        moved = dot(vb[...], jnp.concatenate([p.astype(BF16) for p in pair], axis=1))
        for m in range(2):
            coarse = 1.0 - fi[n + m : n + m + 1, :].astype(F32)
            BASE[n + m] = pair[m] + TIME_STEP * (coarse * moved[:, EZ * m : EZ * m + EZ])

    loads[8].wait()
    for n in range(0, 3072, 128):
        FN[n : n + 128, :] = fb[n : n + 128, :].astype(F32)
    loads[9].wait()
    volume(0)
    volume(2)
    for copy in copies[:12]:
        copy.wait_recv()
    ghosts(0, lambda j: 0.0, lambda i: 0.0, lambda: 0.0)

    def last(packed, n):
        return jnp.where(lane == EZ - 1, unpack(packed, n, EZ - 1), 0.0)

    def moved(packed, n, to):
        return jnp.where(lane == to, unpack(packed, n, to), 0.0)

    def over(axis, value):
        return keep(has_up[axis], value)

    apart = [spread(packed[n]) for n in range(6)]
    put(3, 384, over(1, corner[0]))
    put(3, 896, over(1, pair_xy[32:64, :]))
    put(1, 1152, over(0, corner[1]))
    put(1, 1408, over(0, pair_xy[0:32, :]))
    for j in range(EY):
        put(5, EZ * j, over(2, last(apart[1], EY + j)))
        put(5, 512 + EZ * j, over(2, last(apart[0], j)))
    for i in range(EX):
        put(5, 1024 + EZ * i, over(2, last(apart[4], i * EY + EY - 1)))
        put(5, 1280 + EZ * i, over(2, last(apart[3], i * EY)))
    second = jnp.logical_and(lane >= EY, lane < 2 * EY)
    put(1, 1536, over(0, jnp.where(second, pltpu.roll(apart[2], EZ - 4, 1), 0.0)))
    put(1, 1664, over(0, jnp.where(second, pltpu.roll(apart[0], EZ - 4, 1), 0.0)))
    put(3, 1536, over(1, moved(apart[5], 12, EY - 1) + moved(apart[5], 13, 2 * EY - 1)))
    put(3, 1664, over(1, moved(apart[3], 12, EY - 1) + moved(apart[3], 13, 2 * EY - 1)))

    def correction(pair, first, size):
        rows, lower = slice(64 * pair, 64 * pair + 64), slice(192 + 64 * pair, 256 + 64 * pair)
        cols = slice(first, first + 2 * size)
        both = dot(jnp.concatenate([SX[rows, :], SX[lower, :]], axis=0), CH[:, cols])
        out = both[0:64, :] + (dot(SX[rows, :], CL[:, cols]) + both[64:128, :])
        return out[32:64, 0:size], out[0:32, size : 2 * size]

    def ends(n, at):
        out = jnp.zeros((1, EZ), F32)
        for c in range(CELLS):
            out = jnp.where(lane[0:1] == c, jnp.broadcast_to(near_w[n, c : c + 1, at : at + 1], (1, EZ)), out)
        return out

    def cut(value, n):
        return value[:, EZ * n : EZ * n + EZ]

    xl, xh = correction(0, 0, 512)
    yl, yh = correction(1, 1024, 256)
    zl, zh = correction(2, 1536, 128)
    convert(X, 0, 0, True)
    convert(X, 0, 1, True)
    multiply(0)
    multiply(1)
    for i, j in cells:
        for a in range(3):
            PR[i, j, 32 * a : 32 * a + 32, :] = residual(i, j, a)
    for copy in copies[12:]:
        copy.wait_recv()
    pl.semaphore_wait(know.at[0], known_1)

    xl = [cut(xl, j) * near_w[0, EY + j : EY + j + 1, :] for j in range(EY)]
    xh = [cut(xh, j) * near_w[1, j : j + 1, :] for j in range(EY)]
    yl = [cut(yl, i) * near_w[2, i * EY + EY - 1 : i * EY + EY, :] for i in range(EX)]
    yh = [cut(yh, i) * near_w[3, i * EY : i * EY + 1, :] for i in range(EX)]
    zl = zl * ends(4, EZ - 1)
    zh = zh * ends(5, 0)

    from_z = spread(uz[0]) + zl
    for n, (i, j) in enumerate(cells):
        along_x, along_y, along_z = PR[i, j, 0:32, :], PR[i, j, 32:64, :], PR[i, j, 64:96, :]
        if i == 0:
            along_x = along_x - keep(has_down[0], ux[0, j] + xl[j])
        if j == 0:
            along_y = along_y - keep(has_down[1], uy[0, i] + yl[i])
        below = jnp.where(lane == 0, unpack(from_z, n, 0), 0.0)
        R0[i, j, 0:32, :] = along_x
        R0[i, j, 32:64, :] = along_y
        R0[i, j, 64:96, :] = along_z - keep(has_down[2], below)
    ghosts(1, lambda j: -xh[j] - upper(j, 0), lambda i: -yh[i] - upper(i, 1), lambda: -zh - upper_z())

    def image(i, j, a):
        return diag(a, i * EY + j) * R0[i, j, 32 * a : 32 * a + 32, :] + gathered(i, j, a)

    early = list(started)
    copies = round_trip(R0, P0, 2, image)
    known_2 = announce(know.at[1], [(2, 0, 0), (-2, 0, 0), (0, 2, 0), (0, -2, 0), (2, 0, 1), (-2, 0, -1)])
    for copy in early:
        copy.wait_send()
    zero = jnp.zeros((8, EZ), F32)

    def over_ghosts(value):
        out = zero
        for j in range(EY):
            out = out + fold(value(hx[1, j], hx[2, j], cx[1, j], upper(j, 0)))
        for i in range(EX):
            out = out + fold(value(hy[1, i], hy[2, i], cy[1, i], upper(i, 1)))
        return out

    sum_a, sum_e00 = zero, zero
    for i, j in cells:
        r = R0[i, j]
        sum_a = sum_a + fold(r * r)
        sum_e00 = sum_e00 + fold(r * P0[i, j])
    sum_e00 = sum_e00 + over_ghosts(lambda r, w, c0, c1: r * c0) + fold(hz[1] * cz[...])
    a = total(sum_a)
    e00 = total(sum_e00)
    shift = jnp.where(a > 0.0, e00 / jnp.where(a > 0.0, a, 1.0), 0.0)
    volume(4)
    volume(6)
    loads[10].wait()
    LF[...] = ltb[...].astype(F32).T.astype(BF16)
    for copy in copies:
        copy.wait_recv()
    if known_2:
        pl.semaphore_wait(know.at[1], known_2)
    ghosts(2, lambda j: cx[1, j], lambda i: cy[1, i], lambda: cz[...])
    complete(P0, W1, 2, 1.0)

    apply(W1, 2, 0)
    apply(W1, 2, 1)
    sum_b, sum_c, sum_e01, sum_e11 = zero, zero, zero, zero
    for n, (i, j) in enumerate(cells):
        for k in range(3):
            at = slice(32 * k, 32 * k + 32)
            r, w, p = R0[i, j, at, :], W1[i, j, at, :], P0[i, j, at, :]
            q = w - shift * r
            sum_b = sum_b + fold(r * q)
            sum_c = sum_c + fold(q * q)
            sum_e01 = sum_e01 + fold(q * p)
            sum_e11 = sum_e11 + fold(q * (diag(k, n) * w + gathered(i, j, k) - shift * p))
    top = upper_z()
    q = hz[2] - shift * hz[1]
    sum_e01 = sum_e01 + fold(q * cz[...]) + over_ghosts(lambda r, w, c0, c1: (w - shift * r) * c0)
    sum_e11 = sum_e11 + fold(q * (top - shift * cz[...]))
    sum_e11 = sum_e11 + over_ghosts(lambda r, w, c0, c1: (w - shift * r) * (c1 - shift * c0))
    row = lax.broadcasted_iota(jnp.int32, (8, EZ), 0)
    column = lax.broadcasted_iota(jnp.int32, (1, EZ), 1)
    tile = zero
    for n, value in [(2, sum_b), (3, sum_c), (5, sum_e01), (6, sum_e11)]:
        tile = jnp.where(row == n, jnp.sum(value, axis=0, keepdims=True), tile)
    tile = jnp.broadcast_to(jnp.sum(tile, axis=1, keepdims=True), (8, EZ))
    for n, value in [(0, shift), (1, a), (4, e00)]:
        tile = jnp.where(row == n, value, tile)
    place = core + 2 * me[1]
    mine = lax.broadcasted_iota(jnp.int32, (8, EZ), 1) == 16 * row + place
    own[...] = jnp.sum(jnp.where(mine, tile, 0.0), axis=0, keepdims=True)

    def gather(k, source, landing, targets, sent):
        for n, target in enumerate(targets):
            pltpu.make_async_remote_copy(
                src_ref=source, dst_ref=landing.at[n], send_sem=gather_send.at[k], recv_sem=gather_recv.at[k],
                device_id=target, device_id_type=MESH,
            ).start()
        sent()
        pltpu.make_async_copy(landing, landing, gather_recv.at[k]).wait()

    gather(0, own, ra, [
        {"gx": other_core if c else me[0], "gy": ring[1][z]} for c, z in along(sizes)
    ], lambda: [copy.wait_send() for copy in copies])
    total_row = own[...]
    for n in range(ra.shape[0]):
        total_row = total_row + ra[n]
    own_b[...] = total_row
    gather(1, own_b, rb, [
        {"gx": ring[0][2 * y], "gz": ring[2][z]} for y, z in across(sizes)
    ], lambda: pltpu.make_async_copy(ra, ra, gather_send.at[0]).wait())
    rows = lax.broadcasted_iota(jnp.int32, (16, EZ), 0)
    tile = jnp.where(rows == 0, total_row, 0.0)
    for n in range(rb.shape[0]):
        tile = jnp.where(rows == n + 1, rb[n], tile)
    moments[...] = tile
    pltpu.make_async_copy(rb, rb, gather_send.at[1]).wait()


def finish(*refs):
    (moments, X, R0, W1, hx, hy, hz, BASE, LF, fi, fo_hbm, xo_hbm, GH, ON, FO, XO, new_v, new_x, new_y, new_z, out_sem) = refs
    cells = [(i, j) for i in range(EX) for j in range(EY)]
    lane = lax.broadcasted_iota(jnp.int32, (FD, EZ), 1)
    tile = moments[...]

    held = lax.broadcasted_iota(jnp.int32, (16, EZ), 1) < 16

    def number(n):
        return jnp.where(held, pltpu.roll(tile, EZ - 16 * n, 1) if n else tile, 0.0)

    shift, a, b, c, e00, e01, e11 = [number(n) for n in range(7)]

    def summed(value):
        return jnp.sum(jnp.sum(value, axis=0, keepdims=True), axis=1, keepdims=True)

    norm0, energy0 = summed(a), summed(e00)
    alpha0 = norm0 / energy0
    f = 1.0 - alpha0 * shift
    norm1 = summed(f * f * a - 2.0 * alpha0 * f * b + alpha0 * alpha0 * c)
    energy1 = summed(f * f * e00 - 2.0 * alpha0 * f * e01 + alpha0 * alpha0 * e11)
    mixed = summed(f * e00 - alpha0 * e01)
    beta = norm1 / norm0
    alpha1 = norm1 / (energy1 + 2.0 * beta * mixed + beta * beta * energy0)
    on_r = alpha0 + alpha1 * (1.0 + beta)
    on_w = -alpha1 * alpha0

    for n, (i, j) in enumerate(cells):
        new = X[i, j] + on_r * R0[i, j] + on_w * W1[i, j]
        new_v[i, j] = new
        XO[pl.ds(n, 96, stride=CELLS), :] = new
    copies = [pltpu.make_async_copy(XO, xo_hbm, out_sem.at[0])]
    copies[0].start()
    for j in range(EY):
        new_x[j] = hx[0, j] + on_r * hx[1, j] + on_w * hx[2, j]
    for i in range(EX):
        new_y[i] = hy[0, i] + on_r * hy[1, i] + on_w * hy[2, i]
    new_z[...] = hz[0] + on_r * hz[1] + on_w * hz[2]
    for n, (i, j) in enumerate(cells):
        fine = fi[n : n + 1, :] > 0
        new_faces = faces_of(new_v, new_x, new_y, new_z, lane, i, j)
        old_faces = faces_of(X, hx.at[0], hy.at[0], hz.at[0], lane, i, j)
        for at, (new, old) in enumerate(zip(new_faces, old_faces)):
            GH[32 * at : 32 * at + 32, EZ * n : EZ * n + EZ] = jnp.where(fine, new, old).astype(BF16)
    rows = 384 // CHUNKS
    for chunk in range(CHUNKS):
        at = slice(rows * chunk, rows * chunk + rows)
        for n in range(0, CELLS, 2):
            lifted = dot(LF[at, :], GH[:, EZ * n : EZ * n + 2 * EZ])
            for m in range(2):
                ON[pl.ds(rows * CELLS * chunk + n + m, rows, stride=CELLS), :] = (
                    BASE[n + m, at, :] + TIME_STEP * lifted[:, EZ * m : EZ * m + EZ]
                )
        for n in range(rows * CELLS * chunk, rows * CELLS * (chunk + 1), 128):
            FO[n : n + 128, :] = ON[n : n + 128, :].astype(BF16)
        where = slice(rows * CELLS * chunk, rows * CELLS * (chunk + 1))
        copy = pltpu.make_async_copy(FO.at[where, :], fo_hbm.at[where, :], out_sem.at[1 + chunk])
        copy.start()
        copies.append(copy)
    for copy in copies:
        copy.wait()


def solution(mesh):
    sizes = tuple(mesh.shape[n] for n in ("gx", "gy", "gz"))

    def body(fields, trace_old, face_load, face_diag, fine_flag, coeff, volume_op, lift_op, schur_op):
        vmem = pltpu.VMEM
        field = (EX, EY, 96, EZ)
        copies = 12 + 6 + 6 + 6
        group, column = len(across(sizes)), len(along(sizes))
        scratch = [
            vmem((768, EZ), F32), vmem((768, EZ), F32), vmem((24, EZ), F32),
            vmem((8, EZ), F32), vmem((3072, EZ), BF16), vmem((384, 384), BF16), vmem((192, 384), BF16),
            vmem((192, 192), F32),
            vmem(field, F32), vmem(field, F32),
            vmem((CELLS, 192, EZ), F32), vmem((192, CELLS * EZ), BF16), vmem((192, CELLS * EZ), BF16),
            vmem((384, 192), BF16),
            vmem((3072, EZ), F32),
            vmem((3, EY, FD, EZ), F32), vmem((3, EX, FD, EZ), F32), vmem((3, 8, EZ), F32),
            vmem((2, EY, FD, EZ), F32), vmem((2, EX, FD, EZ), F32), vmem((2, 8, EZ), F32),
            vmem((2, EY, FD, EZ), F32), vmem((2, EX, FD, EZ), F32), vmem((FD, EZ), F32), vmem((2, 8, EZ), F32),
            vmem((3, 8, EZ), F32),
            vmem((1, EZ), F32), vmem((column, 1, EZ), F32), vmem((1, EZ), F32), vmem((group, 1, EZ), F32),
            vmem((8, EZ), F32), vmem((EY, FD, EZ), F32), vmem((EX, FD, EZ), F32), vmem((6, 8, EZ), F32), vmem((8, EZ), F32), vmem((64, EZ), F32), vmem((2, FD, EZ), F32),
            vmem((6, 8, EZ), F32),
            vmem((192, 1792), BF16), vmem((192, 1792), BF16),
            pltpu.SemaphoreType.DMA((11,)),
            pltpu.SemaphoreType.DMA((copies,)), pltpu.SemaphoreType.DMA((copies,)),
            pltpu.SemaphoreType.DMA((2,)), pltpu.SemaphoreType.DMA((2,)), pltpu.SemaphoreType.REGULAR((2,)),
        ]
        state = [
            ((16, EZ), F32), (field, F32), (field, F32), (field, F32),
            ((3, EY, FD, EZ), F32), ((3, EX, FD, EZ), F32), ((3, FD, EZ), F32),
            ((CELLS, 384, EZ), F32), ((384, 192), BF16), ((8, EZ), jnp.int32),
        ]
        in_vmem = pl.BlockSpec(memory_space=pltpu.VMEM)
        kept = pl.pallas_call(
            functools.partial(kernel, sizes),
            out_shape=[jax.ShapeDtypeStruct(*entry) for entry in state],
            in_specs=[pl.BlockSpec(memory_space=pltpu.HBM)] * 9,
            out_specs=[in_vmem] * len(state),
            scratch_shapes=scratch,
            compiler_params=pltpu.CompilerParams(
                collective_id=0, has_side_effects=True, vmem_limit_bytes=32 * 1024 * 1024
            ),
            name="step",
        )(
            *(
                pltpu.with_memory_space_constraint(value, pltpu.HBM)
                for value in (
                    trace_old.reshape(768, EZ), face_load.reshape(768, EZ), face_diag.reshape(24, EZ),
                    fine_flag.reshape(8, EZ), coeff.reshape(8, EZ), fields.reshape(3072, EZ), volume_op, lift_op.T,
                    schur_op,
                )
            )
        )
        out_f, out_x = pl.pallas_call(
            finish,
            out_shape=(jax.ShapeDtypeStruct((3072, EZ), BF16), jax.ShapeDtypeStruct((768, EZ), F32)),
            in_specs=[in_vmem] * len(state),
            out_specs=(pl.BlockSpec(memory_space=pltpu.HBM),) * 2,
            scratch_shapes=[
                vmem((192, CELLS * EZ), BF16), vmem((3072, EZ), F32), vmem((3072, EZ), BF16), vmem((768, EZ), F32),
                vmem(field, F32), vmem((EY, FD, EZ), F32), vmem((EX, FD, EZ), F32), vmem((FD, EZ), F32),
                pltpu.SemaphoreType.DMA((1 + CHUNKS,)),
            ],
            compiler_params=pltpu.CompilerParams(vmem_limit_bytes=24 * 1024 * 1024),
            name="finish",
        )(*kept)
        return out_f.reshape(fields.shape), out_x.reshape(trace_old.shape)

    return jax.shard_map(
        body,
        mesh=mesh,
        in_specs=(
            P(None, "gx", "gy", "gz"),
            P(None, None, "gx", "gy", "gz"),
            P(None, None, "gx", "gy", "gz"),
            P(None, "gx", "gy", "gz"),
            P("gx", "gy", "gz"),
            P("gx", "gy", "gz"),
            P(),
            P(),
            P(),
        ),
        out_specs=(P(None, "gx", "gy", "gz"), P(None, None, "gx", "gy", "gz")),
        check_vma=False,
    )
```

```python
import functools

import jax
import jax.numpy as jnp
from jax import lax
from jax.experimental import pallas as pl
from jax.experimental.pallas import tpu as pltpu
from jax.sharding import PartitionSpec as P

MESH = pl.DeviceIdType.MESH
EX, EY, EZ = 2, 4, 128
CELLS = EX * EY
FD = 32
F32, BF16 = jnp.float32, jnp.bfloat16
TIME_STEP = 0.25
CHUNKS = 3


def dot(a, b):
    return jnp.dot(a, b, preferred_element_type=F32)


def fold(value):
    return jnp.sum(value.reshape(-1, 8, 128), axis=0)


def total(value):
    return jnp.sum(jnp.sum(value, axis=0, keepdims=True), axis=1, keepdims=True)


def across(sizes):
    steps = [(y, z) for y in range(sizes[0] // 2) for z in range(sizes[2]) if y or z]
    return sorted(steps, key=lambda s: -min(s[0], sizes[0] // 2 - s[0]) - min(s[1], sizes[2] - s[1]))


def along(sizes):
    steps = [(c, z) for z in range(sizes[1]) for c in range(2) if c or z]
    return sorted(steps, key=lambda s: -min(s[1], sizes[1] - s[1]) - 0.5 * s[0])


def unpack(packed, n, at):
    return pltpu.roll(packed, (at - n) % EZ, 1)


def squeeze(value):
    out = value[0:8, :]
    for n in range(1, 4):
        out = out + pltpu.roll(value[8 * n : 8 * n + 8, :], 16 * n, 1)
    return out


def spread(value):
    wide = jnp.concatenate([value] + [pltpu.roll(value, EZ - 16 * n, 1) for n in range(1, 4)], axis=0)
    return jnp.where(lax.broadcasted_iota(jnp.int32, wide.shape, 1) < 16, wide, 0.0)


def faces_of(v, hx, hy, hz, lane, i, j):
    n = i * EY + j
    z = v[i, j, 64:96, :]
    return [
        v[i, j, 0:32, :],
        v[i + 1, j, 0:32, :] if i + 1 < EX else hx[j],
        v[i, j, 32:64, :],
        v[i, j + 1, 32:64, :] if j + 1 < EY else hy[i],
        z,
        jnp.where(lane == EZ - 1, unpack(hz[...], n, EZ - 1), pltpu.roll(z, EZ - 1, 1)),
    ]


def kernel(sizes, *refs):
    (x_hbm, b_hbm, diag_hbm, fine_hbm, coeff_hbm, f_hbm, v_hbm, lt_hbm, s_hbm) = refs[:9]
    (moments, X, R0, W1, hx, hy, hz, BASE, LF, fi) = refs[9:19]
    (xn, bn, dg, co, fb, vb, ltb, sf, PR, P0, T, GH, GL, SX, FN,
     gx, gy, gz, ux, uy, uz, cx, cy, cz, cs, zs, own, ra, own_b, rb,
     wt, px, py, near_w, edge, pair_xy, corner, packed, CH, CL,
     load_sem, send_sem, recv_sem, gather_send, gather_recv, know) = refs[19:]
    names = ("gx", "gy", "gz")
    me = [lax.axis_index(n) for n in names]
    has_up = [m < n - 1 for m, n in zip(me, sizes)]
    has_down = [m > 0 for m in me]

    barrier = pltpu.get_barrier_semaphore()

    ring = [[m] + [lax.rem(m + k, n) for k in range(1, n)] for m, n in zip(me, sizes)]

    def at(*steps):
        return {
            names[axis]: ring[axis][step % sizes[axis]] for axis, step in enumerate(steps) if step
        }

    def announce(sem, steps):
        count = 0
        for each in steps:
            if any(step % n for step, n in zip(each, sizes)):
                pl.semaphore_signal(sem, inc=1, device_id=at(*each), device_id_type=MESH)
                count += 1
        return count

    near = [(1, 0, 0), (-1, 0, 0), (0, 1, 0), (0, -1, 0), (0, 0, 1), (0, 0, -1)]
    both = [(p, q) for p in (1, -1) for q in (1, -1)]
    diagonal = [(p, q, 0) for p, q in both] + [(p, 0, q) for p, q in both] + [(0, p, q) for p, q in both]
    loads = [
        pltpu.make_async_copy(src, dst, load_sem.at[k])
        for k, (src, dst) in enumerate(
            [(x_hbm.at[256 * a : 256 * a + 256, :], xn.at[256 * a : 256 * a + 256, :]) for a in range(3)]
            + [(fine_hbm, fi), (coeff_hbm, co), (s_hbm, sf), (diag_hbm, dg), (b_hbm, bn),
               (f_hbm, fb), (v_hbm, vb), (lt_hbm, ltb)]
        )
    ]
    for copy in loads[:3]:
        copy.start()
    partners = announce(barrier, near + diagonal)
    for copy in loads[3:8]:
        copy.start()
    core = lax.rem(me[0], 2)
    other_core = me[0] + 1 - 2 * core

    started = []

    def send(src, dst, *steps):
        k = len(started)
        copy = pltpu.make_async_remote_copy(
            src_ref=src, dst_ref=dst, send_sem=send_sem.at[k], recv_sem=recv_sem.at[k],
            device_id=at(*steps), device_id_type=MESH,
        )
        copy.start()
        started.append(copy)
        return copy

    lane = lax.broadcasted_iota(jnp.int32, (FD, EZ), 1)
    cells = [(i, j) for i in range(EX) for j in range(EY)]

    def keep(flag, value):
        return jnp.where(flag, value, 0.0)

    def pack(pieces, lane_of, first=0, out=None):
        out = jnp.zeros((FD, EZ), F32) if out is None else out
        for n, piece in enumerate(pieces, first):
            out = jnp.where(lane == n, pltpu.roll(piece, (n - lane_of) % EZ, 1), out)
        return out

    def faces(v, k, i, j):
        return faces_of(v, hx.at[k], hy.at[k], hz.at[k], lane, i, j)

    def convert(v, k, half, upper_only=False):
        for n, (i, j) in enumerate(cells):
            if i != half:
                continue
            fresh = (1,) * (i == EX - 1) + (3,) * (j == EY - 1) + (5,) if upper_only else range(6)
            for at, block in enumerate(faces(v, k, i, j)):
                if at not in fresh:
                    continue
                high = block.astype(BF16)
                low = (block - high.astype(F32)).astype(BF16)
                GH[32 * at : 32 * at + 32, EZ * n : EZ * n + EZ] = high
                GL[32 * at : 32 * at + 32, EZ * n : EZ * n + EZ] = low
    def multiply(half):
        for n in range(EY * half, EY * half + EY, 2):
            cols = slice(EZ * n, EZ * n + 2 * EZ)
            both = dot(SX[...], GH[:, cols])
            product = both[0:192, :] + (dot(SX[0:192, :], GL[:, cols]) + both[192:384, :])
            for m in range(2):
                T[n + m] = product[:, EZ * m : EZ * m + EZ] * weight(n + m)

    def apply(v, k, half):
        convert(v, k, half)
        multiply(half)

    def weight(n):
        return wt[n : n + 1, :]

    def gathered(i, j, a):
        n = i * EY + j
        at = 64 * a
        value = T[n, at : at + 32, :]
        if a == 0 and i > 0:
            value = value + T[n - EY, at + 32 : at + 64, :]
        if a == 1 and j > 0:
            value = value + T[n - 1, at + 32 : at + 64, :]
        if a == 2:
            value = value + jnp.where(lane == 0, 0.0, pltpu.roll(T[n, at + 32 : at + 64, :], 1, 1))
        return value

    def upper(i_or_j, axis):
        if axis == 0:
            return T[(EX - 1) * EY + i_or_j, 32:64, :]
        return T[i_or_j * EY + EY - 1, 96:128, :]

    def upper_z():
        return pack([T[n, 160:192, :] for n in range(CELLS)], EZ - 1)

    def diag(a, n):
        return dg[a * CELLS + n : a * CELLS + n + 1, :]

    def round_trip(v, p, k, partial):
        out = []
        done = set()

        def put(i, j, a):
            p[i, j, 32 * a : 32 * a + 32, :] = partial(i, j, a)
            done.add((i, j, a))

        apply(v, k - 1, 0)
        for j in range(EY):
            put(0, j, 0)
        out.append(send(p.at[0, :, 0:32, :], gx.at[k], -1, 0, 0))
        apply(v, k - 1, 1)
        for j in range(EY):
            cx[k - 1, j] = upper(j, 0)
        out.append(send(cx.at[k - 1], ux.at[k - 1], 1, 0, 0))
        for i in range(EX):
            put(i, 0, 1)
        out.append(send(p.at[:, 0, 32:64, :], gy.at[k], 0, -1, 0))
        for i in range(EX):
            cy[k - 1, i] = upper(i, 1)
        out.append(send(cy.at[k - 1], uy.at[k - 1], 0, 1, 0))
        for i, j in cells:
            put(i, j, 2)
        zs[k] = squeeze(pack([p[i, j, 64:96, :] for i, j in cells], 0))
        out.append(send(zs.at[k], gz.at[k], 0, 0, -1))
        cz[...] = upper_z()
        cs[k - 1] = squeeze(cz[...])
        out.append(send(cs.at[k - 1], uz.at[k - 1], 0, 0, 1))
        for i, j in cells:
            for a in range(3):
                if (i, j, a) not in done:
                    put(i, j, a)
        return out

    def ghosts(k, own_x, own_y, own_z):
        for j in range(EY):
            hx[k, j] = keep(has_up[0], gx[k, j] + own_x(j))
        for i in range(EX):
            hy[k, i] = keep(has_up[1], gy[k, i] + own_y(i))
        hz[k] = keep(has_up[2], spread(gz[k]) + own_z())

    def complete(p, out, k, sign):
        from_z = spread(uz[k - 1])
        for n, (i, j) in enumerate(cells):
            along_x, along_y, along_z = p[i, j, 0:32, :], p[i, j, 32:64, :], p[i, j, 64:96, :]
            if i == 0:
                along_x = along_x + sign * keep(has_down[0], ux[k - 1, j])
            if j == 0:
                along_y = along_y + sign * keep(has_down[1], uy[k - 1, i])
            below = jnp.where(lane == 0, unpack(from_z, n, 0), 0.0)
            along_z = along_z + sign * keep(has_down[2], below)
            out[i, j, 0:32, :] = along_x
            out[i, j, 32:64, :] = along_y
            out[i, j, 64:96, :] = along_z

    for a in range(3):
        loads[a].wait()
        for n, (i, j) in enumerate(cells):
            X[i, j, 32 * a : 32 * a + 32, :] = xn[pl.ds(256 * a + n, FD, stride=CELLS), :]
    low_x = [X[0, j, 0:32, :] for j in range(EY)]
    low_y = [X[i, 0, 32:64, :] for i in range(EX)]
    low_z = [X[i, j, 64:96, :] for i, j in cells]
    low = pack(low_y, 0, 12, pack(low_x, 0, 8, pack(low_z, 0)))
    zs[0] = squeeze(low)
    edge[...] = squeeze(pack(low_y, EZ - 1, 12, pack(low_x, EZ - 1, 8)))
    pl.semaphore_wait(barrier, partners)
    copies = [
        send(X.at[0, :, 0:32, :], gx.at[0], -1, 0, 0),
        send(X.at[0, 0, 0:64, :], pair_xy, -1, -1, 0),
        send(X.at[1, 0, 32:64, :], corner.at[0], 1, -1, 0),
        send(X.at[0, EY - 1, 0:32, :], corner.at[1], -1, 1, 0),
        send(zs.at[0], packed.at[0], -1, 0, -1),
        send(zs.at[0], packed.at[1], 1, 0, -1),
        send(edge, packed.at[2], -1, 0, 1),
        send(zs.at[0], packed.at[3], 0, -1, -1),
        send(zs.at[0], packed.at[4], 0, 1, -1),
        send(edge, packed.at[5], 0, -1, 1),
        send(X.at[:, 0, 32:64, :], gy.at[0], 0, -1, 0),
        send(zs.at[0], gz.at[0], 0, 0, -1),
    ]
    for copy in loads[8:]:
        copy.start()
    for copy in loads[3:8]:
        copy.wait()
    wt[...] = fi[...].astype(F32) * co[...]
    s = sf[...]
    high = s.astype(BF16)
    SX[0:192, :] = high
    SX[192:384, :] = (s - high.astype(F32)).astype(BF16)
    hx[0] = jnp.zeros((EY, FD, EZ), F32)
    hy[0] = jnp.zeros((EX, FD, EZ), F32)
    hz[0] = jnp.zeros((FD, EZ), F32)

    def residual(i, j, a):
        n = i * EY + j
        load = bn[pl.ds(a * FD * CELLS + n, FD, stride=CELLS), :]
        return load - diag(a, n) * X[i, j, 32 * a : 32 * a + 32, :] - gathered(i, j, a)

    apply(X, 0, 0)
    for j in range(EY):
        px[j] = residual(0, j, 0)
    copies.append(send(px, gx.at[1], -1, 0, 0))
    apply(X, 0, 1)
    for j in range(EY):
        cx[0, j] = upper(j, 0)
    copies.append(send(cx.at[0], ux.at[0], 1, 0, 0))
    for i in range(EX):
        py[i] = residual(i, 0, 1)
        cy[0, i] = upper(i, 1)
    copies.append(send(py, gy.at[1], 0, -1, 0))
    copies.append(send(cy.at[0], uy.at[0], 0, 1, 0))
    zs[1] = squeeze(pack([residual(i, j, 2) for i, j in cells], 0))
    cs[0] = squeeze(upper_z())
    copies.append(send(zs.at[1], gz.at[1], 0, 0, -1))
    copies.append(send(cs.at[0], uz.at[0], 0, 0, 1))
    for n, step in enumerate(near):
        copies.append(send(wt, near_w.at[n], *step))
    known_1 = announce(know.at[0], near)

    def put(block, first, value):
        cols = slice(first, first + value.shape[1])
        high = value.astype(BF16)
        CH[32 * block : 32 * block + 32, cols] = high
        CL[32 * block : 32 * block + 32, cols] = (value - high.astype(F32)).astype(BF16)

    CH[...] = jnp.zeros(CH.shape, BF16)
    CL[...] = jnp.zeros(CL.shape, BF16)
    for j in range(EY):
        put(1, EZ * j, low_x[j])
    for i in range(EX):
        put(3, 1024 + EZ * i, low_y[i])
    put(5, 1536, low)

    def volume(n):
        pair = [FN[pl.ds(n + m, 384, stride=CELLS), :] for m in range(2)]
        moved = dot(vb[...], jnp.concatenate([p.astype(BF16) for p in pair], axis=1))
        for m in range(2):
            coarse = 1.0 - fi[n + m : n + m + 1, :].astype(F32)
            BASE[n + m] = pair[m] + TIME_STEP * (coarse * moved[:, EZ * m : EZ * m + EZ])

    for copy in copies[:12]:
        copy.wait_recv()
    ghosts(0, lambda j: 0.0, lambda i: 0.0, lambda: 0.0)

    def last(packed, n):
        return jnp.where(lane == EZ - 1, unpack(packed, n, EZ - 1), 0.0)

    def moved(packed, n, to):
        return jnp.where(lane == to, unpack(packed, n, to), 0.0)

    def over(axis, value):
        return keep(has_up[axis], value)

    apart = [spread(packed[n]) for n in range(6)]
    put(3, 384, over(1, corner[0]))
    put(3, 896, over(1, pair_xy[32:64, :]))
    put(1, 1152, over(0, corner[1]))
    put(1, 1408, over(0, pair_xy[0:32, :]))
    for j in range(EY):
        put(5, EZ * j, over(2, last(apart[1], EY + j)))
        put(5, 512 + EZ * j, over(2, last(apart[0], j)))
    for i in range(EX):
        put(5, 1024 + EZ * i, over(2, last(apart[4], i * EY + EY - 1)))
        put(5, 1280 + EZ * i, over(2, last(apart[3], i * EY)))
    second = jnp.logical_and(lane >= EY, lane < 2 * EY)
    put(1, 1536, over(0, jnp.where(second, pltpu.roll(apart[2], EZ - 4, 1), 0.0)))
    put(1, 1664, over(0, jnp.where(second, pltpu.roll(apart[0], EZ - 4, 1), 0.0)))
    put(3, 1536, over(1, moved(apart[5], 12, EY - 1) + moved(apart[5], 13, 2 * EY - 1)))
    put(3, 1664, over(1, moved(apart[3], 12, EY - 1) + moved(apart[3], 13, 2 * EY - 1)))

    def correction(pair, first, size):
        rows, lower = slice(64 * pair, 64 * pair + 64), slice(192 + 64 * pair, 256 + 64 * pair)
        cols = slice(first, first + 2 * size)
        both = dot(jnp.concatenate([SX[rows, :], SX[lower, :]], axis=0), CH[:, cols])
        out = both[0:64, :] + (dot(SX[rows, :], CL[:, cols]) + both[64:128, :])
        return out[32:64, 0:size], out[0:32, size : 2 * size]

    def ends(n, at):
        out = jnp.zeros((1, EZ), F32)
        for c in range(CELLS):
            out = jnp.where(lane[0:1] == c, jnp.broadcast_to(near_w[n, c : c + 1, at : at + 1], (1, EZ)), out)
        return out

    def cut(value, n):
        return value[:, EZ * n : EZ * n + EZ]

    xl, xh = correction(0, 0, 512)
    yl, yh = correction(1, 1024, 256)
    zl, zh = correction(2, 1536, 128)
    convert(X, 0, 0, True)
    convert(X, 0, 1, True)
    multiply(0)
    multiply(1)
    for i, j in cells:
        for a in range(3):
            PR[i, j, 32 * a : 32 * a + 32, :] = residual(i, j, a)
    for copy in copies[12:]:
        copy.wait_recv()
    pl.semaphore_wait(know.at[0], known_1)

    xl = [cut(xl, j) * near_w[0, EY + j : EY + j + 1, :] for j in range(EY)]
    xh = [cut(xh, j) * near_w[1, j : j + 1, :] for j in range(EY)]
    yl = [cut(yl, i) * near_w[2, i * EY + EY - 1 : i * EY + EY, :] for i in range(EX)]
    yh = [cut(yh, i) * near_w[3, i * EY : i * EY + 1, :] for i in range(EX)]
    zl = zl * ends(4, EZ - 1)
    zh = zh * ends(5, 0)

    from_z = spread(uz[0]) + zl
    for n, (i, j) in enumerate(cells):
        along_x, along_y, along_z = PR[i, j, 0:32, :], PR[i, j, 32:64, :], PR[i, j, 64:96, :]
        if i == 0:
            along_x = along_x - keep(has_down[0], ux[0, j] + xl[j])
        if j == 0:
            along_y = along_y - keep(has_down[1], uy[0, i] + yl[i])
        below = jnp.where(lane == 0, unpack(from_z, n, 0), 0.0)
        R0[i, j, 0:32, :] = along_x
        R0[i, j, 32:64, :] = along_y
        R0[i, j, 64:96, :] = along_z - keep(has_down[2], below)
    ghosts(1, lambda j: -xh[j] - upper(j, 0), lambda i: -yh[i] - upper(i, 1), lambda: -zh - upper_z())

    def image(i, j, a):
        return diag(a, i * EY + j) * R0[i, j, 32 * a : 32 * a + 32, :] + gathered(i, j, a)

    early = list(started)
    copies = round_trip(R0, P0, 2, image)
    known_2 = announce(know.at[1], [(2, 0, 0), (-2, 0, 0), (0, 2, 0), (0, -2, 0), (2, 0, 1), (-2, 0, -1)])
    for copy in early:
        copy.wait_send()
    zero = jnp.zeros((8, EZ), F32)

    def over_ghosts(value):
        out = zero
        for j in range(EY):
            out = out + fold(value(hx[1, j], hx[2, j], cx[1, j], upper(j, 0)))
        for i in range(EX):
            out = out + fold(value(hy[1, i], hy[2, i], cy[1, i], upper(i, 1)))
        return out

    sum_a, sum_e00 = zero, zero
    for i, j in cells:
        r = R0[i, j]
        sum_a = sum_a + fold(r * r)
        sum_e00 = sum_e00 + fold(r * P0[i, j])
    sum_e00 = sum_e00 + over_ghosts(lambda r, w, c0, c1: r * c0) + fold(hz[1] * cz[...])
    a = total(sum_a)
    e00 = total(sum_e00)
    shift = jnp.where(a > 0.0, e00 / jnp.where(a > 0.0, a, 1.0), 0.0)
    for copy in copies:
        copy.wait_recv()
    if known_2:
        pl.semaphore_wait(know.at[1], known_2)
    ghosts(2, lambda j: cx[1, j], lambda i: cy[1, i], lambda: cz[...])
    complete(P0, W1, 2, 1.0)

    apply(W1, 2, 0)
    apply(W1, 2, 1)
    sum_b, sum_c, sum_e01, sum_e11 = zero, zero, zero, zero
    for n, (i, j) in enumerate(cells):
        for k in range(3):
            at = slice(32 * k, 32 * k + 32)
            r, w, p = R0[i, j, at, :], W1[i, j, at, :], P0[i, j, at, :]
            q = w - shift * r
            sum_b = sum_b + fold(r * q)
            sum_c = sum_c + fold(q * q)
            sum_e01 = sum_e01 + fold(q * p)
            sum_e11 = sum_e11 + fold(q * (diag(k, n) * w + gathered(i, j, k) - shift * p))
    top = upper_z()
    q = hz[2] - shift * hz[1]
    sum_e01 = sum_e01 + fold(q * cz[...]) + over_ghosts(lambda r, w, c0, c1: (w - shift * r) * c0)
    sum_e11 = sum_e11 + fold(q * (top - shift * cz[...]))
    sum_e11 = sum_e11 + over_ghosts(lambda r, w, c0, c1: (w - shift * r) * (c1 - shift * c0))
    row = lax.broadcasted_iota(jnp.int32, (8, EZ), 0)
    column = lax.broadcasted_iota(jnp.int32, (1, EZ), 1)
    tile = zero
    for n, value in [(2, sum_b), (3, sum_c), (5, sum_e01), (6, sum_e11)]:
        tile = jnp.where(row == n, jnp.sum(value, axis=0, keepdims=True), tile)
    tile = jnp.broadcast_to(jnp.sum(tile, axis=1, keepdims=True), (8, EZ))
    for n, value in [(0, shift), (1, a), (4, e00)]:
        tile = jnp.where(row == n, value, tile)
    place = core + 2 * me[1]
    mine = lax.broadcasted_iota(jnp.int32, (8, EZ), 1) == 16 * row + place
    own[...] = jnp.sum(jnp.where(mine, tile, 0.0), axis=0, keepdims=True)

    def gather(k, source, landing, targets, sent):
        for n, target in enumerate(targets):
            pltpu.make_async_remote_copy(
                src_ref=source, dst_ref=landing.at[n], send_sem=gather_send.at[k], recv_sem=gather_recv.at[k],
                device_id=target, device_id_type=MESH,
            ).start()
        sent()
        pltpu.make_async_copy(landing, landing, gather_recv.at[k]).wait()

    def under_gather():
        for copy in copies:
            copy.wait_send()
        loads[8].wait()
        for n in range(0, 3072, 128):
            FN[n : n + 128, :] = fb[n : n + 128, :].astype(F32)
        loads[9].wait()
        volume(0)
        volume(2)
        volume(4)
        volume(6)
        loads[10].wait()
        LF[...] = ltb[...].astype(F32).T.astype(BF16)

    gather(0, own, ra, [
        {"gx": other_core if c else me[0], "gy": ring[1][z]} for c, z in along(sizes)
    ], under_gather)
    total_row = own[...]
    for n in range(ra.shape[0]):
        total_row = total_row + ra[n]
    own_b[...] = total_row
    gather(1, own_b, rb, [
        {"gx": ring[0][2 * y], "gz": ring[2][z]} for y, z in across(sizes)
    ], lambda: pltpu.make_async_copy(ra, ra, gather_send.at[0]).wait())
    rows = lax.broadcasted_iota(jnp.int32, (16, EZ), 0)
    tile = jnp.where(rows == 0, total_row, 0.0)
    for n in range(rb.shape[0]):
        tile = jnp.where(rows == n + 1, rb[n], tile)
    moments[...] = tile
    pltpu.make_async_copy(rb, rb, gather_send.at[1]).wait()


def finish(*refs):
    (moments, X, R0, W1, hx, hy, hz, BASE, LF, fi, fo_hbm, xo_hbm, GH, ON, FO, XO, new_v, new_x, new_y, new_z, out_sem) = refs
    cells = [(i, j) for i in range(EX) for j in range(EY)]
    lane = lax.broadcasted_iota(jnp.int32, (FD, EZ), 1)
    tile = moments[...]

    held = lax.broadcasted_iota(jnp.int32, (16, EZ), 1) < 16

    def number(n):
        return jnp.where(held, pltpu.roll(tile, EZ - 16 * n, 1) if n else tile, 0.0)

    shift, a, b, c, e00, e01, e11 = [number(n) for n in range(7)]

    def summed(value):
        return jnp.sum(jnp.sum(value, axis=0, keepdims=True), axis=1, keepdims=True)

    norm0, energy0 = summed(a), summed(e00)
    alpha0 = norm0 / energy0
    f = 1.0 - alpha0 * shift
    norm1 = summed(f * f * a - 2.0 * alpha0 * f * b + alpha0 * alpha0 * c)
    energy1 = summed(f * f * e00 - 2.0 * alpha0 * f * e01 + alpha0 * alpha0 * e11)
    mixed = summed(f * e00 - alpha0 * e01)
    beta = norm1 / norm0
    alpha1 = norm1 / (energy1 + 2.0 * beta * mixed + beta * beta * energy0)
    on_r = alpha0 + alpha1 * (1.0 + beta)
    on_w = -alpha1 * alpha0

    for n, (i, j) in enumerate(cells):
        new = X[i, j] + on_r * R0[i, j] + on_w * W1[i, j]
        new_v[i, j] = new
        XO[pl.ds(n, 96, stride=CELLS), :] = new
    copies = [pltpu.make_async_copy(XO, xo_hbm, out_sem.at[0])]
    copies[0].start()
    for j in range(EY):
        new_x[j] = hx[0, j] + on_r * hx[1, j] + on_w * hx[2, j]
    for i in range(EX):
        new_y[i] = hy[0, i] + on_r * hy[1, i] + on_w * hy[2, i]
    new_z[...] = hz[0] + on_r * hz[1] + on_w * hz[2]
    for n, (i, j) in enumerate(cells):
        fine = fi[n : n + 1, :] > 0
        new_faces = faces_of(new_v, new_x, new_y, new_z, lane, i, j)
        old_faces = faces_of(X, hx.at[0], hy.at[0], hz.at[0], lane, i, j)
        for at, (new, old) in enumerate(zip(new_faces, old_faces)):
            GH[32 * at : 32 * at + 32, EZ * n : EZ * n + EZ] = jnp.where(fine, new, old).astype(BF16)
    rows = 384 // CHUNKS
    for chunk in range(CHUNKS):
        at = slice(rows * chunk, rows * chunk + rows)
        for n in range(0, CELLS, 2):
            lifted = dot(LF[at, :], GH[:, EZ * n : EZ * n + 2 * EZ])
            for m in range(2):
                ON[pl.ds(rows * CELLS * chunk + n + m, rows, stride=CELLS), :] = (
                    BASE[n + m, at, :] + TIME_STEP * lifted[:, EZ * m : EZ * m + EZ]
                )
        for n in range(rows * CELLS * chunk, rows * CELLS * (chunk + 1), 128):
            FO[n : n + 128, :] = ON[n : n + 128, :].astype(BF16)
        where = slice(rows * CELLS * chunk, rows * CELLS * (chunk + 1))
        copy = pltpu.make_async_copy(FO.at[where, :], fo_hbm.at[where, :], out_sem.at[1 + chunk])
        copy.start()
        copies.append(copy)
    for copy in copies:
        copy.wait()


def solution(mesh):
    sizes = tuple(mesh.shape[n] for n in ("gx", "gy", "gz"))

    def body(fields, trace_old, face_load, face_diag, fine_flag, coeff, volume_op, lift_op, schur_op):
        vmem = pltpu.VMEM
        field = (EX, EY, 96, EZ)
        copies = 12 + 6 + 6 + 6
        group, column = len(across(sizes)), len(along(sizes))
        scratch = [
            vmem((768, EZ), F32), vmem((768, EZ), F32), vmem((24, EZ), F32),
            vmem((8, EZ), F32), vmem((3072, EZ), BF16), vmem((384, 384), BF16), vmem((192, 384), BF16),
            vmem((192, 192), F32),
            vmem(field, F32), vmem(field, F32),
            vmem((CELLS, 192, EZ), F32), vmem((192, CELLS * EZ), BF16), vmem((192, CELLS * EZ), BF16),
            vmem((384, 192), BF16),
            vmem((3072, EZ), F32),
            vmem((3, EY, FD, EZ), F32), vmem((3, EX, FD, EZ), F32), vmem((3, 8, EZ), F32),
            vmem((2, EY, FD, EZ), F32), vmem((2, EX, FD, EZ), F32), vmem((2, 8, EZ), F32),
            vmem((2, EY, FD, EZ), F32), vmem((2, EX, FD, EZ), F32), vmem((FD, EZ), F32), vmem((2, 8, EZ), F32),
            vmem((3, 8, EZ), F32),
            vmem((1, EZ), F32), vmem((column, 1, EZ), F32), vmem((1, EZ), F32), vmem((group, 1, EZ), F32),
            vmem((8, EZ), F32), vmem((EY, FD, EZ), F32), vmem((EX, FD, EZ), F32), vmem((6, 8, EZ), F32), vmem((8, EZ), F32), vmem((64, EZ), F32), vmem((2, FD, EZ), F32),
            vmem((6, 8, EZ), F32),
            vmem((192, 1792), BF16), vmem((192, 1792), BF16),
            pltpu.SemaphoreType.DMA((11,)),
            pltpu.SemaphoreType.DMA((copies,)), pltpu.SemaphoreType.DMA((copies,)),
            pltpu.SemaphoreType.DMA((2,)), pltpu.SemaphoreType.DMA((2,)), pltpu.SemaphoreType.REGULAR((2,)),
        ]
        state = [
            ((16, EZ), F32), (field, F32), (field, F32), (field, F32),
            ((3, EY, FD, EZ), F32), ((3, EX, FD, EZ), F32), ((3, FD, EZ), F32),
            ((CELLS, 384, EZ), F32), ((384, 192), BF16), ((8, EZ), jnp.int32),
        ]
        in_vmem = pl.BlockSpec(memory_space=pltpu.VMEM)
        kept = pl.pallas_call(
            functools.partial(kernel, sizes),
            out_shape=[jax.ShapeDtypeStruct(*entry) for entry in state],
            in_specs=[pl.BlockSpec(memory_space=pltpu.HBM)] * 9,
            out_specs=[in_vmem] * len(state),
            scratch_shapes=scratch,
            compiler_params=pltpu.CompilerParams(
                collective_id=0, has_side_effects=True, vmem_limit_bytes=32 * 1024 * 1024
            ),
            name="step",
        )(
            *(
                pltpu.with_memory_space_constraint(value, pltpu.HBM)
                for value in (
                    trace_old.reshape(768, EZ), face_load.reshape(768, EZ), face_diag.reshape(24, EZ),
                    fine_flag.reshape(8, EZ), coeff.reshape(8, EZ), fields.reshape(3072, EZ), volume_op, lift_op.T,
                    schur_op,
                )
            )
        )
        out_f, out_x = pl.pallas_call(
            finish,
            out_shape=(jax.ShapeDtypeStruct((3072, EZ), BF16), jax.ShapeDtypeStruct((768, EZ), F32)),
            in_specs=[in_vmem] * len(state),
            out_specs=(pl.BlockSpec(memory_space=pltpu.HBM),) * 2,
            scratch_shapes=[
                vmem((192, CELLS * EZ), BF16), vmem((3072, EZ), F32), vmem((3072, EZ), BF16), vmem((768, EZ), F32),
                vmem(field, F32), vmem((EY, FD, EZ), F32), vmem((EX, FD, EZ), F32), vmem((FD, EZ), F32),
                pltpu.SemaphoreType.DMA((1 + CHUNKS,)),
            ],
            compiler_params=pltpu.CompilerParams(vmem_limit_bytes=24 * 1024 * 1024),
            name="finish",
        )(*kept)
        return out_f.reshape(fields.shape), out_x.reshape(trace_old.shape)

    return jax.shard_map(
        body,
        mesh=mesh,
        in_specs=(
            P(None, "gx", "gy", "gz"),
            P(None, None, "gx", "gy", "gz"),
            P(None, None, "gx", "gy", "gz"),
            P(None, "gx", "gy", "gz"),
            P("gx", "gy", "gz"),
            P("gx", "gy", "gz"),
            P(),
            P(),
            P(),
        ),
        out_specs=(P(None, "gx", "gy", "gz"), P(None, None, "gx", "gy", "gz")),
        check_vma=False,
    )
```
